32 devices in a mesh: fsdp: 8 (over z, y), seq: 4 (over x, core).
Axes of the slice: x: 2, y: 2, z: 4, core: 2. Of those that a mesh axis runs over, the one named last changes fastest.
Arguments:
- tokens: bfloat16 [2, 8, 512, 1024], P(None, 'fsdp', 'seq'), may hold values from -6 to 6
- cotangent: bfloat16 [2, 8, 512, 1024], P(None, 'fsdp', 'seq'), may hold values from -6 to 6
- lengths: int32 [2, 8], P(None, 'fsdp'), may hold values from 256 to 512, as said below
- adapter_index: int32 [2, 8], P(None, 'fsdp'), may hold values from 0 to 7
- step_count: int32 [1], replicated, may hold values from 1 to 20
- w_in: bfloat16 [1024, 8208], P('fsdp'), may hold values from -0.1875 to 0.1875
- w_out: bfloat16 [2048, 1024], P('fsdp'), may hold values from -0.125 to 0.125
- w_gu: bfloat16 [1024, 5632], P('fsdp'), may hold values from -0.1875 to 0.1875
- w_down: bfloat16 [2816, 1024], P('fsdp'), may hold values from -0.109375 to 0.109375
- conv_weight: float32 [4, 6144], replicated, may hold values from -2.5 to 2.5
- norm_gains: float32 [2, 1024], replicated, may hold values from 0.5 to 1.5
- head_gain: float32 [256], replicated, may hold values from 0.5 to 1.5
- decay_rate: float32 [8], replicated, may hold values from 0.0001953125 to 0.04
- decay_bias: float32 [8], replicated, may hold values from -3 to 3
- adapters: float32 [26880, 128], P('fsdp'), may hold values from -0.3 to 0.3
- first_moment: float32 [26880, 128], P('fsdp'), may hold values from -0.00032346824 to 0.00032346824
- second_moment: float32 [26880, 128], P('fsdp'), may hold values from 8.719308e-11 to 8.719308e-10
Outputs:
- mixed: bfloat16 [2, 8, 512, 1024], P(None, 'fsdp', 'seq')
- grad_tokens: bfloat16 [2, 8, 512, 1024], P(None, 'fsdp', 'seq')
- update: float32 [26880, 128], P('fsdp')
- new_first: float32 [26880, 128], P('fsdp')
- new_second: float32 [26880, 128], P('fsdp')
- grad_norm: float32 [1], replicated
The draws below stay inside these ranges and needn't reach their ends.
Inputs may be any that keep to these rules, and one draw needn't show every extreme that they name: `lengths`: in each micro-batch one sequence has exactly 512 valid positions and another 512 // 2.
All inputs are finite; a program needn't handle non-finite values.
Results may differ from the reference program's by a relative error of at most 0.022.
Values may be sent and summed in bfloat16 or wider, within the bound.
No kernel may reach another device: no remote copies, remote signals or barrier semaphores. Data moves between devices by JAX's collectives and lax.ppermute only.
A program may use at most 384 MiB of HBM per device.

```python
import math
from functools import partial
import jax
import jax.numpy as jnp
from jax import lax

D = 1024
DV = 256
FF = 2816
CONV = 4
SPAN = 64
ADAPTERS = 8
RANK = 16
MB = 2
HV = 8
VW = 2048
LEN = 512
SEQS = 8
ADAPT_COLS = 128
R = 26880


def draw_lengths(key, part):
    drawn = jax.random.randint(key, (MB, SEQS), LEN // 2, LEN + 1)
    longest = jax.random.randint(jax.random.fold_in(key, 7), (MB,), 0, SEQS)
    offset = jax.random.randint(jax.random.fold_in(key, 11), (MB,), 1, SEQS)
    shortest = (longest + offset) % SEQS
    columns = jnp.arange(SEQS)[None, :]
    drawn = jnp.where(columns == longest[:, None], LEN, drawn)
    drawn = jnp.where(columns == shortest[:, None], LEN // 2, drawn)
    return drawn.astype(jnp.int32)


def plant(values, rng, low, top_value):
    index_at = [jax.random.randint(jax.random.fold_in(rng, axis), (), 0, length) for axis, length in enumerate(values.shape)]
    widest = values.shape.index(max(values.shape))
    beside = index_at[:widest] + [(index_at[widest] + 1) % values.shape[widest]] + index_at[widest + 1:]
    return values.at[tuple(index_at)].set(low).at[tuple(beside)].set(top_value)


def shard_levels(key, extent, shards, low, largest):
    level = 1.0
    for dim, parts in shards:
        draws = jax.random.uniform(jax.random.fold_in(jax.random.fold_in(key, 6), dim), (parts,), jnp.float32, low / len(shards), largest / len(shards))
        level = level * jnp.repeat(jnp.exp(draws), extent[dim] // parts).reshape((-1,) + (1,) * (len(extent) - 1 - dim))
    return level


def gaussian(key, extent, width, limit, cuts=(), kind=jnp.bfloat16):
    values = width * jax.random.normal(key, extent, jnp.float32)
    if cuts:
        values = values * shard_levels(key, extent, cuts, -0.22, 0.18)
    return jnp.clip(values, -limit, limit).astype(kind)


def setup_inputs(seed: int = 0) -> dict:
    key_of = jax.random.split(jax.random.key(seed), 18)
    return {
        "tokens": gaussian(key_of[0], (MB, SEQS, LEN, D), 1.0, 6.0, ((1, 8), (2, 4))),
        "cotangent": gaussian(key_of[1], (MB, SEQS, LEN, D), 1.0, 6.0, ((1, 8), (2, 4))),
        "lengths": draw_lengths(jax.random.fold_in(key_of[17], 71), 0),
        "adapter_index": plant(jax.random.randint(key_of[3], (MB, SEQS), 0, ADAPTERS), jax.random.fold_in(key_of[3], 1), 0, ADAPTERS - 1).astype(jnp.int32),
        "step_count": jax.random.randint(key_of[4], (1,), 1, 21).astype(jnp.int32),
        "w_in": gaussian(key_of[5], (D, 4 * VW + 2 * HV), D ** -0.5, 0.1875, ((0, 8),)),
        "w_out": gaussian(key_of[6], (VW, D), VW ** -0.5, 0.125, ((0, 8),)),
        "w_gu": gaussian(key_of[7], (D, 2 * FF), D ** -0.5, 0.1875, ((0, 8),)),
        "w_down": gaussian(key_of[8], (FF, D), FF ** -0.5, 0.109375, ((0, 8),)),
        "conv_weight": gaussian(key_of[9], (CONV, 3 * VW), 0.5, 2.5, (), jnp.float32),
        "norm_gains": jnp.clip(1.0 + 0.1 * jax.random.normal(key_of[10], (2, D), jnp.float32), 0.5, 1.5),
        "head_gain": jnp.clip(1.0 + 0.1 * jax.random.normal(key_of[11], (DV,), jnp.float32), 0.5, 1.5),
        "decay_rate": jnp.clip(jnp.exp(jax.random.uniform(key_of[12], (HV,), jnp.float32, math.log(0.0001953125), math.log(0.04))), 0.0001953125, 0.04),
        "decay_bias": gaussian(key_of[13], (HV,), 1.0, 3.0, (), jnp.float32),
        "adapters": gaussian(key_of[14], (R, ADAPT_COLS), 0.05, 0.3, ((0, 8),), jnp.float32),
        "first_moment": gaussian(key_of[15], (R, ADAPT_COLS), (0.1 * (R * ADAPT_COLS) ** -0.5), 0.00032346824, ((0, 8),), jnp.float32),
        "second_moment": jnp.clip(jnp.exp(math.log(8.719308053350971e-10) - 2.3025851 * jax.random.uniform(key_of[16], (R, ADAPT_COLS), jnp.float32) ** shard_levels(key_of[16], (R, ADAPT_COLS), ((0, 8),), -0.2, 0.2)), 8.719307914573093e-11, 8.719308053350971e-10),
    }


@jax.custom_vjp
def low(v):
    return lax.optimization_barrier(v.astype(jnp.bfloat16)).astype(jnp.float32)

@jax.custom_vjp
def reduced_rank_backward(v):
    return v

def low_keep(v):
    return (low(v), None)

def low_pass(kept, grad):
    return (grad,)

def back_keep(v):
    return (v, None)

def back_low(kept, grad):
    return (low(grad),)
low.defvjp(low_keep, low_pass)
reduced_rank_backward.defvjp(back_keep, back_low)
highest = lax.Precision.HIGHEST
epsilon = 1e-06
CLIP_LIMIT = 1.0
LEARN_RATE = 0.01
FIRST_DECAY = 0.9
SECOND_DECAY = 0.999
ADAM_EPSILON = 1e-08
WEIGHT_DECAY = 0.1

def both_round(values):
    return low(reduced_rank_backward(values))

def precise_product(left, right):
    return jnp.dot(left, right, preferred_element_type=jnp.float32, precision=highest)

def rms_norm(inputs, scales):
    return inputs * lax.rsqrt(lax.optimization_barrier(jnp.mean(inputs * inputs, -1, keepdims=True)) + epsilon) * scales

def swiglu(gate_up_projection):
    half_width = gate_up_projection.shape[1] // 2
    return jax.nn.silu(gate_up_projection[:, :half_width]) * gate_up_projection[:, half_width:]

def head_post(attended, gate_pre, head_gain):
    row_count, head_count, head_size = attended.shape
    normed = rms_norm(attended, head_gain)
    return (normed * jax.nn.silu(gate_pre).reshape(row_count, head_count, head_size)).reshape(row_count, head_count * head_size)

def mixer_inputs(extended, small_part, conv_weight, decay_rate, decay_bias):
    row_count = small_part.shape[0]
    head_count = decay_rate.shape[0]
    tap_count = conv_weight.shape[0]
    convolved = conv_weight[0] * extended[0:row_count]
    for tap_index in range(1, tap_count):
        convolved = convolved + conv_weight[tap_index] * extended[tap_index:tap_index + row_count]
    active = jax.nn.silu(convolved)
    value_width = active.shape[1] // 3
    queries = active[:, :value_width].reshape(row_count, 2 * head_count, -1)
    keys = active[:, value_width:2 * value_width].reshape(row_count, 2 * head_count, -1)
    values = active[:, 2 * value_width:].reshape(row_count, head_count, -1)
    queries = queries * lax.rsqrt(lax.optimization_barrier(jnp.sum(queries * queries, -1, keepdims=True)) + epsilon) * queries.shape[2] ** (-0.5)
    keys = keys * lax.rsqrt(lax.optimization_barrier(jnp.sum(keys * keys, -1, keepdims=True)) + epsilon)
    queries = queries.reshape(row_count, head_count, -1) * 0.5 ** 0.5
    keys = keys.reshape(row_count, head_count, -1) * 0.5 ** 0.5
    betas = jax.nn.sigmoid(small_part[:, head_count:])
    log_gates = -decay_rate * jax.nn.softplus(small_part[:, :head_count] + decay_bias)
    return (queries, keys, values, betas, log_gates)

def span_update(state, block):
    queries, keys, values, betas, log_gates = block
    block_len = queries.shape[0]
    cumulative = jnp.cumsum(log_gates, 0)
    positions = jnp.arange(block_len)
    inclusive = (positions[:, None] >= positions[None, :])[None, :, :]
    strictly = (positions[:, None] > positions[None, :])[None, :, :]
    spread_log = (cumulative[:, None, :] - cumulative[None, :, :]).transpose(2, 0, 1)
    ratios = jnp.where(inclusive, jnp.exp(jnp.where(inclusive, spread_log, 0.0)), 0.0)
    key_key = jnp.einsum('thd,shd->hts', keys, keys, precision=highest)
    lower = jnp.where(strictly, ratios * key_key, 0.0) * betas.T[:, :, None]
    nilpotent = -lower
    inverse = jnp.eye(block_len, dtype=jnp.float32)[None] + nilpotent
    power_term = nilpotent
    for _ in range(block_len.bit_length() - 2):
        power_term = jnp.matmul(power_term, power_term, precision=highest)
        inverse = inverse + jnp.matmul(inverse, power_term, precision=highest)
    transform = inverse * betas.T[:, None, :]
    decays = jnp.exp(cumulative)
    from_state = jnp.einsum('thd,hdw->thw', keys, state, precision=highest)
    pseudo = jnp.einsum('hts,shw->thw', transform, values - decays[:, :, None] * from_state, precision=highest)
    query_key = jnp.einsum('thd,shd->hts', queries, keys, precision=highest) * ratios
    outputs = decays[:, :, None] * jnp.einsum('thd,hdw->thw', queries, state, precision=highest)
    outputs = outputs + jnp.einsum('hts,shw->thw', query_key, pseudo, precision=highest)
    final_log = cumulative[-1]
    weighted = keys * jnp.exp(final_log[None, :] - cumulative)[:, :, None]
    new_state = jnp.exp(final_log)[:, None, None] * state + jnp.einsum('thd,thw->hdw', weighted, pseudo, precision=highest)
    return (new_state, outputs)

def run_delta(queries, keys, values, betas, log_gates, start_state):
    row_count = queries.shape[0]
    block_count = row_count // SPAN

    def blocked(array):
        return array.reshape((block_count, SPAN) + array.shape[1:])
    final_state, outputs = lax.scan(jax.checkpoint(span_update), start_state, (blocked(queries), blocked(keys), blocked(values), blocked(betas), blocked(log_gates)))
    return (final_state, outputs.reshape((row_count,) + outputs.shape[2:]))

def split_adapters(flat, model_width, value_width, hidden):
    column_count = flat.shape[1]
    row_counts = [4 * model_width, 2 * model_width, value_width, hidden, 4 * value_width, model_width, 2 * hidden, model_width]
    pieces = []
    offset = 0
    for rows_here in row_counts:
        pieces.append(flat[offset:offset + rows_here])
        offset = offset + rows_here
    return (pieces[0].reshape(4, model_width, column_count), pieces[1].reshape(2, model_width, column_count), pieces[2], pieces[3], pieces[4].reshape(4, value_width, column_count), pieces[5], pieces[6].reshape(2, hidden, column_count), pieces[7])

def low_rank_adapter(input_reduced_rank, left_adapter_matrix, right_adapter_matrix, column_mask_values):
    reduced = both_round(precise_product(input_reduced_rank, left_adapter_matrix) * column_mask_values)
    return precise_product(reduced, right_adapter_matrix.T)

def layer(inputs, adapt, full_in, complete_output_weight, complete_gate_up_weight, complete_down_weight, conv_weight, norm_gains, head_gain, decay_rate, decay_bias, column_mask_values):
    row_count, model_width = inputs.shape
    head_count = decay_rate.shape[0]
    value_width = conv_weight.shape[1] // 3
    head_size = value_width // head_count
    hidden = complete_gate_up_weight.shape[1] // 2
    tap_count = conv_weight.shape[0]
    adapter_projection_left, adapter_gate_up_left, adapter_output_left, adapter_down_left, adapter_projection_right, adapter_output_right, adapter_gate_up_right, adapter_down_right = split_adapters(low(adapt), model_width, value_width, hidden)
    first_normalized = both_round(rms_norm(inputs, norm_gains[0]))
    adapter_contribution = [low_rank_adapter(first_normalized, adapter_projection_left[part], adapter_projection_right[part], column_mask_values) for part in range(4)]
    adapter_contribution.append(jnp.zeros((row_count, 2 * head_count), jnp.float32))
    projected = reduced_rank_backward(precise_product(first_normalized, full_in) + jnp.concatenate(adapter_contribution, 1))
    conv_in = both_round(projected[:, :3 * value_width])
    gate_pre = projected[:, 3 * value_width:4 * value_width]
    small_part = projected[:, 4 * value_width:]
    extended = jnp.concatenate([jnp.zeros((tap_count - 1, 3 * value_width), jnp.float32), conv_in], 0)
    queries, keys, values, betas, log_gates = mixer_inputs(extended, small_part, conv_weight, decay_rate, decay_bias)
    final_state, attended = run_delta(queries, keys, values, betas, log_gates, jnp.zeros((head_count, head_size, head_size), jnp.float32))
    gated_values = both_round(head_post(attended, gate_pre, head_gain))
    adapter_branch = reduced_rank_backward(precise_product(gated_values, complete_output_weight) + low_rank_adapter(gated_values, adapter_output_left, adapter_output_right, column_mask_values))
    middle = inputs + adapter_branch
    second_normalized = both_round(rms_norm(middle, norm_gains[1]))
    gate_up_projection = reduced_rank_backward(precise_product(second_normalized, complete_gate_up_weight) + jnp.concatenate([low_rank_adapter(second_normalized, adapter_gate_up_left[0], adapter_gate_up_right[0], column_mask_values), low_rank_adapter(second_normalized, adapter_gate_up_left[1], adapter_gate_up_right[1], column_mask_values)], 1))
    swiglu_output = both_round(swiglu(gate_up_projection))
    down_projection = reduced_rank_backward(precise_product(swiglu_output, complete_down_weight) + low_rank_adapter(swiglu_output, adapter_down_left, adapter_down_right, column_mask_values))
    return middle + down_projection

def reference(tokens, cotangent, lengths, adapter_index, step_count, w_in, w_out, w_gu, w_down, conv_weight, norm_gains, head_gain, decay_rate, decay_bias, adapters, first_moment, second_moment):
    column_count = adapters.shape[1]
    fixed = partial(layer, full_in=w_in.astype(jnp.float32), complete_output_weight=w_out.astype(jnp.float32), complete_gate_up_weight=w_gu.astype(jnp.float32), complete_down_weight=w_down.astype(jnp.float32), conv_weight=conv_weight, norm_gains=norm_gains, head_gain=head_gain, decay_rate=decay_rate, decay_bias=decay_bias)
    flat_tokens = tokens.reshape(MB * SEQS, LEN, D).astype(jnp.float32)
    flat_cot = cotangent.reshape(MB * SEQS, LEN, D).astype(jnp.float32)
    flat_lengths = lengths.reshape(MB * SEQS).astype(jnp.int32)
    flat_index = adapter_index.reshape(MB * SEQS).astype(jnp.int32)

    def one_sequence(total, items):
        inputs, cot_rows, length_here, index_here = items
        column_mask_values = (jnp.arange(column_count).astype(jnp.int32) // RANK == index_here).astype(jnp.float32)
        row_mask = (jnp.arange(LEN).astype(jnp.int32) < length_here).astype(jnp.float32)[:, None]
        result, pull = jax.vjp(partial(fixed, column_mask_values=column_mask_values), inputs, adapters)
        grad_inputs, grad_adapt = pull(cot_rows * row_mask)
        return (total + grad_adapt, (result.astype(jnp.bfloat16), grad_inputs.astype(jnp.bfloat16)))
    total, (results, grads) = lax.scan(one_sequence, jnp.zeros_like(adapters), (flat_tokens, flat_cot, flat_lengths, flat_index))
    norm_value = jnp.sqrt(jnp.sum(total * total))
    clipped = total * (CLIP_LIMIT / jnp.maximum(norm_value, CLIP_LIMIT))
    new_first = FIRST_DECAY * first_moment + (1.0 - FIRST_DECAY) * clipped
    new_second = SECOND_DECAY * second_moment + (1.0 - SECOND_DECAY) * clipped * clipped
    counter = step_count[0].astype(jnp.float32)
    corrected_first = new_first / (1.0 - jnp.power(FIRST_DECAY, counter))
    corrected_second = new_second / (1.0 - jnp.power(SECOND_DECAY, counter))
    update = -LEARN_RATE * (corrected_first / (jnp.sqrt(corrected_second) + ADAM_EPSILON) + WEIGHT_DECAY * adapters)
    return (results.reshape(MB, SEQS, LEN, D), grads.reshape(MB, SEQS, LEN, D), update, new_first, new_second, norm_value.reshape(1))
```

```python
from functools import partial

import jax
import jax.numpy as jnp
from jax import lax
from jax.experimental import pallas as pl
from jax.experimental.pallas import tpu as pltpu
from jax.sharding import PartitionSpec as P

RANK = 16
epsilon = 1e-06
CLIP_LIMIT = 1.0
LEARN_RATE = 0.01
FIRST_DECAY = 0.9
SECOND_DECAY = 0.999
ADAM_EPSILON = 1e-08
WEIGHT_DECAY = 0.1
VMEM_LIMIT = 56 << 20

f32 = jnp.float32
bf16 = jnp.bfloat16
highest = lax.Precision.HIGHEST


def nn(a, b, precision=None):
    return lax.dot_general(
        a, b, (((1,), (0,)), ((), ())), precision=precision, preferred_element_type=f32
    )


def nt(a, b, precision=None):
    return lax.dot_general(
        a, b, (((1,), (1,)), ((), ())), precision=precision, preferred_element_type=f32
    )


def tn(a, b, precision=None):
    return lax.dot_general(
        a, b, (((0,), (0,)), ((), ())), precision=precision, preferred_element_type=f32
    )


def swapped(value, bit):
    count = lax.axis_size("seq")
    return lax.ppermute(value, "seq", [(i, i ^ bit) for i in range(count)])


def gather_far(value):
    return value, swapped(value, 2)


def gather_near(value, beyond):
    return value, swapped(value, 1), beyond, swapped(beyond, 1)


def gather_seq(value):
    return gather_near(*gather_far(value))


def in_seq_order(blocks):
    here = lax.axis_index("seq")
    for bit in (1, 2):
        flip = here & bit != 0
        blocks = [jnp.where(flip, blocks[k ^ bit], blocks[k]) for k in range(4)]
    return blocks


def scatter_far(far):
    return swapped(far, 2)


def scatter_near(near, beside, got):
    got = got.astype(f32)
    return near + got[0] + swapped((beside.astype(f32) + got[1]).astype(bf16), 1).astype(f32)


def scatter_seq(near, beyond, pair):
    got = swapped(pair, 1).astype(f32)
    return near + got[0] + swapped((beyond.astype(f32) + got[1]).astype(bf16), 2).astype(f32)


def held(values, *others):
    return lax.optimization_barrier((tuple(values), *others))[0]


def ring_order(count):
    return list(range(0, count, 2)) + list(range(count - 1, 0, -2))


def after(value, *others):
    return lax.optimization_barrier((value, *others))[0]


class RingGather:
    def __init__(self, value):
        count, here = lax.axis_size("fsdp"), lax.axis_index("fsdp")
        order = ring_order(count)
        place = [order.index(d) for d in range(count)]
        rows = value.shape[0]
        halves = rows // 2 % 16 == 0
        table = []
        for d in range(count):
            source = [order[(place[d] - k) % count] * rows for k in range(count)]
            at = [source[0]]
            for hop in range(1, count // 2 + 1):
                last = 2 * hop == count
                at.append(source[hop])
                if not last:
                    at.append(source[count - hop])
                elif halves:
                    at.append(source[hop] + rows // 2)
            table.append(at)
        self.count, self.hop, self.rows, self.halves = count, 0, rows, halves
        self.table = jnp.asarray(table, jnp.int32)[here]
        self.ahead = [(order[i], order[(i + 1) % count]) for i in range(count)]
        self.behind = [(b, a) for a, b in self.ahead]
        self.right = self.left = value
        self.blocks = [value]

    def advance(self, *others):
        self.hop += 1
        right, left = self.right, self.left
        half = self.rows // 2
        last = 2 * self.hop == self.count
        if last and self.halves:
            right, left = right[:half], left[half:]
        right = lax.ppermute(right, "fsdp", self.ahead)
        if not last or self.halves:
            left = lax.ppermute(left, "fsdp", self.behind)
        self.right, self.left, *others = lax.optimization_barrier((right, left, *others))
        self.blocks.append(self.right)
        if not last or self.halves:
            self.blocks.append(self.left)
        return others

    def done(self):
        return 2 * self.hop >= self.count


def butterfly(value, axis, bits=None):
    count = lax.axis_size(axis)
    for bit in [1 << i for i in range(count.bit_length() - 1)] if bits is None else bits:
        value = value + lax.ppermute(value, axis, [(i, i ^ bit) for i in range(count)])
    return value


def low(x):
    return x.astype(bf16)


def load_w_in(table, pieces, w_in):
    at = pieces[0].shape[1] - w_in.shape[1]
    for i, piece in enumerate(pieces):
        w_in[pl.ds(pl.multiple_of(table[i], 16), piece.shape[0]), :] = piece[:, at:]


def split_out(step, me, table, *refs):
    pieces, out = refs[:-1], refs[-1]
    span = out.shape[1]
    for i, piece in enumerate(pieces):
        row = table[i]
        out[(row // span) ^ me[0], pl.ds(pl.multiple_of(row % span, step), piece.shape[0]), :] = piece[...]


def load_w_out(me, step, quarters, w_out):
    wide = quarters[0].shape[1] // 2
    for k, quarter in enumerate(quarters):
        cols = pl.ds(pl.multiple_of((me[0] ^ k) * wide, 128), wide)
        for j in range(0, quarter.shape[0], step):
            for i in range(2):
                w_out[2 * j + i * step : 2 * j + (i + 1) * step, cols] = quarter[j : j + step, i * wide : (i + 1) * wide]


def rows_of(ref, pieces):
    span = pieces[0].shape[0]
    for k, piece in enumerate(pieces):
        ref[k * span : (k + 1) * span, :] = piece[...].astype(ref.dtype)


def block_order(micro):
    return (1, (2, 3)) if micro == 0 else (2, (1, 3))


def block_out(micro, near, single, pair, col, value):
    span = near.shape[0]
    cols = slice(col, col + value.shape[1])
    one, two = block_order(micro)
    near[:, cols] = value[:span]
    single[:, cols] = low(value[one * span : (one + 1) * span])
    for i, k in enumerate(two):
        pair[i, :, cols] = low(value[k * span : (k + 1) * span])


def tile_masks(size):
    rows = lax.broadcasted_iota(jnp.int32, (size, size), 0)
    columns = lax.broadcasted_iota(jnp.int32, (size, size), 1)
    return rows, columns


def unit_lower_inverses(lowers, inverses, keep):
    size = keep[0].shape[0]
    rows, columns = tile_masks(size)
    eye = jnp.where(rows == columns, 1.0, 0.0).astype(f32)
    block = 1
    while block < size:
        wide = 2 * block
        inside = (rows // wide == columns // wide) & (rows // block != columns // block)
        if block == 1:
            for lower, inverse in zip(lowers, inverses):
                inverse[...] = eye - jnp.where(inside, lower[...], 0.0)
        else:
            for lower, inverse, right in zip(lowers, inverses, keep):
                right[...] = nn(jnp.where(inside, lower[...], 0.0), inverse[...], highest)
            for inverse, right in zip(inverses, keep):
                inverse[...] = inverse[...] - nn(inverse[...], right[...], highest)
        block = wide


def shifted_rows(value, count, offset):
    if offset == 0:
        return value[:count]
    if offset % 8 == 0:
        return value[offset : offset + count]
    return pltpu.roll(value, value.shape[0] - offset, 0)[:count]


def half_sum(x):
    half = x.shape[1] // 2
    left = jnp.sum(x[:, :half], 1, keepdims=True)
    right = jnp.sum(x[:, half:], 1, keepdims=True)
    lane = lax.broadcasted_iota(jnp.int32, x.shape, 1)
    return jnp.where(lane < half, left, right)


def half_rsqrt(x):
    half = x.shape[1] // 2
    sq = x * x
    left = lax.rsqrt(jnp.sum(sq[:, :half], 1, keepdims=True) + epsilon)
    right = lax.rsqrt(jnp.sum(sq[:, half:], 1, keepdims=True) + epsilon)
    lane = lax.broadcasted_iota(jnp.int32, x.shape, 1)
    return jnp.where(lane < half, left, right)


def conv_block(ext, cw, start, col, span, width):
    window = ext[pl.ds(start, span + 8), col : col + width]
    out = None
    for j in range(4):
        term = shifted_rows(window, span, 5 + j) * cw[j : j + 1, col : col + width]
        out = term if out is None else out + term
    return out


def gates(gs, rb, start, span, col, tri):
    z = gs[pl.ds(start, span), col : col + 128]
    moved = z + rb[1:2, :]
    soft = jnp.maximum(moved, 0.0) + jnp.log(1.0 + jnp.exp(-jnp.abs(moved)))
    return lax.logistic(z), nn(tri, -rb[0:1, :] * soft, highest), lax.logistic(moved)


def decay_ratio(c, c_row, inclusive):
    return jnp.where(inclusive, jnp.exp(jnp.where(inclusive, c - c_row, 0.0)), 0.0)


class Layout:
    def __init__(self, width, value_width, hidden, parts):
        counts = [4 * width, 2 * width, value_width, hidden, 4 * value_width, width, 2 * hidden, width]
        at = [sum(counts[:i]) for i in range(8)]
        self.a_in, self.a_gu, self.a_out, self.a_down, self.b_in, self.b_out, self.b_gu, self.b_down = at
        self.total = sum(counts)
        self.width, self.value_width, self.hidden = width, value_width, hidden
        self.own = value_width // parts


def own_columns(ref, rows, at, here, own):
    return ref[rows, pl.ds(pl.multiple_of(at + here * own, 128), own)]


def load_in_adapters(lay, micro, here, adapt, a_in, b_in):
    rows = slice(micro * RANK, (micro + 1) * RANK)
    b_in[...] = jnp.zeros_like(b_in)
    for p in range(4):
        a_in[p * RANK : (p + 1) * RANK, :] = adapt[rows, lay.a_in + p * lay.width : lay.a_in + (p + 1) * lay.width]
        b_in[p * RANK : (p + 1) * RANK, p * lay.own : (p + 1) * lay.own] = own_columns(
            adapt, rows, lay.b_in + p * lay.value_width, here, lay.own
        )


def mixer_forward(lay, micro, heads, span, blocks, count, me, table, *refs):
    pieces, refs = refs[:count], refs[count:]
    (x0, x1, x2, x3, gain, adapt, cw, rb, hg,
     h1, z_in, pre, gs, gated, o_out, u_out, s_out, t_out, p_out, r_out,
     w_in, ext, state, kqs, vs, a_in, b_in, keep) = refs
    load_w_in(table, pieces, w_in)
    head = 256
    here = me[0]
    rows = blocks * span
    own = lay.own
    mine = slice(micro * RANK, (micro + 1) * RANK)
    load_in_adapters(lay, micro, here, adapt, a_in, b_in)
    for k, piece in enumerate((x0, x1, x2, x3)):
        x = piece[...].astype(f32)
        h1[k * span : (k + 1) * span, :] = low(
            x * lax.rsqrt(jnp.mean(x * x, 1, keepdims=True) + epsilon) * gain[...]
        )
    z_in[...] = low(nt(h1[...], a_in[...]))
    ext[0:8, :] = jnp.zeros((8, ext.shape[1]), f32)
    for col in range(0, 4 * own + 128, 256):
        wide = min(256, 4 * own + 128 - col)
        value = nn(h1[...], w_in[:, col : col + wide])
        if col < 4 * own:
            value = value + nn(z_in[...], b_in[:, col : col + wide])
        for k in range(blocks):
            part = value[k * span : (k + 1) * span]
            start = pl.multiple_of((k ^ here) * span, span)
            if col < 3 * own:
                part = low(part)
                pre[pl.ds(start, span), col : col + wide] = part
                ext[pl.ds(start + 8, span), col : col + wide] = part.astype(f32)
            else:
                gs[pl.ds(start, span), col - 3 * own : col - 3 * own + wide] = part

    grow, gcol = tile_masks(span)
    inclusive = grow >= gcol
    strictly = grow > gcol
    tri = jnp.where(inclusive, 1.0, 0.0).astype(f32)
    scale_k = 0.5**0.5
    scale_q = 128 ** (-0.5) * 0.5**0.5

    def prepare(n, carry):
        start = pl.multiple_of(n * span, span)
        betas, running, _ = gates(gs, rb, start, span, own, tri)
        running_t = running.T
        for h in range(heads):
            q = conv_block(ext, cw, start, h * head, span, head)
            k = conv_block(ext, cw, start, (heads + h) * head, span, head)
            v = conv_block(ext, cw, start, (2 * heads + h) * head, span, head)
            q = q * lax.logistic(q)
            k = k * lax.logistic(k)
            vs[h, n] = v * lax.logistic(v)
            q = q * (half_rsqrt(q) * scale_q)
            k = k * (half_rsqrt(k) * scale_k)
            kqs[h, n, :span] = k
            kqs[h, n, span:] = q
            both = nt(kqs[h, n], k)
            ratio = decay_ratio(running[:, h : h + 1], running_t[h : h + 1, :], inclusive)
            kr = jnp.where(strictly, ratio * both[:span], 0.0)
            r_out[h, n] = kr
            p_out[h, n] = both[span:] * ratio
            keep[1, h * blocks + n] = kr * betas[:, heads + h : heads + h + 1]
        return carry

    lax.fori_loop(0, blocks, prepare, 0)
    pairs = [(h, n) for h in range(heads) for n in range(blocks)]
    unit_lower_inverses(
        [keep.at[1, h * blocks + n] for h, n in pairs],
        [t_out.at[h, n] for h, n in pairs],
        [keep.at[0, h * blocks + n] for h, n in pairs],
    )
    state[...] = jnp.zeros_like(state)

    def advance(n, carry):
        start = pl.multiple_of(n * span, span)
        row = pl.multiple_of((n ^ here) * span, span)
        betas, running, _ = gates(gs, rb, start, span, own, tri)
        for h in range(heads):
            cols = slice(h * head, (h + 1) * head)
            c, b = running[:, h : h + 1], betas[:, heads + h : heads + h + 1]
            d = jnp.exp(c)
            last = c[span - 1 : span, :]
            old = state[h]
            s_out[h, n] = old
            seen = nn(kqs[h, n], old)
            u = nn(t_out[h, n], b * (vs[h, n] - d * seen[:span]))
            o = d * seen[span:] + nn(p_out[h, n], u)
            u_out[pl.ds(start, span), cols] = u
            o_out[pl.ds(start, span), cols] = o
            state[h] = jnp.exp(last) * old + tn(kqs[h, n, :span] * jnp.exp(last - c), u)
            norm = o * lax.rsqrt(jnp.mean(o * o, 1, keepdims=True) + epsilon) * hg[...]
            gate = gs[pl.ds(start, span), cols]
            gated[pl.ds(row, span), cols] = low(norm * (gate * lax.logistic(gate)))
        return carry

    lax.fori_loop(0, blocks, advance, 0)


def mixer_output(lay, micro, step, me, q0, q1, q2, q3, gated, adapt, near, single, pair, z_out, w_out):
    mine = slice(micro * RANK, (micro + 1) * RANK)
    load_w_out(me, step, (q0, q1, q2, q3), w_out)
    z_out[...] = low(nt(gated[...], own_columns(adapt, mine, lay.a_out, me[0], lay.own)))
    for col in range(0, lay.width, 256):
        value = nn(gated[...], w_out[:, col : col + 256]) + nn(
            z_out[...], adapt[mine, lay.b_out + col : lay.b_out + col + 256]
        )
        block_out(micro, near, single, pair, col, value)


def mixer_backward(lay, micro, heads, span, blocks, windows, count, step_rows, me, table, *refs):
    pieces, quarters, refs = refs[:count], refs[count : count + 4], refs[count + 4 :]
    (g0, g1, g2, g3, adapt, cw, rb, hg, z_out, h1, z_in, pre, gs, gated, o_in, u_in, s_in, t_in, p_in, r_in,
     ga_gu, g_hidden, gb_down, near, single, pair, send_near, send_single, send_pair,
     w_in, w_out, ext, back, dstate, a_in, b_in, gbranch, dgated, dproj, dsmall, flat) = refs
    load_w_in(table, pieces, w_in)
    load_w_out(me, step_rows, quarters, w_out)
    head = 256
    here = me[0]
    own = lay.own
    width = lay.width
    mine = slice(micro * RANK, (micro + 1) * RANK)
    load_in_adapters(lay, micro, here, adapt, a_in, b_in)
    rows_of(gbranch, (g0, g1, g2, g3))
    a_out = own_columns(adapt, mine, lay.a_out, here, own)
    gz_out = low(nt(gbranch[...], adapt[mine, lay.b_out : lay.b_out + width]))
    for col in range(0, own, 256):
        dgated[:, col : col + 256] = low(
            nt(gbranch[...], w_out[col : col + 256, :]) + nn(gz_out, a_out[:, col : col + 256])
        )
    ga_out = tn(gz_out, gated[...])
    gb_out = tn(z_out[...], gbranch[...])

    grow, gcol = tile_masks(span)
    inclusive = grow >= gcol
    strictly = grow > gcol
    tri = jnp.where(inclusive, 1.0, 0.0).astype(f32)
    scale_k = 0.5**0.5
    scale_q = 128 ** (-0.5) * 0.5**0.5
    ext[0:8, :] = jnp.zeros((8, ext.shape[1]), f32)
    ext[8:, :] = pre[...].astype(f32)
    back[...] = jnp.zeros_like(back)
    dstate[...] = jnp.zeros_like(dstate)
    lane = lax.broadcasted_iota(jnp.int32, (span, 128), 1)
    sub = lax.broadcasted_iota(jnp.int32, (span, 128), 0)
    final = lax.broadcasted_iota(jnp.int32, (span, 1), 0) == span - 1

    def step(i, carry):
        n = blocks - 1 - i
        row = pl.multiple_of((n ^ here) * span, span)
        start = pl.multiple_of(n * span, span)
        betas, running, slope = gates(gs, rb, start, span, own, tri)
        running_t = running.T
        drunning = jnp.zeros((span, 128), f32)
        by_row = jnp.zeros((span, 128), f32)
        dbetas = jnp.zeros((span, 128), f32)
        for h in range(heads):
            cols = slice(h * head, (h + 1) * head)
            cq = conv_block(ext, cw, start, h * head, span, head)
            ck = conv_block(ext, cw, start, (heads + h) * head, span, head)
            cv = conv_block(ext, cw, start, (2 * heads + h) * head, span, head)
            sq, sk, sv = lax.logistic(cq), lax.logistic(ck), lax.logistic(cv)
            qa, ka, v = cq * sq, ck * sk, cv * sv
            rq, rk = half_rsqrt(qa), half_rsqrt(ka)
            q = qa * (rq * scale_q)
            k = ka * (rk * scale_k)
            kq = jnp.concatenate([k, q], 0)
            c = running[:, h : h + 1]
            b = betas[:, heads + h : heads + h + 1]
            d = jnp.exp(c)
            last = c[span - 1 : span, :]
            w = jnp.exp(last - c)
            inv, att, kr = t_in[h, n], p_in[h, n], r_in[h, n]
            u = u_in[pl.ds(start, span), cols]
            o = o_in[pl.ds(start, span), cols]
            old = s_in[h, n]
            after = dstate[h]
            gate = gs[pl.ds(start, span), cols]
            dy = dgated[pl.ds(row, span), cols].astype(f32)
            sg = lax.logistic(gate)
            r = lax.rsqrt(jnp.mean(o * o, 1, keepdims=True) + epsilon)
            dn = dy * (gate * sg) * hg[...]
            normed = o * r
            dproj[pl.ds(row, span), (3 * heads + h) * head : (3 * heads + h + 1) * head] = low(
                dy * (normed * hg[...]) * (sg * (1.0 + gate * (1.0 - sg)))
            )
            do = r * (dn - normed * jnp.mean(normed * dn, 1, keepdims=True))
            seen = nn(kq, old)
            x = v - d * seen[:span]
            du = tn(att, do) + nn(k * w, after)
            datt = jnp.where(inclusive, nt(do, u), 0.0)
            dweighted = nt(u, after)
            y = tn(inv, du)
            dlow = jnp.where(strictly, -nt(y, u), 0.0)
            dx = b * y
            db = jnp.sum(y * x, 1, keepdims=True) + jnp.sum(dlow * kr, 1, keepdims=True)
            dseen = jnp.concatenate([-(d * dx), d * do], 0)
            dstate[h] = jnp.exp(last) * after + tn(kq, dseen)
            dkq = nt(dseen, old)
            dd = jnp.sum(do * seen[span:] - dx * seen[:span], 1, keepdims=True)
            ratio = decay_ratio(c, running_t[h : h + 1, :], inclusive)
            dboth = jnp.concatenate([dlow * b * ratio, datt * ratio], 0)
            dkq = dkq + nn(dboth, k)
            dk = dkq[:span] + tn(dboth, kq) + dweighted * w
            dq = dkq[span:]
            grown = dlow * (b * kr) + datt * att
            dw = jnp.sum(dweighted * k, 1, keepdims=True) * w
            dlast = jnp.exp(last) * jnp.sum(
                jnp.sum(after * old, 1, keepdims=True), 0, keepdims=True
            ) + jnp.sum(dw, 0, keepdims=True)
            dc = jnp.sum(grown, 1, keepdims=True) - dw + dd * d + jnp.where(final, dlast, 0.0)
            drunning = drunning + jnp.where(lane == h, dc, 0.0)
            by_row = by_row + jnp.where(sub == h, jnp.sum(grown, 0, keepdims=True), 0.0)
            dbetas = dbetas + jnp.where(lane == heads + h, db, 0.0)
            dqa = rq * scale_q * dq - qa * (rq * rq * rq * scale_q) * half_sum(qa * dq)
            dka = rk * scale_k * dk - ka * (rk * rk * rk * scale_k) * half_sum(ka * dk)
            for part, grad, sig, act in ((0, dqa, sq, cq), (1, dka, sk, ck), (2, dx, sv, cv)):
                col = (part * heads + h) * head
                through = grad * (sig * (1.0 + act * (1.0 - sig)))
                window = jnp.concatenate([through, back[:, col : col + head]], 0)
                back[:, col : col + head] = through[:8]
                out = None
                for j in range(4):
                    term = shifted_rows(window, span, 3 - j) * cw[j : j + 1, col : col + head]
                    out = term if out is None else out + term
                dproj[pl.ds(row, span), col : col + head] = low(out)
        dlog = tn(tri, drunning - by_row.T, highest)
        dsmall[pl.ds(row, span), :] = low(
            -rb[0:1, :] * slope * dlog + dbetas * betas * (1.0 - betas)
        )
        return carry

    lax.fori_loop(0, blocks, step, 0)
    gz_in = low(nt(dproj[...], b_in[...]))
    for col in range(0, width, 256):
        value = (
            nt(dproj[...], w_in[col : col + 256, : 4 * own])
            + nt(dsmall[...], w_in[col : col + 256, 4 * own :])
            + nn(gz_in, a_in[:, col : col + 256])
        )
        block_out(micro, near, single, pair, col, value)
    flat[...] = jnp.zeros_like(flat)
    ga_in = low(tn(gz_in, h1[...]))
    for p in range(4):
        flat[:, lay.a_in + p * width : lay.a_in + (p + 1) * width] = ga_in[p * RANK : (p + 1) * RANK]
        gb = tn(z_in[...], dproj[:, p * own : (p + 1) * own])
        flat[:, pl.ds(pl.multiple_of(lay.b_in + p * lay.value_width + here * own, 128), own)] = low(
            gb[p * RANK : (p + 1) * RANK]
        )
    flat[:, pl.ds(pl.multiple_of(lay.a_out + here * own, 128), own)] = low(ga_out)
    flat[:, lay.b_out : lay.b_out + width] = low(gb_out)
    for i in range(2):
        flat[:, lay.a_gu + i * width : lay.a_gu + (i + 1) * width] = ga_gu[i * RANK : (i + 1) * RANK, :]
    hidden = lay.hidden
    flat[:, lay.a_down : lay.a_down + hidden] = g_hidden[:RANK, :]
    for i in range(2):
        flat[:, lay.b_gu + i * hidden : lay.b_gu + (i + 1) * hidden] = g_hidden[(i + 1) * RANK : (i + 2) * RANK, :]
    flat[:, lay.b_down : lay.b_down + width] = gb_down[...]
    quarter = send_near.shape[2]
    one, two = block_order(micro)
    sends = {0: send_near, one: send_single, two[0]: send_pair.at[0], two[1]: send_pair.at[1]}
    for k, send in sends.items():
        for f, window in enumerate(windows):
            at = pl.multiple_of(window + (here ^ k) * quarter, 128)
            send[f] = flat[:, pl.ds(at, quarter)]


def feed_forward(lay, micro, h0, h1, h2, h3, g0, g1, g2, g3, w_gu, w_down, adapt, hidden,
                 near, single, pair, gnear, gsingle, gpair, ga_gu, g_own, gb_down,
                 hs, gs, a_gu, b_gate, b_up, gate, up, act, ggate, gup):
    width = lay.width
    mine = slice(micro * RANK, (micro + 1) * RANK)
    wide = act.shape[1]
    rows_of(hs, (h0, h1, h2, h3))
    rows_of(gs, (g0, g1, g2, g3))
    for i in range(2):
        a_gu[i * RANK : (i + 1) * RANK, :] = adapt[mine, lay.a_gu + i * width : lay.a_gu + (i + 1) * width]
    at = [(3 * micro + i) * RANK for i in range(3)]
    a_down = hidden[at[0] : at[0] + RANK, :]
    b_gate[...] = jnp.zeros_like(b_gate)
    b_up[...] = jnp.zeros_like(b_up)
    b_gate[:RANK, :] = hidden[at[1] : at[1] + RANK, :]
    b_up[RANK:, :] = hidden[at[2] : at[2] + RANK, :]
    b_down = adapt[mine, lay.b_down : lay.b_down + width]
    z_gu = low(nt(hs[...], a_gu[...]))
    gz_down = low(nt(gs[...], b_down))
    for col in range(0, wide, 256):
        cols = slice(col, col + 256)
        ga = nn(hs[...], w_gu[:, cols]) + nn(z_gu, b_gate[:, cols])
        ua = nn(hs[...], w_gu[:, wide + col : wide + col + 256]) + nn(z_gu, b_up[:, cols])
        sig = lax.logistic(ga)
        silu = ga * sig
        act[:, cols] = low(silu * ua)
        da = low(nt(gs[...], w_down[cols, :]) + nn(gz_down, a_down[:, cols])).astype(f32)
        ggate[:, cols] = low(da * ua * (sig * (1.0 + ga * (1.0 - sig))))
        gup[:, cols] = low(da * silu)
    gz_gu = low(nt(ggate[...], b_gate[...]) + nt(gup[...], b_up[...]))
    for col in range(0, width, 256):
        cols = slice(col, col + 256)
        value = (
            nt(ggate[...], w_gu[cols, :wide]) + nt(gup[...], w_gu[cols, wide:]) + nn(gz_gu, a_gu[:, cols])
        )
        block_out(micro, gnear, gsingle, gpair, col, value)
    z_down = low(nt(act[...], a_down))
    for col in range(0, width, 256):
        cols = slice(col, col + 256)
        value = nn(act[...], w_down[:, cols]) + nn(z_down, b_down[:, cols])
        block_out(micro, near, single, pair, col, value)
    ga_gu[...] = low(tn(gz_gu, hs[...]))
    gb_down[...] = low(tn(z_down, gs[...]))
    g_own[:RANK, :] = low(tn(gz_down, act[...]))
    g_own[RANK : 2 * RANK, :] = low(tn(z_gu, ggate[...])[:RANK])
    g_own[2 * RANK :, :] = low(tn(z_gu, gup[...])[RANK:])


def adapter_rows(windows, me, c0, c1, c2, c3, out):
    here = me[0]
    out[...] = jnp.zeros_like(out)
    quarter = c0.shape[2]
    for k, piece in enumerate((c0, c1, c2, c3)):
        for f, window in enumerate(windows):
            cols = pl.ds(pl.multiple_of(window + (here ^ k) * quarter, 128), quarter)
            out[:, cols] = out[:, cols] + piece[f]


SMEM = pl.BlockSpec(memory_space=pltpu.SMEM)
VMEM = pl.BlockSpec(memory_space=pltpu.VMEM)


def kernel_call(body, name, out_shape, scratch, args, scalars=1, flops=0):
    specs = [SMEM if i < scalars else VMEM for i in range(len(args))]
    size = sum(a.size * a.dtype.itemsize for a in args)
    return pl.pallas_call(
        body,
        out_shape=tuple(out_shape),
        in_specs=specs,
        out_specs=tuple([VMEM] * len(out_shape)),
        scratch_shapes=scratch,
        compiler_params=pltpu.CompilerParams(vmem_limit_bytes=VMEM_LIMIT),
        cost_estimate=pl.CostEstimate(flops=flops, bytes_accessed=int(size), transcendentals=0),
        name=name,
    )(*args)


def rms_norm(inputs, scales):
    return inputs * lax.rsqrt(jnp.mean(inputs * inputs, -1, keepdims=True) + epsilon) * scales


def own_lanes(value, start, size):
    return lax.dynamic_slice_in_dim(value, start, size, axis=value.ndim - 1)


def shards(
    tokens,
    cotangent,
    lengths,
    adapter_index,
    step_count,
    w_in,
    w_out,
    w_gu,
    w_down,
    conv_weight,
    norm_gains,
    head_gain,
    decay_rate,
    decay_bias,
    adapters,
    first_moment,
    second_moment,
):
    micro_count, _, span, width = tokens.shape
    ranks = lax.axis_size("fsdp")
    parts = lax.axis_size("seq")
    here = lax.axis_index("seq")
    place = lax.axis_index("fsdp")
    all_heads = decay_rate.shape[0]
    heads = all_heads // parts
    value_width = conv_weight.shape[1] // 3
    own = value_width // parts
    hidden = w_gu.shape[1] // 2
    piece = w_down.shape[0] // parts
    wide = -(-hidden // parts // 256) * 256
    padded = wide // ranks
    columns = adapters.shape[1]
    shard_rows = adapters.shape[0]
    rows = parts * span
    me = here.astype(jnp.int32).reshape(1)
    lay = Layout(width, value_width, hidden, parts)
    shape = jax.ShapeDtypeStruct

    def heads_slice(part):
        return own_lanes(w_in, part * value_width + here * own, own)

    small = jnp.concatenate(
        [
            own_lanes(w_in, 4 * value_width + here * heads, heads),
            own_lanes(w_in, 4 * value_width + all_heads + here * heads, heads),
            jnp.zeros((w_in.shape[0], 128 - 2 * heads), bf16),
        ],
        1,
    )
    in_rows = w_in.shape[0]
    local_out = own_lanes(w_out, here * (width // parts), width // parts)
    local_in = jnp.concatenate(
        [local_out[:in_rows], local_out[in_rows:]] + [heads_slice(p) for p in range(4)] + [small], 1
    )
    ring = RingGather(local_in)

    window = -(-(shard_rows + 127) // (128 * parts)) * 128 * parts
    quarter = window // parts
    windows = [shard_rows * f // 128 * 128 for f in range(ranks)]
    flat_width = windows[-1] + window
    offset = (shard_rows * place) % 128
    picks = lax.dynamic_update_slice(
        jnp.zeros((ranks, 128), jnp.int32), jnp.pad(adapter_index.T, ((0, 0), (0, 128 - micro_count))), (place, 0)
    )
    bits = [1 << i for i in range(ranks.bit_length() - 1)]
    picks = butterfly(picks, "fsdp", bits[:2])
    framed = lax.dynamic_update_slice(
        jnp.zeros((window, columns), bf16), adapters.astype(bf16), (offset, 0)
    )
    framed = lax.dynamic_slice_in_dim(framed, here * quarter, quarter, 0)
    conv_own = jnp.concatenate(
        [own_lanes(conv_weight, p * value_width + here * own, own) for p in range(3)], 1
    )
    rate_bias = jnp.zeros((8, 128), f32)
    rate_bias = rate_bias.at[0, :heads].set(lax.dynamic_slice(decay_rate, (here * heads,), (heads,)))
    rate_bias = rate_bias.at[1, :heads].set(lax.dynamic_slice(decay_bias, (here * heads,), (heads,)))
    gain_row = head_gain.reshape(1, -1)
    head = head_gain.shape[0]

    far_tokens = [gather_far(tokens[m, 0]) for m in range(micro_count)]
    framed, conv_own, rate_bias, table, picks = ring.advance(
        framed, conv_own, rate_bias, ring.table, picks
    )
    picks = butterfly(picks, "fsdp", bits[2:])
    wanted = (picks[:, :micro_count, None] * RANK + jnp.arange(RANK)[None, None, :]).reshape(-1)
    select = (wanted[:, None] == jnp.arange(columns)[None, :]).astype(bf16)
    chosen = nt(select, framed).astype(bf16).reshape(ranks, micro_count * RANK, quarter)
    chosen = lax.all_to_all(chosen, "fsdp", 0, 0)

    unit = after(jnp.arange(wide), ring.right)
    unit_of = (unit // padded) * w_down.shape[0] + here * piece + unit % padded
    unit_of = jnp.where(unit % padded < piece, unit_of, -1)
    spread = (jnp.arange(hidden)[:, None] == unit_of[None, :]).astype(bf16)
    local_gu = jnp.concatenate(
        [nn(w_gu[:, i * hidden : (i + 1) * hidden], spread).astype(bf16) for i in range(2)], 1
    )
    local_down = jnp.pad(
        lax.dynamic_slice_in_dim(w_down, here * piece, piece, 0), ((0, padded - piece), (0, 0))
    )
    pieces = [gather_near(*far) for far in far_tokens]
    chosen, local_gu, local_down, pieces = ring.advance(chosen, local_gu, local_down, pieces)

    chosen, beyond = gather_far(chosen)
    chosen, beyond = ring.advance(chosen, beyond)
    (chosen,) = ring.advance(gather_near(chosen, beyond))
    while not ring.done():
        ring.advance()
    quarter_width = 2 * (width // parts)
    out_sorted = pl.pallas_call(
        partial(split_out, min(block.shape[0] for block in ring.blocks)),
        grid=(1,),
        out_shape=shape((parts, width // parts, quarter_width), bf16),
        in_specs=[SMEM, SMEM]
        + [pl.BlockSpec((block.shape[0], quarter_width), lambda i: (0, 0)) for block in ring.blocks],
        out_specs=pl.BlockSpec((parts, width // parts, quarter_width), lambda i: (0, 0, 0)),
        name="split_out",
    )(me, table, *ring.blocks)
    out_quarters = [swapped(out_sorted[k], k) if k else out_sorted[k] for k in range(parts)]
    (adapt,) = kernel_call(
        partial(adapter_rows, windows),
        "adapter_rows",
        [shape((micro_count * RANK, flat_width), bf16)],
        [],
        (me, *chosen),
    )
    count = len(ring.blocks)
    whole = (me, table, *ring.blocks)

    def hidden_rows(at):
        return adapt[:, at : at + hidden].reshape(micro_count, 1, RANK, hidden)

    used = jnp.concatenate(
        [hidden_rows(at) for at in (lay.a_down, lay.b_gu, lay.b_gu + hidden)], 1
    ).reshape(3 * micro_count * RANK, hidden)
    hidden_own = nn(used, spread).astype(bf16)
    full_gu = lax.all_gather(after(local_gu, ring.right), "fsdp", axis=0, tiled=True)
    full_down = lax.all_gather(after(local_down, ring.right), "fsdp", axis=0, tiled=True)

    blocks_f32 = [shape((span, width), f32), shape((span, width), bf16), shape((2, span, width), bf16)]
    send = (ranks, RANK, quarter)
    blocks = parts
    saved_shapes = [
        shape((rows, width), bf16),
        shape((rows, 4 * RANK), bf16),
        shape((rows, 3 * own), bf16),
        shape((rows, own + 128), f32),
        shape((rows, own), bf16),
        shape((rows, own), f32),
        shape((rows, own), f32),
        shape((heads, blocks, head, head), f32),
    ] + [shape((heads, blocks, span, span), f32)] * 3
    weights = [pltpu.VMEM((width, 4 * own + 128), bf16), pltpu.VMEM((own, width), bf16)]
    in_adapters = [pltpu.VMEM((4 * RANK, width), bf16), pltpu.VMEM((4 * RANK, 4 * own), bf16)]

    positions = here * span + jnp.arange(span)
    first_gain = norm_gains[0].reshape(1, -1)
    micros = range(micro_count)
    inputs = [tokens[m, 0].astype(f32) for m in micros]
    cots = [
        cotangent[m, 0].astype(f32) * (positions < lengths[m, 0]).astype(f32)[:, None] for m in micros
    ]
    cot_pieces = [gather_seq(low(cots[m])) for m in micros]

    def forward(m):
        outs = kernel_call(
            partial(mixer_forward, lay, m, heads, span, blocks, count),
            "mixer_forward",
            saved_shapes,
            [
                weights[0],
                pltpu.VMEM((rows + 8, 3 * own), f32),
                pltpu.VMEM((heads, head, head), f32),
                pltpu.VMEM((heads, blocks, 2 * span, head), f32),
                pltpu.VMEM((heads, blocks, span, head), f32),
                *in_adapters,
                pltpu.VMEM((2, heads * blocks, span, span), f32),
            ],
            (*whole, *pieces[m], first_gain, adapt, conv_own, rate_bias, gain_row),
            scalars=2,
            flops=6_000_000_000,
        )
        return outs

    def output(m, gated):
        outs = kernel_call(
            partial(mixer_output, lay, m, in_rows),
            "mixer_output",
            blocks_f32 + [shape((rows, RANK), bf16)],
            [weights[1]],
            (me, *out_quarters, gated, adapt),
            flops=1_000_000_000,
        )
        return outs[:3], outs[3]

    def feed(m, h2, cot):
        outs = kernel_call(
            partial(feed_forward, lay, m),
            "feed_forward",
            blocks_f32
            + blocks_f32
            + [
                shape((2 * RANK, width), bf16),
                shape((3 * RANK, wide), bf16),
                shape((RANK, width), bf16),
            ],
            [
                pltpu.VMEM((rows, width), bf16),
                pltpu.VMEM((rows, width), bf16),
                pltpu.VMEM((2 * RANK, width), bf16),
                pltpu.VMEM((2 * RANK, wide), bf16),
                pltpu.VMEM((2 * RANK, wide), bf16),
                pltpu.VMEM((8, 128), f32),
                pltpu.VMEM((8, 128), f32),
                pltpu.VMEM((rows, wide), bf16),
                pltpu.VMEM((rows, wide), bf16),
                pltpu.VMEM((rows, wide), bf16),
            ],
            (*h2, *cot, full_gu, full_down, adapt, hidden_own),
            scalars=0,
            flops=5_000_000_000,
        )
        return outs[:3], outs[3:6], outs[6:]

    def backward(m, g_branch, saved, small_grads):
        ga_gu, g_own, gb_down = small_grads
        outs = kernel_call(
            partial(mixer_backward, lay, m, heads, span, blocks, windows, count, in_rows),
            "mixer_backward",
            blocks_f32 + [shape(send, bf16), shape(send, bf16), shape((2, *send), bf16)],
            [
                *weights,
                pltpu.VMEM((rows + 8, 3 * own), f32),
                pltpu.VMEM((8, 3 * own), f32),
                pltpu.VMEM((heads, head, head), f32),
                *in_adapters,
                pltpu.VMEM((rows, width), bf16),
                pltpu.VMEM((rows, own), bf16),
                pltpu.VMEM((rows, 4 * own), bf16),
                pltpu.VMEM((rows, 128), bf16),
                pltpu.VMEM((RANK, flat_width), bf16),
            ],
            (
                *whole,
                *out_quarters,
                *g_branch,
                adapt,
                conv_own,
                rate_bias,
                gain_row,
                *saved,
                ga_gu,
                nt(g_own, spread).astype(bf16),
                gb_down,
            ),
            scalars=2,
            flops=9_000_000_000,
        )
        return outs[:3], outs[3:]

    def second_norm(middle):
        h2, pull = jax.vjp(partial(rms_norm, scales=norm_gains[1]), middle)
        return low(h2), pull

    def input_gradient(m, g_middle, g_h1):
        pull = jax.vjp(partial(rms_norm, scales=norm_gains[0]), inputs[m])[1]
        return low(g_middle + pull(low(g_h1).astype(f32))[0])

    saved0 = forward(0)
    out0, z_out0 = output(0, saved0[4])
    got0 = scatter_far(out0[2])
    saved1 = forward(1)
    got0, saved1 = held((got0, saved1))
    middle0 = inputs[0] + scatter_near(out0[0], out0[1], got0)
    out1, z_out1 = output(1, saved1[4])
    middle1 = inputs[1] + scatter_seq(*out1)
    h20, pull0 = second_norm(middle0)
    h20 = gather_seq(h20)
    h21, pull1 = second_norm(middle1)
    h20, h21 = held((h20, h21))
    far1 = gather_far(h21)
    last0, g_out0, grads0 = feed(0, h20, cot_pieces[0])
    far1, last0, g_out0, grads0 = held((far1, last0, g_out0, grads0))
    h21 = gather_near(*far1)
    g_got0 = scatter_far(g_out0[2])
    last1, g_out1, grads1 = feed(1, h21, cot_pieces[1])
    g_got0, last1, g_out1, grads1 = held((g_got0, last1, g_out1, grads1))
    g_h20 = scatter_near(g_out0[0], g_out0[1], g_got0)
    g_h21 = scatter_seq(*g_out1)
    g_middle0 = cots[0] + pull0(low(g_h20).astype(f32))[0]
    branch0 = gather_seq(low(g_middle0))
    g_middle1 = cots[1] + pull1(low(g_h21).astype(f32))[0]
    branch0, g_middle1 = held((branch0, g_middle1))
    far1 = gather_far(low(g_middle1))
    last_got0 = scatter_far(last0[2])
    g_in0, sums0 = backward(0, branch0, (z_out0, *saved0), grads0)
    far1, last_got0, g_in0, sums0 = held((far1, last_got0, g_in0, sums0))
    branch1 = gather_near(*far1)
    mixed0 = low(middle0 + scatter_near(last0[0], last0[1], last_got0))
    sums_got0 = scatter_far(sums0[2])
    g_in_got0 = scatter_far(g_in0[2])
    g_in1, sums1 = backward(1, branch1, (z_out1, *saved1), grads1)
    sums_got0, g_in_got0, g_in1, sums1 = held((sums_got0, g_in_got0, g_in1, sums1))
    mixed1 = low(middle1 + scatter_seq(*last1))
    total1 = low(scatter_seq(sums1[0].astype(f32), *sums1[1:]))
    total0 = low(scatter_near(sums0[0].astype(f32), sums0[1], sums_got0))
    grad_tokens0 = input_gradient(0, g_middle0, scatter_near(g_in0[0], g_in0[1], g_in_got0))
    grad_tokens1 = input_gradient(1, g_middle1, scatter_seq(*g_in1))
    arrived = lax.all_to_all(jnp.concatenate([total0, total1], 1), "fsdp", 0, 0)
    mine = tn(arrived.reshape(-1, quarter), select)
    at = here * quarter + jnp.arange(quarter)
    mine = jnp.where(((at >= offset) & (at < offset + shard_rows))[:, None], mine, 0.0)
    squares = jnp.full((8, 128), jnp.sum(mine * mine))
    squares = butterfly(butterfly(squares, "seq"), "fsdp")[0, 0]
    shard_grad = jnp.concatenate(in_seq_order(gather_seq(low(mine))), 0)
    shard_grad = lax.dynamic_slice_in_dim(shard_grad, offset, shard_rows, 0).astype(f32)
    norm_value = jnp.sqrt(squares)
    clipped = shard_grad * (CLIP_LIMIT / jnp.maximum(norm_value, CLIP_LIMIT))
    new_first = FIRST_DECAY * first_moment + (1.0 - FIRST_DECAY) * clipped
    new_second = SECOND_DECAY * second_moment + (1.0 - SECOND_DECAY) * clipped * clipped
    counter = step_count[0].astype(f32)
    corrected_first = new_first / (1.0 - jnp.power(FIRST_DECAY, counter))
    corrected_second = new_second / (1.0 - jnp.power(SECOND_DECAY, counter))
    update = -LEARN_RATE * (
        corrected_first / (jnp.sqrt(corrected_second) + ADAM_EPSILON) + WEIGHT_DECAY * adapters
    )
    return (
        jnp.stack([mixed0, mixed1], 0)[:, None],
        jnp.stack([grad_tokens0, grad_tokens1], 0)[:, None],
        update,
        new_first,
        new_second,
        norm_value.reshape(1),
    )


def solution(mesh):
    in_specs = (
        P(None, "fsdp", "seq", None),
        P(None, "fsdp", "seq", None),
        P(None, "fsdp"),
        P(None, "fsdp"),
        P(),
        P("fsdp", None),
        P("fsdp", None),
        P("fsdp", None),
        P("fsdp", None),
        P(),
        P(),
        P(),
        P(),
        P(),
        P("fsdp", None),
        P("fsdp", None),
        P("fsdp", None),
    )
    out_specs = (
        P(None, "fsdp", "seq", None),
        P(None, "fsdp", "seq", None),
        P("fsdp", None),
        P("fsdp", None),
        P("fsdp", None),
        P(),
    )
    return jax.shard_map(shards, mesh=mesh, in_specs=in_specs, out_specs=out_specs, check_vma=False)
```

```python
from functools import partial

import jax
import jax.numpy as jnp
from jax import lax
from jax.experimental import pallas as pl
from jax.experimental.pallas import tpu as pltpu
from jax.sharding import PartitionSpec as P

RANK = 16
epsilon = 1e-06
CLIP_LIMIT = 1.0
LEARN_RATE = 0.01
FIRST_DECAY = 0.9
SECOND_DECAY = 0.999
ADAM_EPSILON = 1e-08
WEIGHT_DECAY = 0.1
VMEM_LIMIT = 56 << 20

f32 = jnp.float32
bf16 = jnp.bfloat16
high = lax.Precision.HIGH


def nn(a, b, precision=None):
    return lax.dot_general(
        a, b, (((1,), (0,)), ((), ())), precision=precision, preferred_element_type=f32
    )


def nt(a, b, precision=None):
    return lax.dot_general(
        a, b, (((1,), (1,)), ((), ())), precision=precision, preferred_element_type=f32
    )


def tn(a, b, precision=None):
    return lax.dot_general(
        a, b, (((0,), (0,)), ((), ())), precision=precision, preferred_element_type=f32
    )


def swapped(value, bit):
    count = lax.axis_size("seq")
    return lax.ppermute(value, "seq", [(i, i ^ bit) for i in range(count)])


def gather_far(value):
    return value, swapped(value, 2)


def gather_near(value, beyond):
    return value, swapped(value, 1), beyond, swapped(beyond, 1)


def gather_seq(value):
    return gather_near(*gather_far(value))


def in_seq_order(blocks):
    here = lax.axis_index("seq")
    for bit in (1, 2):
        flip = here & bit != 0
        blocks = [jnp.where(flip, blocks[k ^ bit], blocks[k]) for k in range(4)]
    return blocks


def scatter_far(far):
    return swapped(far, 2)


def scatter_near(near, beside, got):
    got = got.astype(f32)
    return near + got[0] + swapped((beside.astype(f32) + got[1]).astype(bf16), 1).astype(f32)


def scatter_seq(near, beyond, pair):
    got = swapped(pair, 1).astype(f32)
    return near + got[0] + swapped((beyond.astype(f32) + got[1]).astype(bf16), 2).astype(f32)


def held(values, *others):
    return lax.optimization_barrier((tuple(values), *others))[0]


def ring_order(count):
    return list(range(0, count, 2)) + list(range(count - 1, 0, -2))


def after(value, *others):
    return lax.optimization_barrier((value, *others))[0]


class RingGather:
    def __init__(self, value):
        count, here = lax.axis_size("fsdp"), lax.axis_index("fsdp")
        order = ring_order(count)
        place = [order.index(d) for d in range(count)]
        rows = value.shape[0]
        halves = rows // 2 % 16 == 0
        table = []
        for d in range(count):
            source = [order[(place[d] - k) % count] * rows for k in range(count)]
            at = [source[0]]
            for hop in range(1, count // 2 + 1):
                last = 2 * hop == count
                at.append(source[hop])
                if not last:
                    at.append(source[count - hop])
                elif halves:
                    at.append(source[hop] + rows // 2)
            table.append(at)
        self.count, self.hop, self.rows, self.halves = count, 0, rows, halves
        self.table = jnp.asarray(table, jnp.int32)[here]
        self.ahead = [(order[i], order[(i + 1) % count]) for i in range(count)]
        self.behind = [(b, a) for a, b in self.ahead]
        self.right = self.left = value
        self.blocks = [value]

    def advance(self, *others):
        self.hop += 1
        right, left = self.right, self.left
        half = self.rows // 2
        last = 2 * self.hop == self.count
        if last and self.halves:
            right, left = right[:half], left[half:]
        right = lax.ppermute(right, "fsdp", self.ahead)
        if not last or self.halves:
            left = lax.ppermute(left, "fsdp", self.behind)
        self.right, self.left, *others = lax.optimization_barrier((right, left, *others))
        self.blocks.append(self.right)
        if not last or self.halves:
            self.blocks.append(self.left)
        return others

    def done(self):
        return 2 * self.hop >= self.count


def butterfly(value, axis, bits=None):
    count = lax.axis_size(axis)
    for bit in [1 << i for i in range(count.bit_length() - 1)] if bits is None else bits:
        value = value + lax.ppermute(value, axis, [(i, i ^ bit) for i in range(count)])
    return value


def total_over(value, axis):
    count = lax.axis_size(axis)
    bit = 1
    if (count.bit_length() - 1) % 2:
        value = value + lax.ppermute(value, axis, [(i, i ^ bit) for i in range(count)])
        bit = 2
    while bit < count:
        one, two, three = [
            lax.ppermute(value, axis, [(i, i ^ k) for i in range(count)]) for k in (bit, 2 * bit, 3 * bit)
        ]
        value = (value + one) + (two + three)
        bit *= 4
    return value


def low(x):
    return x.astype(bf16)


def lnn(a, b):
    return nn(low(a), low(b))


def lnt(a, b):
    return nt(low(a), low(b))


def ltn(a, b):
    return tn(low(a), low(b))


def load_w_in(table, pieces, w_in):
    at = pieces[0].shape[1] - w_in.shape[1]
    for i, piece in enumerate(pieces):
        w_in[pl.ds(pl.multiple_of(table[i], 16), piece.shape[0]), :] = piece[:, at:]


def split_out(step, me, table, *refs):
    pieces, out = refs[:-1], refs[-1]
    span = out.shape[1]
    for i, piece in enumerate(pieces):
        row = table[i]
        out[(row // span) ^ me[0], pl.ds(pl.multiple_of(row % span, step), piece.shape[0]), :] = piece[...]


def load_w_out(me, step, quarters, w_out):
    wide = quarters[0].shape[1] // 2
    for k, quarter in enumerate(quarters):
        cols = pl.ds(pl.multiple_of((me[0] ^ k) * wide, 128), wide)
        for j in range(0, quarter.shape[0], step):
            for i in range(2):
                w_out[2 * j + i * step : 2 * j + (i + 1) * step, cols] = quarter[j : j + step, i * wide : (i + 1) * wide]


def rows_of(ref, pieces):
    span = pieces[0].shape[0]
    for k, piece in enumerate(pieces):
        ref[k * span : (k + 1) * span, :] = piece[...].astype(ref.dtype)


def block_order(far_first):
    return (1, (2, 3)) if far_first else (2, (1, 3))


def block_out(far_first, near, single, pair, col, value):
    span = near.shape[0]
    cols = slice(col, col + value.shape[1])
    one, two = block_order(far_first)
    near[:, cols] = value[:span]
    single[:, cols] = low(value[one * span : (one + 1) * span])
    for i, k in enumerate(two):
        pair[i, :, cols] = low(value[k * span : (k + 1) * span])


def tile_masks(size):
    rows = lax.broadcasted_iota(jnp.int32, (size, size), 0)
    columns = lax.broadcasted_iota(jnp.int32, (size, size), 1)
    return rows, columns


def unit_lower_inverses(lowers, inverses, keep):
    size = keep[0].shape[0]
    rows, columns = tile_masks(size)
    eye = jnp.where(rows == columns, 1.0, 0.0).astype(f32)
    block = 1
    while block < size:
        wide = 2 * block
        inside = (rows // wide == columns // wide) & (rows // block != columns // block)
        if block == 1:
            for lower, inverse in zip(lowers, inverses):
                inverse[...] = eye - jnp.where(inside, lower[...], 0.0)
        else:
            for lower, inverse, right in zip(lowers, inverses, keep):
                right[...] = nn(jnp.where(inside, lower[...], 0.0), inverse[...], high)
            for inverse, right in zip(inverses, keep):
                inverse[...] = inverse[...] - nn(inverse[...], right[...], high)
        block = wide


def shifted_rows(value, count, offset):
    if offset == 0:
        return value[:count]
    if offset % 8 == 0:
        return value[offset : offset + count]
    return pltpu.roll(value, value.shape[0] - offset, 0)[:count]


def half_sum(x):
    half = x.shape[1] // 2
    left = jnp.sum(x[:, :half], 1, keepdims=True)
    right = jnp.sum(x[:, half:], 1, keepdims=True)
    lane = lax.broadcasted_iota(jnp.int32, x.shape, 1)
    return jnp.where(lane < half, left, right)


def half_rsqrt(x):
    half = x.shape[1] // 2
    sq = x * x
    left = lax.rsqrt(jnp.sum(sq[:, :half], 1, keepdims=True) + epsilon)
    right = lax.rsqrt(jnp.sum(sq[:, half:], 1, keepdims=True) + epsilon)
    lane = lax.broadcasted_iota(jnp.int32, x.shape, 1)
    return jnp.where(lane < half, left, right)


def conv_block(ext, cw, start, col, span, width):
    window = ext[pl.ds(start, span + 8), col : col + width]
    out = None
    for j in range(4):
        term = shifted_rows(window, span, 5 + j) * cw[j : j + 1, col : col + width]
        out = term if out is None else out + term
    return out


def gates(gs, rb, start, span, col, tri):
    z = gs[pl.ds(start, span), col : col + 128]
    moved = z + rb[1:2, :]
    soft = jnp.maximum(moved, 0.0) + jnp.log(1.0 + jnp.exp(-jnp.abs(moved)))
    return lax.logistic(z), nn(tri, -rb[0:1, :] * soft, high), lax.logistic(moved)


def decay_ratio(c, c_row, inclusive):
    return jnp.where(inclusive, jnp.exp(jnp.where(inclusive, c - c_row, 0.0)), 0.0)


class Layout:
    def __init__(self, width, value_width, hidden, parts):
        counts = [4 * width, 2 * width, value_width, hidden, 4 * value_width, width, 2 * hidden, width]
        at = [sum(counts[:i]) for i in range(8)]
        self.a_in, self.a_gu, self.a_out, self.a_down, self.b_in, self.b_out, self.b_gu, self.b_down = at
        self.total = sum(counts)
        self.width, self.value_width, self.hidden = width, value_width, hidden
        self.own = value_width // parts


def mixer_forward(lay, heads, span, blocks, count, flow, me, table, *refs):
    (x0, x1, x2, x3, gain, a_in, b_in, cw, rb, hg), refs = refs[:10], refs[10:]
    pieces, refs = refs[:count], refs[count:]
    (h1, z_in, pre, gate_out, small_out, gated, ou_out, s_out, tri_out, w_in), scratch = refs[:10], refs[10:]
    gs, ext, state, kqs, vs, keep = scratch

    def weights():
        flow.need(10 + count)
        load_w_in(table, pieces, w_in)
        flow.give(9)

    mixer_prepare(
        lay, heads, span, blocks, flow, me, weights, w_in, (x0, x1, x2, x3, gain, a_in, b_in, cw, rb),
        (h1, z_in, pre, gate_out, small_out, kqs, vs, tri_out), (gs, ext, keep), 10, (0, 1, 2, 3, 4), (8,)
    )
    mixer_advance(heads, span, blocks, me, (gate_out, small_out, kqs, vs, tri_out, rb, hg), (gated, ou_out, s_out), state)


def mixer_first(lay, heads, span, blocks, flow, me, x0, x1, x2, x3, gain, a_in, b_in, cw, rb, w_in,
                h1, z_in, pre, gate_out, small_out, kqs, vs, tri_out, gs, ext, keep):
    mixer_prepare(
        lay, heads, span, blocks, flow, me, partial(flow.need, 10), w_in, (x0, x1, x2, x3, gain, a_in, b_in, cw, rb),
        (h1, z_in, pre, gate_out, small_out, kqs, vs, tri_out), (gs, ext, keep), 9, (0, 1, 2, 3, 4), (5, 6, 7)
    )


def mixer_second(lay, micro, heads, span, blocks, flow, me, kqs, vs, tri, gate_in, small_in, rb, hg, a_out, b_out, w_out,
                 near, single, pair, z_out, gated, ou_out, s_out, state):
    flow.need(7)
    mixer_advance(heads, span, blocks, me, (gate_in, small_in, kqs, vs, tri, rb, hg), (gated, ou_out, s_out), state)
    flow.give(4, 5, 6)
    flow.need(10)
    project_output(lay, micro, gated, a_out, b_out, w_out, near, single, pair, z_out)


def mixer_prepare(lay, heads, span, blocks, flow, me, weights, w_in, ins, outs, scratch, small_ins, early, late):
    x0, x1, x2, x3, gain, a_in, b_in, cw, rb = ins
    h1, z_in, pre, gate_out, small_out, kqs, vs, tri_out = outs
    gs, ext, keep = scratch
    head = 256
    here = me[0]
    own = lay.own
    flow.need(5)
    for k, piece in enumerate((x0, x1, x2, x3)):
        x = piece[...].astype(f32)
        h1[k * span : (k + 1) * span, :] = low(
            x * lax.rsqrt(jnp.mean(x * x, 1, keepdims=True) + epsilon) * gain[...]
        )
    flow.need(small_ins)
    z_in[...] = low(nt(h1[...], a_in[...]))
    weights()
    ext[0:8, :] = jnp.zeros((8, ext.shape[1]), f32)
    for col in range(0, 4 * own + 128, 256):
        wide = min(256, 4 * own + 128 - col)
        value = nn(h1[...], w_in[:, col : col + wide])
        if col < 4 * own:
            value = value + nn(z_in[...], b_in[:, col : col + wide])
        for k in range(blocks):
            part = value[k * span : (k + 1) * span]
            start = pl.multiple_of((k ^ here) * span, span)
            if col < 3 * own:
                part = low(part)
                pre[pl.ds(start, span), col : col + wide] = part
                ext[pl.ds(start + 8, span), col : col + wide] = part.astype(f32)
            else:
                at = col - 3 * own
                if at < own:
                    gate_out[pl.ds(start, span), at : at + wide] = low(part)
                else:
                    small_out[pl.ds(start, span), :] = part
    flow.give(*early)
    grow, gcol = tile_masks(span)
    inclusive = grow >= gcol
    strictly = grow > gcol
    tri = jnp.where(inclusive, 1.0, 0.0).astype(f32)
    scale_k = 0.5**0.5
    scale_q = 128 ** (-0.5) * 0.5**0.5

    def prepare(n, carry):
        start = pl.multiple_of(n * span, span)
        betas, running, _ = gates(small_out, rb, start, span, 0, tri)
        running_t = running.T
        for h in range(heads):
            q = conv_block(ext, cw, start, h * head, span, head)
            k = conv_block(ext, cw, start, (heads + h) * head, span, head)
            v = conv_block(ext, cw, start, (2 * heads + h) * head, span, head)
            q = q * lax.logistic(q)
            k = k * lax.logistic(k)
            vs[h, n] = (v * lax.logistic(v)).astype(vs.dtype)
            q = low(q * (half_rsqrt(q) * scale_q))
            k = low(k * (half_rsqrt(k) * scale_k))
            kqs[h, n, :span] = k
            kqs[h, n, span:] = q
            both = nt(kqs[h, n], k)
            ratio = decay_ratio(running[:, h : h + 1], running_t[h : h + 1, :], inclusive)
            kr = jnp.where(strictly, ratio * both[:span], 0.0)
            tri_out[2, h, n] = low(kr)
            tri_out[1, h, n] = low(both[span:] * ratio)
            keep[1, h * blocks + n] = kr * betas[:, heads + h : heads + h + 1]
        return carry

    lax.fori_loop(0, blocks, prepare, 0)
    pairs = [(h, n) for h in range(heads) for n in range(blocks)]
    unit_lower_inverses(
        [keep.at[1, h * blocks + n] for h, n in pairs],
        [keep.at[2, h * blocks + n] for h, n in pairs],
        [keep.at[0, h * blocks + n] for h, n in pairs],
    )
    for h, n in pairs:
        tri_out[0, h, n] = low(keep[2, h * blocks + n])
    flow.give(*late)


def mixer_advance(heads, span, blocks, me, ins, outs, state):
    gate_in, small_in, kqs, vs, tri_in, rb, hg = ins
    gated, ou_out, s_out = outs
    head = 256
    here = me[0]
    grow, gcol = tile_masks(span)
    tri = jnp.where(grow >= gcol, 1.0, 0.0).astype(f32)
    state[...] = jnp.zeros_like(state)

    def advance(n, carry):
        start = pl.multiple_of(n * span, span)
        row = pl.multiple_of((n ^ here) * span, span)
        betas, running, _ = gates(small_in, rb, start, span, 0, tri)
        for h in range(heads):
            cols = slice(h * head, (h + 1) * head)
            c, b = running[:, h : h + 1], betas[:, heads + h : heads + h + 1]
            d = jnp.exp(c)
            last = c[span - 1 : span, :]
            old = state[h]
            low_old = low(old)
            s_out[h, n] = low_old
            seen = nn(kqs[h, n], low_old)
            u = low(nn(tri_in[0, h, n], low(b * (vs[h, n].astype(f32) - d * seen[:span]))))
            o = d * seen[span:] + nn(tri_in[1, h, n], u)
            ou_out[1, pl.ds(start, span), cols] = u
            ou_out[0, pl.ds(start, span), cols] = low(o)
            weighted = low(kqs[h, n, :span].astype(f32) * jnp.exp(last - c))
            state[h] = jnp.exp(last) * old + tn(weighted, u)
            norm = o * lax.rsqrt(jnp.mean(o * o, 1, keepdims=True) + epsilon) * hg[...]
            gate = gate_in[pl.ds(start, span), cols].astype(f32)
            gated[pl.ds(row, span), cols] = low(norm * (gate * lax.logistic(gate)))
        return carry

    lax.fori_loop(0, blocks, advance, 0)


def project_output(lay, micro, gated, a_out, b_out, w_out, near, single, pair, z_out):
    z_out[...] = low(nt(gated[...], a_out[...]))
    for col in range(0, lay.width, 256):
        value = nn(gated[...], w_out[:, col : col + 256]) + nn(z_out[...], b_out[:, col : col + 256])
        block_out(True, near, single, pair, col, value)


def mixer_output(lay, micro, step, flow, me, gated, a_out, b_out, q0, q1, q2, q3, near, single, pair, z_out, w_out):
    flow.need(7)
    load_w_out(me, step, (q0, q1, q2, q3), w_out)
    flow.give(4)
    project_output(lay, micro, gated, a_out, b_out, w_out, near, single, pair, z_out)


def mixer_backward(lay, micro, heads, span, blocks, windows, flow, me, g0, g1, g2, g3, a_out, b_out, w_out,
                   a_in, b_in, cw, rb, hg, pre, gates_in, small_in, ou_in, s_in, tri_in,
                   z_out, gated, z_in, w_in, h1,
                   ga_gu, g_hidden, gb_down, near, single, pair, send_near, send_single, send_pair,
                   ext, back, dstate, gbranch, dgated, dproj, dsmall, flat):
    head = 256
    here = me[0]
    own = lay.own
    width = lay.width
    flow.need(7)
    rows_of(gbranch, (g0, g1, g2, g3))
    gz_out = low(nt(gbranch[...], b_out[...]))
    for col in range(0, own, 256):
        dgated[:, col : col + 256] = low(
            nt(gbranch[...], w_out[col : col + 256, :]) + nn(gz_out, a_out[:, col : col + 256])
        )
    flow.need(18)
    grow, gcol = tile_masks(span)
    inclusive = grow >= gcol
    strictly = grow > gcol
    tri = jnp.where(inclusive, 1.0, 0.0).astype(f32)
    scale_k = 0.5**0.5
    scale_q = 128 ** (-0.5) * 0.5**0.5
    ext[0:8, :] = jnp.zeros((8, ext.shape[1]), f32)
    ext[8:, :] = pre[...].astype(f32)
    back[...] = jnp.zeros_like(back)
    dstate[...] = jnp.zeros_like(dstate)
    lane = lax.broadcasted_iota(jnp.int32, (span, 128), 1)
    sub = lax.broadcasted_iota(jnp.int32, (span, 128), 0)
    final = lax.broadcasted_iota(jnp.int32, (span, 1), 0) == span - 1

    def step(i, carry):
        n = blocks - 1 - i
        row = pl.multiple_of((n ^ here) * span, span)
        start = pl.multiple_of(n * span, span)
        betas, running, slope = gates(small_in, rb, start, span, 0, tri)
        running_t = running.T
        drunning = jnp.zeros((span, 128), f32)
        by_row = jnp.zeros((span, 128), f32)
        dbetas = jnp.zeros((span, 128), f32)
        for h in range(heads):
            cols = slice(h * head, (h + 1) * head)
            cq = conv_block(ext, cw, start, h * head, span, head)
            ck = conv_block(ext, cw, start, (heads + h) * head, span, head)
            cv = conv_block(ext, cw, start, (2 * heads + h) * head, span, head)
            sq, sk, sv = lax.logistic(cq), lax.logistic(ck), lax.logistic(cv)
            qa, ka, v = cq * sq, ck * sk, cv * sv
            rq, rk = half_rsqrt(qa), half_rsqrt(ka)
            q = qa * (rq * scale_q)
            k = ka * (rk * scale_k)
            kq = jnp.concatenate([low(k), low(q)], 0)
            c = running[:, h : h + 1]
            b = betas[:, heads + h : heads + h + 1]
            d = jnp.exp(c)
            last = c[span - 1 : span, :]
            w = jnp.exp(last - c)
            inv, att = tri_in[0, h, n], tri_in[1, h, n]
            kr = tri_in[2, h, n].astype(f32)
            u = ou_in[1, pl.ds(start, span), cols]
            o = ou_in[0, pl.ds(start, span), cols].astype(f32)
            old = s_in[h, n]
            after = dstate[h]
            gate = gates_in[pl.ds(start, span), cols].astype(f32)
            dy = dgated[pl.ds(row, span), cols].astype(f32)
            sg = lax.logistic(gate)
            r = lax.rsqrt(jnp.mean(o * o, 1, keepdims=True) + epsilon)
            dn = dy * (gate * sg) * hg[...]
            normed = o * r
            dproj[pl.ds(row, span), (3 * heads + h) * head : (3 * heads + h + 1) * head] = low(
                dy * (normed * hg[...]) * (sg * (1.0 + gate * (1.0 - sg)))
            )
            do = r * (dn - normed * jnp.mean(normed * dn, 1, keepdims=True))
            seen = nn(kq, old)
            low_after, low_do = low(after), low(do)
            x = v - d * seen[:span]
            du = tn(att, low_do) + lnn(k * w, low_after)
            datt = jnp.where(inclusive, nt(low_do, u), 0.0)
            dweighted = nt(u, low_after)
            y = ltn(inv, du)
            dlow = jnp.where(strictly, -lnt(y, u), 0.0)
            dx = b * y
            db = jnp.sum(y * x, 1, keepdims=True) + jnp.sum(dlow * kr, 1, keepdims=True)
            dseen = jnp.concatenate([low(-(d * dx)), low(d * do)], 0)
            dstate[h] = jnp.exp(last) * after + tn(kq, dseen)
            dkq = nt(dseen, old)
            dd = jnp.sum(do * seen[span:] - dx * seen[:span], 1, keepdims=True)
            ratio = decay_ratio(c, running_t[h : h + 1, :], inclusive)
            dboth = jnp.concatenate([low(dlow * b * ratio), low(datt * ratio)], 0)
            dkq = dkq + nn(dboth, kq[:span])
            dk = dkq[:span] + tn(dboth, kq) + dweighted * w
            dq = dkq[span:]
            grown = dlow * (b * kr) + datt * att
            dw = jnp.sum(dweighted * k, 1, keepdims=True) * w
            dlast = jnp.exp(last) * jnp.sum(
                jnp.sum(after * old.astype(f32), 1, keepdims=True), 0, keepdims=True
            ) + jnp.sum(dw, 0, keepdims=True)
            dc = jnp.sum(grown, 1, keepdims=True) - dw + dd * d + jnp.where(final, dlast, 0.0)
            drunning = drunning + jnp.where(lane == h, dc, 0.0)
            by_row = by_row + jnp.where(sub == h, jnp.sum(grown, 0, keepdims=True), 0.0)
            dbetas = dbetas + jnp.where(lane == heads + h, db, 0.0)
            dqa = rq * scale_q * dq - qa * (rq * rq * rq * scale_q) * half_sum(qa * dq)
            dka = rk * scale_k * dk - ka * (rk * rk * rk * scale_k) * half_sum(ka * dk)
            for part, grad, sig, act in ((0, dqa, sq, cq), (1, dka, sk, ck), (2, dx, sv, cv)):
                col = (part * heads + h) * head
                through = grad * (sig * (1.0 + act * (1.0 - sig)))
                window = jnp.concatenate([through, back[:, col : col + head]], 0)
                back[:, col : col + head] = through[:8]
                out = None
                for j in range(4):
                    term = shifted_rows(window, span, 3 - j) * cw[j : j + 1, col : col + head]
                    out = term if out is None else out + term
                dproj[pl.ds(row, span), col : col + head] = low(out)
        dlog = tn(tri, drunning - by_row.T, high)
        dsmall[pl.ds(row, span), :] = low(
            -rb[0:1, :] * slope * dlog + dbetas * betas * (1.0 - betas)
        )
        return carry

    lax.fori_loop(0, blocks, step, 0)
    flow.need(26)
    gz_in = low(nt(dproj[...], b_in[...]))
    for col in range(0, width, 256):
        value = (
            nt(dproj[...], w_in[col : col + 256, : 4 * own])
            + nt(dsmall[...], w_in[col : col + 256, 4 * own :])
            + nn(gz_in, a_in[:, col : col + 256])
        )
        block_out(micro == 0, near, single, pair, col, value)
    flow.give(0, 1, 2)
    ga_out = tn(gz_out, gated[...])
    gb_out = tn(z_out[...], gbranch[...])
    flat[...] = jnp.zeros_like(flat)
    ga_in = low(tn(gz_in, h1[...]))
    for p in range(4):
        flat[:, lay.a_in + p * width : lay.a_in + (p + 1) * width] = ga_in[p * RANK : (p + 1) * RANK]
        gb = tn(z_in[...], dproj[:, p * own : (p + 1) * own])
        flat[:, pl.ds(pl.multiple_of(lay.b_in + p * lay.value_width + here * own, 128), own)] = low(
            gb[p * RANK : (p + 1) * RANK]
        )
    flat[:, pl.ds(pl.multiple_of(lay.a_out + here * own, 128), own)] = low(ga_out)
    flat[:, lay.b_out : lay.b_out + width] = low(gb_out)
    for i in range(2):
        flat[:, lay.a_gu + i * width : lay.a_gu + (i + 1) * width] = ga_gu[i * RANK : (i + 1) * RANK, :]
    hidden = lay.hidden
    flat[:, lay.a_down : lay.a_down + hidden] = g_hidden[:RANK, :]
    for i in range(2):
        flat[:, lay.b_gu + i * hidden : lay.b_gu + (i + 1) * hidden] = g_hidden[(i + 1) * RANK : (i + 2) * RANK, :]
    flat[:, lay.b_down : lay.b_down + width] = gb_down[...]
    quarter = send_near.shape[2]
    one, two = block_order(micro == 0)
    sends = {0: send_near, one: send_single, two[0]: send_pair.at[0], two[1]: send_pair.at[1]}
    for k, send in sends.items():
        for f, window in enumerate(windows):
            at = pl.multiple_of(window + (here ^ k) * quarter, 128)
            send[f] = flat[:, pl.ds(at, quarter)]


def feed_forward_blocks(lay, micro, count, flow, table, *refs):
    ins, pieces, rest = refs[:6], refs[6 : 6 + count], refs[6 + count :]
    outs, w_gu, scratch = rest[6:15], rest[15], rest[16:]

    def weights():
        flow.need(6 + count)
        load_w_in(table, pieces, w_gu)
        flow.give(9)

    feed_forward(lay, micro, flow, weights, 12 + count, w_gu, ins, rest[:6], outs, scratch)


def feed_forward_whole(lay, micro, flow, *refs):
    ins, w_gu, rest = refs[:6], refs[6], refs[7:]
    feed_forward(lay, micro, flow, partial(flow.need, 7), 13, w_gu, ins, rest[:6], rest[6:15], rest[15:])


def feed_forward(lay, micro, flow, weights, last_ins, w_gu, ins, more_ins, outs, scratch):
    h0, h1, h2, h3, a_gu, hidden = ins
    g0, g1, g2, g3, b_down, w_down = more_ins
    near, single, pair, gnear, gsingle, gpair, ga_gu, g_own, gb_down = outs
    hs, gs, b_gate, b_up, act, ggate, gup, gates, ups = scratch
    width = lay.width
    wide = act.shape[1]
    flow.need(6)
    rows_of(hs, (h0, h1, h2, h3))
    at = [(3 * micro + i) * RANK for i in range(3)]
    a_down = hidden[at[0] : at[0] + RANK, :]
    b_gate[...] = jnp.zeros_like(b_gate)
    b_up[...] = jnp.zeros_like(b_up)
    b_gate[:RANK, :] = hidden[at[1] : at[1] + RANK, :]
    b_up[RANK:, :] = hidden[at[2] : at[2] + RANK, :]
    z_gu = low(nt(hs[...], a_gu[...]))
    weights()
    for col in range(0, wide, 256):
        cols = slice(col, col + 256)
        gates[:, cols] = nn(hs[...], w_gu[:, cols]) + nn(z_gu, b_gate[:, cols])
        ups[:, cols] = nn(hs[...], w_gu[:, wide + col : wide + col + 256]) + nn(z_gu, b_up[:, cols])
    flow.need(last_ins)
    rows_of(gs, (g0, g1, g2, g3))
    gz_down = low(nt(gs[...], b_down[...]))
    for col in range(0, wide, 256):
        cols = slice(col, col + 256)
        ga, ua = gates[:, cols], ups[:, cols]
        sig = lax.logistic(ga)
        silu = ga * sig
        act[:, cols] = low(silu * ua)
        da = low(nt(gs[...], w_down[cols, :]) + nn(gz_down, a_down[:, cols])).astype(f32)
        ggate[:, cols] = low(da * ua * (sig * (1.0 + ga * (1.0 - sig))))
        gup[:, cols] = low(da * silu)
    gz_gu = low(nt(ggate[...], b_gate[...]) + nt(gup[...], b_up[...]))
    for col in range(0, width, 256):
        cols = slice(col, col + 256)
        value = (
            nt(ggate[...], w_gu[cols, :wide]) + nt(gup[...], w_gu[cols, wide:]) + nn(gz_gu, a_gu[:, cols])
        )
        block_out(micro == 0, gnear, gsingle, gpair, col, value)
    flow.give(3, 4, 5)
    z_down = low(nt(act[...], a_down))
    for col in range(0, width, 256):
        cols = slice(col, col + 256)
        value = nn(act[...], w_down[:, cols]) + nn(z_down, b_down[:, cols])
        block_out(micro == 0, near, single, pair, col, value)
    ga_gu[...] = low(tn(gz_gu, hs[...]))
    gb_down[...] = low(tn(z_down, gs[...]))
    g_own[:RANK, :] = low(tn(gz_down, act[...]))
    g_own[RANK : 2 * RANK, :] = low(tn(z_gu, ggate[...])[:RANK])
    g_own[2 * RANK :, :] = low(tn(z_gu, gup[...])[RANK:])


def adapter_rows(lay, micro_count, windows, flow, me, c0, c1, c2, c3, *refs):
    here = me[0]
    outs, used, flat = refs[:-2], refs[-2], refs[-1]
    width, own, hidden = lay.width, lay.own, lay.hidden
    flat[...] = jnp.zeros_like(flat)
    flow.need(4)
    quarter = c0.shape[2]
    for k, piece in enumerate((c0, c1, c2, c3)):
        for f, window in enumerate(windows):
            cols = pl.ds(pl.multiple_of(window + (here ^ k) * quarter, 128), quarter)
            flat[:, cols] = flat[:, cols] + piece[f]

    def own_columns(rows, at):
        return flat[rows, pl.ds(pl.multiple_of(at + here * own, 128), own)]

    for m in range(micro_count):
        rows = slice(m * RANK, (m + 1) * RANK)
        a_in, b_in, a_gu, a_out, b_out, b_down = outs[6 * m : 6 * (m + 1)]
        b_in[...] = jnp.zeros_like(b_in)
        for p in range(4):
            part = slice(p * RANK, (p + 1) * RANK)
            a_in[part, :] = flat[rows, lay.a_in + p * width : lay.a_in + (p + 1) * width]
            b_in[part, p * own : (p + 1) * own] = own_columns(rows, lay.b_in + p * lay.value_width)
        for i in range(2):
            a_gu[i * RANK : (i + 1) * RANK, :] = flat[rows, lay.a_gu + i * width : lay.a_gu + (i + 1) * width]
        a_out[...] = own_columns(rows, lay.a_out)
        b_out[...] = flat[rows, lay.b_out : lay.b_out + width]
        b_down[...] = flat[rows, lay.b_down : lay.b_down + width]
        for i, at in enumerate((lay.a_down, lay.b_gu, lay.b_gu + hidden)):
            used[(3 * m + i) * RANK : (3 * m + i + 1) * RANK, :] = flat[rows, at : at + hidden]


SMEM = pl.BlockSpec(memory_space=pltpu.SMEM)
VMEM = pl.BlockSpec(memory_space=pltpu.VMEM)


class Flow:
    def __init__(self, stages, far_in, near_in, far_out, near_out, sems):
        self.coming = [
            pltpu.make_async_copy(far, near, sems.at[i]) for i, (far, near) in enumerate(zip(far_in, near_in))
        ]
        at = len(self.coming)
        self.going = [
            pltpu.make_async_copy(near, far, sems.at[at + i]) for i, (far, near) in enumerate(zip(far_out, near_out))
        ]
        self.sent, self.stages = set(), list(stages) + [len(self.coming)]
        self.started = self.ready = 0
        self.start()

    def start(self):
        if self.stages:
            upto = self.stages.pop(0)
            for copy in self.coming[self.started : upto]:
                copy.start()
            self.started = upto

    def need(self, upto):
        while self.ready < upto:
            if self.ready == self.started:
                self.start()
            self.coming[self.ready].wait()
            self.ready += 1
            if self.ready == self.started:
                self.start()

    def give(self, *which):
        for i in which:
            if i not in self.sent:
                self.sent.add(i)
                self.going[i].start()

    def close(self):
        self.need(len(self.coming))
        self.give(*range(len(self.going)))
        for copy in self.going:
            copy.wait()


def flowing(body, stages, scalars, arrays, results, *refs):
    smem, refs = refs[:scalars], refs[scalars:]
    far_in, refs = refs[:arrays], refs[arrays:]
    far_out, refs = refs[:results], refs[results:]
    near_in, refs = refs[:arrays], refs[arrays:]
    near_out, refs = refs[:results], refs[results:]
    sems, scratch = refs[0], refs[1:]
    flow = Flow(stages, far_in, near_in, far_out, near_out, sems)
    body(flow, *smem, *near_in, *near_out, *scratch)
    flow.close()


def kernel_call(body, name, out_shape, scratch, args, scalars=1, flops=0, stages=()):
    size = sum(a.size * a.dtype.itemsize for a in args) + sum(o.size * o.dtype.itemsize for o in out_shape)
    arrays = args[scalars:]
    far = pl.BlockSpec(memory_space=pl.ANY)
    buffers = [pltpu.VMEM(a.shape, a.dtype) for a in (*arrays, *out_shape)]
    return pl.pallas_call(
        partial(flowing, body, stages, scalars, len(arrays), len(out_shape)),
        out_shape=tuple(out_shape),
        in_specs=[SMEM] * scalars + [far] * len(arrays),
        out_specs=tuple([far] * len(out_shape)),
        scratch_shapes=[*buffers, pltpu.SemaphoreType.DMA((len(buffers),)), *scratch],
        compiler_params=pltpu.CompilerParams(vmem_limit_bytes=VMEM_LIMIT),
        cost_estimate=pl.CostEstimate(flops=flops, bytes_accessed=int(size), transcendentals=0),
        name=name,
    )(*args)


class Kernels:
    def __init__(self, lay, heads, head, span, blocks, width, own, wide, windows, quarter, flat, ranks, step):
        shape = jax.ShapeDtypeStruct
        rows = blocks * span
        self.lay, self.sizes = lay, (heads, span, blocks)
        self.windows, self.step = windows, step
        self.blocks = [shape((span, width), f32), shape((span, width), bf16), shape((2, span, width), bf16)]
        send = (ranks, RANK, quarter)
        self.sends = [shape(send, bf16), shape(send, bf16), shape((2, *send), bf16)]
        self.z_out = shape((rows, RANK), bf16)
        self.saved = [
            shape((rows, width), bf16),
            shape((rows, 4 * RANK), bf16),
            shape((rows, 3 * own), bf16),
            shape((rows, own), bf16),
            shape((rows, 128), f32),
            shape((rows, own), bf16),
            shape((2, rows, own), bf16),
            shape((heads, blocks, head, head), bf16),
            shape((3, heads, blocks, span, span), bf16),
        ]
        self.small = [shape((2 * RANK, width), bf16), shape((3 * RANK, wide), bf16), shape((RANK, width), bf16)]
        self.w_gu = shape((width, 2 * wide), bf16)
        self.w_in, self.w_out = shape((width, 4 * own + 128), bf16), shape((own, width), bf16)
        ext = pltpu.VMEM((rows + 8, 3 * own), f32)
        state = pltpu.VMEM((heads, head, head), f32)
        self.kq = shape((heads, blocks, 2 * span, head), bf16)
        self.v = shape((heads, blocks, span, head), bf16)
        keep = pltpu.VMEM((3, heads * blocks, span, span), f32)
        self.state = state
        self.first_scratch = [pltpu.VMEM((8, 128), f32), ext, keep]
        self.forward_scratch = [
            pltpu.VMEM((8, 128), f32),
            ext,
            state,
            pltpu.VMEM(self.kq.shape, bf16),
            pltpu.VMEM(self.v.shape, f32),
            keep,
        ]
        self.feed_scratch = (
            [pltpu.VMEM((rows, width), bf16)] * 2
            + [pltpu.VMEM((2 * RANK, wide), bf16)] * 2
            + [pltpu.VMEM((rows, wide), bf16)] * 3
            + [pltpu.VMEM((rows, wide), f32)] * 2
        )
        self.backward_scratch = [
            ext,
            pltpu.VMEM((8, 3 * own), f32),
            state,
            pltpu.VMEM((rows, width), bf16),
            pltpu.VMEM((rows, own), bf16),
            pltpu.VMEM((rows, 4 * own), bf16),
            pltpu.VMEM((rows, 128), bf16),
            pltpu.VMEM((RANK, flat), bf16),
        ]

    def forward(self, m, me, table, w_in, x, gain, adapters, cw, rb, hg):
        outs = kernel_call(
            partial(mixer_forward, self.lay, *self.sizes, len(w_in)),
            "mixer_forward",
            self.saved + [self.w_in],
            self.forward_scratch,
            (me, table, *x, gain, *adapters, cw, rb, hg, *w_in),
            scalars=2,
            stages=(5,),
            flops=6_000_000_000,
        )
        return outs[:-1], outs[-1]

    def first(self, m, me, w_in, x, gain, adapters, cw, rb):
        return kernel_call(
            partial(mixer_first, self.lay, *self.sizes),
            "mixer_first",
            self.saved[:5] + [self.kq, self.v, self.saved[8]],
            self.first_scratch,
            (me, *x, gain, *adapters, cw, rb, w_in),
            stages=(5,),
            flops=5_000_000_000,
        )

    def second(self, m, me, w_out, done, adapters, rb, hg):
        h1, z_in, pre, gate, small, kq, v, tri = done
        outs = kernel_call(
            partial(mixer_second, self.lay, m, *self.sizes),
            "mixer_second",
            self.blocks + [self.z_out] + self.saved[5:8],
            [self.state],
            (me, kq, v, tri, gate, small, rb, hg, *adapters, w_out),
            flops=3_000_000_000,
        )
        return outs[:3], outs[3], (h1, z_in, pre, gate, small, *outs[4:], tri)

    def output(self, m, me, w_out, gated, adapters):
        outs = kernel_call(
            partial(mixer_output, self.lay, m, self.step),
            "mixer_output",
            self.blocks + [self.z_out, self.w_out],
            [],
            (me, gated, *adapters, *w_out),
            flops=1_000_000_000,
        )
        return outs[:3], outs[3], outs[4]

    def feed(self, m, table, h2, cot, w_gu, w_down, a_gu, b_down, hidden):
        whole = len(w_gu) == 1
        outs = kernel_call(
            partial(feed_forward_whole, self.lay, m) if whole else partial(feed_forward_blocks, self.lay, m, len(w_gu)),
            "feed_forward",
            self.blocks * 2 + self.small + ([] if whole else [self.w_gu]),
            self.feed_scratch,
            (*([] if whole else [table]), *h2, a_gu, hidden, *w_gu, *cot, b_down, w_down),
            scalars=0 if whole else 1,
            stages=(6, 6 + len(w_gu)),
            flops=5_000_000_000,
        )
        return outs[:3], outs[3:6], outs[6:9], w_gu[0] if whole else outs[9]

    def backward(self, m, me, w_in, w_out, g_branch, in_adapters, out_adapters, cw, rb, hg, z_out, saved, small):
        h1, z_in, pre, gates_in, small_in, gated, ou_in, s_in, tri_in = saved
        outs = kernel_call(
            partial(mixer_backward, self.lay, m, *self.sizes, self.windows),
            "mixer_backward",
            self.blocks + self.sends,
            self.backward_scratch,
            (
                me,
                *g_branch,
                *out_adapters,
                w_out,
                *in_adapters,
                cw,
                rb,
                hg,
                pre,
                gates_in,
                small_in,
                ou_in,
                s_in,
                tri_in,
                z_out,
                gated,
                z_in,
                w_in,
                h1,
                *small,
            ),
            stages=(7, 18),
            flops=9_000_000_000,
        )
        return outs[:3], outs[3:]


def rms_norm(inputs, scales):
    return inputs * lax.rsqrt(jnp.mean(inputs * inputs, -1, keepdims=True) + epsilon) * scales


def own_lanes(value, start, size):
    return lax.dynamic_slice_in_dim(value, start, size, axis=value.ndim - 1)


def shards(
    tokens,
    cotangent,
    lengths,
    adapter_index,
    step_count,
    w_in,
    w_out,
    w_gu,
    w_down,
    conv_weight,
    norm_gains,
    head_gain,
    decay_rate,
    decay_bias,
    adapters,
    first_moment,
    second_moment,
):
    micro_count, _, span, width = tokens.shape
    ranks = lax.axis_size("fsdp")
    parts = lax.axis_size("seq")
    here = lax.axis_index("seq")
    place = lax.axis_index("fsdp")
    all_heads = decay_rate.shape[0]
    heads = all_heads // parts
    value_width = conv_weight.shape[1] // 3
    own = value_width // parts
    hidden = w_gu.shape[1] // 2
    piece = w_down.shape[0] // parts
    wide = -(-hidden // parts // 256) * 256
    padded = wide // ranks
    columns = adapters.shape[1]
    shard_rows = adapters.shape[0]
    rows = parts * span
    me = here.astype(jnp.int32).reshape(1)
    lay = Layout(width, value_width, hidden, parts)
    shape = jax.ShapeDtypeStruct

    def heads_slice(part):
        return own_lanes(w_in, part * value_width + here * own, own)

    small = jnp.concatenate(
        [
            own_lanes(w_in, 4 * value_width + here * heads, heads),
            own_lanes(w_in, 4 * value_width + all_heads + here * heads, heads),
            jnp.zeros((w_in.shape[0], 128 - 2 * heads), bf16),
        ],
        1,
    )
    in_rows = w_in.shape[0]
    local_out = own_lanes(w_out, here * (width // parts), width // parts)
    local_in = jnp.concatenate(
        [local_out[:in_rows], local_out[in_rows:]] + [heads_slice(p) for p in range(4)] + [small], 1
    )
    ring = RingGather(local_in)

    window = -(-(shard_rows + 127) // (128 * parts)) * 128 * parts
    quarter = window // parts
    windows = [shard_rows * f // 128 * 128 for f in range(ranks)]
    flat_width = windows[-1] + window
    offset = (shard_rows * place) % 128
    picks = lax.dynamic_update_slice(
        jnp.zeros((ranks, 128), jnp.int32), jnp.pad(adapter_index.T, ((0, 0), (0, 128 - micro_count))), (place, 0)
    )
    bits = [1 << i for i in range(ranks.bit_length() - 1)]
    picks = butterfly(picks, "fsdp", bits[:2])
    framed = lax.dynamic_update_slice(
        jnp.zeros((window, columns), bf16), adapters.astype(bf16), (offset, 0)
    )
    framed = lax.dynamic_slice_in_dim(framed, here * quarter, quarter, 0)
    conv_own = jnp.concatenate(
        [own_lanes(conv_weight, p * value_width + here * own, own) for p in range(3)], 1
    )
    rate_bias = jnp.zeros((8, 128), f32)
    rate_bias = rate_bias.at[0, :heads].set(lax.dynamic_slice(decay_rate, (here * heads,), (heads,)))
    rate_bias = rate_bias.at[1, :heads].set(lax.dynamic_slice(decay_bias, (here * heads,), (heads,)))
    gain_row = head_gain.reshape(1, -1)

    far_tokens = [gather_far(tokens[m, 0]) for m in range(micro_count)]
    positions = here * span + jnp.arange(span)
    cots = [
        cotangent[m, 0].astype(f32) * (positions < lengths[m, 0]).astype(f32)[:, None]
        for m in range(micro_count)
    ]
    framed, conv_own, rate_bias, table, picks = ring.advance(
        framed, conv_own, rate_bias, ring.table, picks
    )
    picks = butterfly(picks, "fsdp", bits[2:])
    wanted = (picks[:, :micro_count, None] * RANK + jnp.arange(RANK)[None, None, :]).reshape(-1)
    select = (wanted[:, None] == jnp.arange(columns)[None, :]).astype(bf16)
    chosen = nt(select, framed).astype(bf16).reshape(ranks, micro_count * RANK, quarter)
    chosen = lax.all_to_all(chosen, "fsdp", 0, 0)

    unit = after(jnp.arange(wide), ring.right)
    unit_of = (unit // padded) * w_down.shape[0] + here * piece + unit % padded
    unit_of = jnp.where(unit % padded < piece, unit_of, -1)
    spread = (jnp.arange(hidden)[:, None] == unit_of[None, :]).astype(bf16)
    local_gu = jnp.concatenate(
        [nn(w_gu[:, i * hidden : (i + 1) * hidden], spread).astype(bf16) for i in range(2)], 1
    )
    local_down = jnp.pad(
        lax.dynamic_slice_in_dim(w_down, here * piece, piece, 0), ((0, padded - piece), (0, 0))
    )
    pieces = [gather_near(*far) for far in far_tokens]
    far_cots = [gather_far(low(cot)) for cot in cots]
    chosen, local_gu, local_down, pieces, far_cots = ring.advance(
        chosen, local_gu, local_down, pieces, far_cots
    )
    cot_pieces = [gather_near(*far) for far in far_cots]

    chosen, beyond = gather_far(chosen)
    chosen, beyond, cot_pieces = ring.advance(chosen, beyond, cot_pieces)
    (chosen,) = ring.advance(gather_near(chosen, beyond))
    while not ring.done():
        ring.advance()
    quarter_width = 2 * (width // parts)
    out_sorted = pl.pallas_call(
        partial(split_out, min(block.shape[0] for block in ring.blocks)),
        grid=(1,),
        out_shape=shape((parts, width // parts, quarter_width), bf16),
        in_specs=[SMEM, SMEM]
        + [pl.BlockSpec((block.shape[0], quarter_width), lambda i: (0, 0)) for block in ring.blocks],
        out_specs=pl.BlockSpec((parts, width // parts, quarter_width), lambda i: (0, 0, 0)),
        name="split_out",
    )(me, table, *ring.blocks)
    out_quarters = [swapped(out_sorted[k], k) if k else out_sorted[k] for k in range(parts)]
    per_micro = [
        shape((4 * RANK, width), bf16),
        shape((4 * RANK, 4 * own), bf16),
        shape((2 * RANK, width), bf16),
        shape((RANK, own), bf16),
        shape((RANK, width), bf16),
        shape((RANK, width), bf16),
    ]
    *adapted, used = kernel_call(
        partial(adapter_rows, lay, micro_count, windows),
        "adapter_rows",
        per_micro * micro_count + [shape((3 * micro_count * RANK, hidden), bf16)],
        [pltpu.VMEM((micro_count * RANK, flat_width), bf16)],
        (me, *chosen),
    )
    adapted = [adapted[6 * m : 6 * (m + 1)] for m in range(micro_count)]
    hidden_own = nn(used, spread).astype(bf16)
    second_ring = RingGather(after(local_gu, ring.right))
    full_down = lax.all_gather(after(local_down, ring.right), "fsdp", axis=0, tiled=True)

    first_gain = norm_gains[0].reshape(1, -1)
    micros = range(micro_count)
    inputs = [tokens[m, 0].astype(f32) for m in micros]
    kernels = Kernels(
        lay, heads, head_gain.shape[0], span, parts, width, own, wide, windows, quarter, flat_width, ranks, in_rows
    )

    def feed(m, h2, cot, w_gu):
        return kernels.feed(m, table, h2, cot, w_gu, full_down, adapted[m][2], adapted[m][5], hidden_own)

    def backward(m, g_branch, z_out, saved, small_grads):
        return kernels.backward(
            m,
            me,
            full_in,
            full_out,
            g_branch,
            adapted[m][:2],
            adapted[m][3:5],
            conv_own,
            rate_bias,
            gain_row,
            z_out,
            saved,
            small_grads,
        )

    def second_norm(middle):
        h2, pull = jax.vjp(partial(rms_norm, scales=norm_gains[1]), middle)
        return low(h2), pull

    def input_gradient(m, g_middle, g_h1):
        pull = jax.vjp(partial(rms_norm, scales=norm_gains[0]), inputs[m])[1]
        return low(g_middle + pull(low(g_h1).astype(f32))[0])

    saved0, full_in = kernels.forward(
        0, me, table, ring.blocks, pieces[0], first_gain, adapted[0][:2], conv_own, rate_bias, gain_row
    )
    (saved0,) = second_ring.advance(saved0)
    out0, z_out0, full_out = kernels.output(0, me, out_quarters, saved0[5], adapted[0][3:5])
    got0 = scatter_far(out0[2])
    begun1 = kernels.first(1, me, full_in, pieces[1], first_gain, adapted[1][:2], conv_own, rate_bias)
    got0, begun1 = second_ring.advance(got0, begun1)
    middle0 = inputs[0] + scatter_near(out0[0], out0[1], got0)
    h20, pull0 = second_norm(middle0)
    far0 = gather_far(h20)
    begun1 = held(begun1, h20)
    out1, z_out1, saved1 = kernels.second(1, me, full_out, begun1, adapted[1][3:5], rate_bias, gain_row)
    far0, out1 = second_ring.advance(far0, out1)
    (h20,) = second_ring.advance(gather_near(*far0))
    while not second_ring.done():
        second_ring.advance()
    got1 = scatter_far(out1[2])
    last0, g_out0, grads0, full_gu = feed(0, h20, cot_pieces[0], second_ring.blocks)
    got1, last0, g_out0, grads0 = held((got1, last0, g_out0, grads0))
    middle1 = inputs[1] + scatter_near(out1[0], out1[1], got1)
    h21, pull1 = second_norm(middle1)
    h21 = gather_seq(h21)
    g_out0, h21 = held((g_out0, h21))
    g_got0 = scatter_far(g_out0[2])
    last1, g_out1, grads1, full_gu = feed(1, h21, cot_pieces[1], [full_gu])
    g_got0, last1, g_out1, grads1 = held((g_got0, last1, g_out1, grads1))
    g_h20 = scatter_near(g_out0[0], g_out0[1], g_got0)
    g_middle0 = cots[0] + pull0(low(g_h20).astype(f32))[0]
    branch0 = gather_far(low(g_middle0))
    hidden0, hidden1 = [nt(g[1], spread).astype(bf16) for g in (grads0, grads1)]
    branch0, hidden0, hidden1 = held((branch0, hidden0, hidden1))
    branch0 = gather_near(*branch0)
    g_h21 = after(scatter_seq(*g_out1), branch0[2])
    g_middle1 = cots[1] + pull1(low(g_h21).astype(f32))[0]
    branch0, g_middle1, last0 = held((branch0, g_middle1, last0))
    far1 = gather_far(low(g_middle1))
    last_got0 = scatter_far(last0[2])
    g_in0, sums0 = backward(0, branch0, z_out0, saved0, (grads0[0], hidden0, grads0[2]))
    far1, last_got0, g_in0, sums0 = held((far1, last_got0, g_in0, sums0))
    branch1 = gather_near(*far1)
    mixed0 = low(middle0 + scatter_near(last0[0], last0[1], last_got0))
    sums_got0 = scatter_far(sums0[2])
    g_in_got0 = scatter_far(g_in0[2])
    g_in1, sums1 = backward(1, branch1, z_out1, saved1, (grads1[0], hidden1, grads1[2]))
    sums_got0, g_in_got0, g_in1, sums1 = held((sums_got0, g_in_got0, g_in1, sums1))
    mixed1 = low(middle1 + scatter_seq(*last1))
    total1 = low(scatter_seq(sums1[0].astype(f32), *sums1[1:]))
    total0 = low(scatter_near(sums0[0].astype(f32), sums0[1], sums_got0))
    grad_tokens0 = input_gradient(0, g_middle0, scatter_near(g_in0[0], g_in0[1], g_in_got0))
    grad_tokens1 = input_gradient(1, g_middle1, scatter_seq(*g_in1))
    arrived = lax.all_to_all(jnp.concatenate([total0, total1], 1), "fsdp", 0, 0)
    mine = tn(arrived.reshape(-1, quarter), select)
    at = here * quarter + jnp.arange(quarter)
    mine = jnp.where(((at >= offset) & (at < offset + shard_rows))[:, None], mine, 0.0)
    squares = jnp.full((8, 128), jnp.sum(mine * mine))
    shard_grad = jnp.concatenate(in_seq_order(gather_seq(low(mine))), 0)
    squares = total_over(squares, "seq")
    squares, shard_grad = held((squares, shard_grad))
    squares = total_over(squares, "fsdp")[0, 0]
    shard_grad = lax.dynamic_slice_in_dim(shard_grad, offset, shard_rows, 0).astype(f32)
    norm_value = jnp.sqrt(squares)
    clipped = shard_grad * (CLIP_LIMIT / jnp.maximum(norm_value, CLIP_LIMIT))
    new_first = FIRST_DECAY * first_moment + (1.0 - FIRST_DECAY) * clipped
    new_second = SECOND_DECAY * second_moment + (1.0 - SECOND_DECAY) * clipped * clipped
    counter = step_count[0].astype(f32)
    corrected_first = new_first / (1.0 - jnp.power(FIRST_DECAY, counter))
    corrected_second = new_second / (1.0 - jnp.power(SECOND_DECAY, counter))
    update = -LEARN_RATE * (
        corrected_first / (jnp.sqrt(corrected_second) + ADAM_EPSILON) + WEIGHT_DECAY * adapters
    )
    return (
        jnp.stack([mixed0, mixed1], 0)[:, None],
        jnp.stack([grad_tokens0, grad_tokens1], 0)[:, None],
        update,
        new_first,
        new_second,
        norm_value.reshape(1),
    )


def solution(mesh):
    in_specs = (
        P(None, "fsdp", "seq", None),
        P(None, "fsdp", "seq", None),
        P(None, "fsdp"),
        P(None, "fsdp"),
        P(),
        P("fsdp", None),
        P("fsdp", None),
        P("fsdp", None),
        P("fsdp", None),
        P(),
        P(),
        P(),
        P(),
        P(),
        P("fsdp", None),
        P("fsdp", None),
        P("fsdp", None),
    )
    out_specs = (
        P(None, "fsdp", "seq", None),
        P(None, "fsdp", "seq", None),
        P("fsdp", None),
        P("fsdp", None),
        P("fsdp", None),
        P(),
    )
    return jax.shard_map(shards, mesh=mesh, in_specs=in_specs, out_specs=out_specs, check_vma=False)
```

```python
from functools import partial

import jax
import jax.numpy as jnp
from jax import lax
from jax.experimental import pallas as pl
from jax.experimental.pallas import tpu as pltpu
from jax.sharding import PartitionSpec as P

RANK = 16
epsilon = 1e-06
CLIP_LIMIT = 1.0
LEARN_RATE = 0.01
FIRST_DECAY = 0.9
SECOND_DECAY = 0.999
ADAM_EPSILON = 1e-08
WEIGHT_DECAY = 0.1
VMEM_LIMIT = 56 << 20

f32 = jnp.float32
bf16 = jnp.bfloat16
high = lax.Precision.HIGH


def nn(a, b, precision=None):
    return lax.dot_general(
        a, b, (((1,), (0,)), ((), ())), precision=precision, preferred_element_type=f32
    )


def nt(a, b, precision=None):
    return lax.dot_general(
        a, b, (((1,), (1,)), ((), ())), precision=precision, preferred_element_type=f32
    )


def tn(a, b, precision=None):
    return lax.dot_general(
        a, b, (((0,), (0,)), ((), ())), precision=precision, preferred_element_type=f32
    )


def swapped(value, bit):
    count = lax.axis_size("seq")
    return lax.ppermute(value, "seq", [(i, i ^ bit) for i in range(count)])


def gather_far(value):
    return value, swapped(value, 2)


def gather_near(value, beyond):
    return value, swapped(value, 1), beyond, swapped(beyond, 1)


def gather_seq(value):
    return gather_near(*gather_far(value))


def in_seq_order(blocks):
    here = lax.axis_index("seq")
    for bit in (1, 2):
        flip = here & bit != 0
        blocks = [jnp.where(flip, blocks[k ^ bit], blocks[k]) for k in range(4)]
    return blocks


def scatter_far(far):
    return swapped(far, 2)


def scatter_near(near, beside, got):
    got = got.astype(f32)
    return near + got[0] + swapped((beside.astype(f32) + got[1]).astype(bf16), 1).astype(f32)


def scatter_seq(near, beyond, pair):
    got = swapped(pair, 1).astype(f32)
    return near + got[0] + swapped((beyond.astype(f32) + got[1]).astype(bf16), 2).astype(f32)


def held(values, *others):
    return lax.optimization_barrier((tuple(values), *others))[0]


def ring_order(count):
    return list(range(0, count, 2)) + list(range(count - 1, 0, -2))


def after(value, *others):
    return lax.optimization_barrier((value, *others))[0]


class RingGather:
    def __init__(self, value):
        count, here = lax.axis_size("fsdp"), lax.axis_index("fsdp")
        order = ring_order(count)
        place = [order.index(d) for d in range(count)]
        rows = value.shape[0]
        halves = rows // 2 % 16 == 0
        table = []
        for d in range(count):
            source = [order[(place[d] - k) % count] * rows for k in range(count)]
            at = [source[0]]
            for hop in range(1, count // 2 + 1):
                last = 2 * hop == count
                at.append(source[hop])
                if not last:
                    at.append(source[count - hop])
                elif halves:
                    at.append(source[hop] + rows // 2)
            table.append(at)
        self.count, self.hop, self.rows, self.halves = count, 0, rows, halves
        self.table = jnp.asarray(table, jnp.int32)[here]
        self.ahead = [(order[i], order[(i + 1) % count]) for i in range(count)]
        self.behind = [(b, a) for a, b in self.ahead]
        self.right = self.left = value
        self.blocks = [value]

    def advance(self, *others):
        self.hop += 1
        right, left = self.right, self.left
        half = self.rows // 2
        last = 2 * self.hop == self.count
        if last and self.halves:
            right, left = right[:half], left[half:]
        right = lax.ppermute(right, "fsdp", self.ahead)
        if not last or self.halves:
            left = lax.ppermute(left, "fsdp", self.behind)
        self.right, self.left, *others = lax.optimization_barrier((right, left, *others))
        self.blocks.append(self.right)
        if not last or self.halves:
            self.blocks.append(self.left)
        return others

    def done(self):
        return 2 * self.hop >= self.count


def butterfly(value, axis, bits=None):
    count = lax.axis_size(axis)
    for bit in [1 << i for i in range(count.bit_length() - 1)] if bits is None else bits:
        value = value + lax.ppermute(value, axis, [(i, i ^ bit) for i in range(count)])
    return value


def total_over(value, axis):
    count = lax.axis_size(axis)
    bit = 1
    if (count.bit_length() - 1) % 2:
        value = value + lax.ppermute(value, axis, [(i, i ^ bit) for i in range(count)])
        bit = 2
    while bit < count:
        one, two, three = [
            lax.ppermute(value, axis, [(i, i ^ k) for i in range(count)]) for k in (bit, 2 * bit, 3 * bit)
        ]
        value = (value + one) + (two + three)
        bit *= 4
    return value


def low(x):
    return x.astype(bf16)


def lnn(a, b):
    return nn(low(a), low(b))


def lnt(a, b):
    return nt(low(a), low(b))


def ltn(a, b):
    return tn(low(a), low(b))


def load_w_in(table, pieces, w_in):
    at = pieces[0].shape[1] - w_in.shape[1]
    for i, piece in enumerate(pieces):
        w_in[pl.ds(pl.multiple_of(table[i], 16), piece.shape[0]), :] = piece[:, at:]


def split_out(step, me, table, *refs):
    pieces, outs = refs[:-4], refs[-4:]
    span = outs[0].shape[0]
    for i, piece in enumerate(pieces):
        row = table[i]
        for k, out in enumerate(outs):

            @pl.when((row // span) ^ me[0] == k)
            def _():
                out[pl.ds(pl.multiple_of(row % span, step), piece.shape[0]), :] = piece[...]


def load_w_out(me, step, quarters, w_out):
    wide = quarters[0].shape[1] // 2
    for k, quarter in enumerate(quarters):
        cols = pl.ds(pl.multiple_of((me[0] ^ k) * wide, 128), wide)
        for j in range(0, quarter.shape[0], step):
            for i in range(2):
                w_out[2 * j + i * step : 2 * j + (i + 1) * step, cols] = quarter[j : j + step, i * wide : (i + 1) * wide]


def rows_of(ref, pieces):
    span = pieces[0].shape[0]
    for k, piece in enumerate(pieces):
        ref[k * span : (k + 1) * span, :] = piece[...].astype(ref.dtype)


def block_order(far_first):
    return (1, (2, 3)) if far_first else (2, (1, 3))


def block_out(far_first, near, single, pair, col, value):
    span = near.shape[0]
    cols = slice(col, col + value.shape[1])
    one, two = block_order(far_first)
    near[:, cols] = value[:span]
    single[:, cols] = low(value[one * span : (one + 1) * span])
    for i, k in enumerate(two):
        pair[i, :, cols] = low(value[k * span : (k + 1) * span])


def tile_masks(size):
    rows = lax.broadcasted_iota(jnp.int32, (size, size), 0)
    columns = lax.broadcasted_iota(jnp.int32, (size, size), 1)
    return rows, columns


def unit_lower_inverses(lowers, inverses, keep):
    size = keep[0].shape[0]
    rows, columns = tile_masks(size)
    eye = jnp.where(rows == columns, 1.0, 0.0).astype(f32)
    block = 1
    while block < size:
        wide = 2 * block
        inside = (rows // wide == columns // wide) & (rows // block != columns // block)
        if block == 1:
            for lower, inverse in zip(lowers, inverses):
                inverse[...] = eye - jnp.where(inside, lower[...], 0.0)
        else:
            for lower, inverse, right in zip(lowers, inverses, keep):
                right[...] = nn(jnp.where(inside, lower[...], 0.0), inverse[...], high)
            for inverse, right in zip(inverses, keep):
                inverse[...] = inverse[...] - nn(inverse[...], right[...], high)
        block = wide


def shifted_rows(value, count, offset):
    if offset == 0:
        return value[:count]
    if offset % 8 == 0:
        return value[offset : offset + count]
    return pltpu.roll(value, value.shape[0] - offset, 0)[:count]


def half_sum(x):
    half = x.shape[1] // 2
    left = jnp.sum(x[:, :half], 1, keepdims=True)
    right = jnp.sum(x[:, half:], 1, keepdims=True)
    lane = lax.broadcasted_iota(jnp.int32, x.shape, 1)
    return jnp.where(lane < half, left, right)


def half_rsqrt(x):
    half = x.shape[1] // 2
    sq = x * x
    left = lax.rsqrt(jnp.sum(sq[:, :half], 1, keepdims=True) + epsilon)
    right = lax.rsqrt(jnp.sum(sq[:, half:], 1, keepdims=True) + epsilon)
    lane = lax.broadcasted_iota(jnp.int32, x.shape, 1)
    return jnp.where(lane < half, left, right)


def conv_block(ext, cw, start, col, span, width):
    window = ext[pl.ds(start, span + 8), col : col + width]
    out = None
    for j in range(4):
        term = shifted_rows(window, span, 5 + j) * cw[j : j + 1, col : col + width]
        out = term if out is None else out + term
    return out


def gates(gs, rb, start, span, col, tri):
    z = gs[pl.ds(start, span), col : col + 128]
    moved = z + rb[1:2, :]
    soft = jnp.maximum(moved, 0.0) + jnp.log(1.0 + jnp.exp(-jnp.abs(moved)))
    return lax.logistic(z), nn(tri, -rb[0:1, :] * soft, high), lax.logistic(moved)


def decay_ratio(c, c_row, inclusive):
    return jnp.where(inclusive, jnp.exp(jnp.where(inclusive, c - c_row, 0.0)), 0.0)


class Layout:
    def __init__(self, width, value_width, hidden, parts):
        counts = [4 * width, 2 * width, value_width, hidden, 4 * value_width, width, 2 * hidden, width]
        at = [sum(counts[:i]) for i in range(8)]
        self.a_in, self.a_gu, self.a_out, self.a_down, self.b_in, self.b_out, self.b_gu, self.b_down = at
        self.total = sum(counts)
        self.width, self.value_width, self.hidden = width, value_width, hidden
        self.own = value_width // parts


def mixer_forward(lay, heads, span, blocks, count, flow, me, table, *refs):
    (x0, x1, x2, x3, gain, a_in, b_in, cw, rb, hg), refs = refs[:10], refs[10:]
    pieces, refs = refs[:count], refs[count:]
    (h1, z_in, pre, gate_out, small_out, gated, ou_out, s_out, tri_out, w_in), scratch = refs[:10], refs[10:]
    gs, ext, state, kqs, vs, keep = scratch

    def weights():
        flow.need(10 + count)
        load_w_in(table, pieces, w_in)
        flow.give(9)

    mixer_prepare(
        lay, heads, span, blocks, flow, me, weights, w_in, (x0, x1, x2, x3, gain, a_in, b_in, cw, rb),
        (h1, z_in, pre, gate_out, small_out, kqs, vs, tri_out), (gs, ext, keep), 10, (0, 1, 2, 3, 4), (8,)
    )
    mixer_advance(heads, span, blocks, me, (gate_out, small_out, kqs, vs, tri_out, rb, hg), (gated, ou_out, s_out), state)


def mixer_first(lay, heads, span, blocks, flow, me, x0, x1, x2, x3, gain, a_in, b_in, cw, rb, w_in,
                h1, z_in, pre, gate_out, small_out, kqs, vs, tri_out, gs, ext, keep):
    mixer_prepare(
        lay, heads, span, blocks, flow, me, partial(flow.need, 10), w_in, (x0, x1, x2, x3, gain, a_in, b_in, cw, rb),
        (h1, z_in, pre, gate_out, small_out, kqs, vs, tri_out), (gs, ext, keep), 9, (0, 1, 2, 3, 4), (5, 6, 7)
    )


def mixer_second(lay, micro, heads, span, blocks, flow, me, kqs, vs, tri, gate_in, small_in, rb, hg, a_out, b_out, w_out,
                 near, single, pair, z_out, gated, ou_out, s_out, state):
    flow.need(7)
    mixer_advance(heads, span, blocks, me, (gate_in, small_in, kqs, vs, tri, rb, hg), (gated, ou_out, s_out), state)
    flow.give(4, 5, 6)
    flow.need(10)
    project_output(lay, micro, gated, a_out, b_out, w_out, near, single, pair, z_out)


def mixer_prepare(lay, heads, span, blocks, flow, me, weights, w_in, ins, outs, scratch, small_ins, early, late):
    x0, x1, x2, x3, gain, a_in, b_in, cw, rb = ins
    h1, z_in, pre, gate_out, small_out, kqs, vs, tri_out = outs
    gs, ext, keep = scratch
    head = 256
    here = me[0]
    own = lay.own
    flow.need(5)
    for k, piece in enumerate((x0, x1, x2, x3)):
        x = piece[...].astype(f32)
        h1[k * span : (k + 1) * span, :] = low(
            x * lax.rsqrt(jnp.mean(x * x, 1, keepdims=True) + epsilon) * gain[...]
        )
    flow.need(small_ins)
    z_in[...] = low(nt(h1[...], a_in[...]))
    weights()
    ext[0:8, :] = jnp.zeros((8, ext.shape[1]), f32)
    for col in range(0, 4 * own + 128, 256):
        wide = min(256, 4 * own + 128 - col)
        value = nn(h1[...], w_in[:, col : col + wide])
        if col < 4 * own:
            value = value + nn(z_in[...], b_in[:, col : col + wide])
        for k in range(blocks):
            part = value[k * span : (k + 1) * span]
            start = pl.multiple_of((k ^ here) * span, span)
            if col < 3 * own:
                part = low(part)
                pre[pl.ds(start, span), col : col + wide] = part
                ext[pl.ds(start + 8, span), col : col + wide] = part.astype(f32)
            else:
                at = col - 3 * own
                if at < own:
                    gate_out[pl.ds(start, span), at : at + wide] = low(part)
                else:
                    small_out[pl.ds(start, span), :] = part
    flow.give(*early)
    grow, gcol = tile_masks(span)
    inclusive = grow >= gcol
    strictly = grow > gcol
    tri = jnp.where(inclusive, 1.0, 0.0).astype(f32)
    scale_k = 0.5**0.5
    scale_q = 128 ** (-0.5) * 0.5**0.5

    def prepare(n, carry):
        start = pl.multiple_of(n * span, span)
        betas, running, _ = gates(small_out, rb, start, span, 0, tri)
        running_t = running.T
        for h in range(heads):
            q = conv_block(ext, cw, start, h * head, span, head)
            k = conv_block(ext, cw, start, (heads + h) * head, span, head)
            v = conv_block(ext, cw, start, (2 * heads + h) * head, span, head)
            q = q * lax.logistic(q)
            k = k * lax.logistic(k)
            vs[h, n] = (v * lax.logistic(v)).astype(vs.dtype)
            q = low(q * (half_rsqrt(q) * scale_q))
            k = low(k * (half_rsqrt(k) * scale_k))
            kqs[h, n, :span] = k
            kqs[h, n, span:] = q
            both = nt(kqs[h, n], k)
            ratio = decay_ratio(running[:, h : h + 1], running_t[h : h + 1, :], inclusive)
            kr = jnp.where(strictly, ratio * both[:span], 0.0)
            tri_out[2, h, n] = low(kr)
            tri_out[1, h, n] = low(both[span:] * ratio)
            keep[1, h * blocks + n] = kr * betas[:, heads + h : heads + h + 1]
        return carry

    lax.fori_loop(0, blocks, prepare, 0)
    pairs = [(h, n) for h in range(heads) for n in range(blocks)]
    unit_lower_inverses(
        [keep.at[1, h * blocks + n] for h, n in pairs],
        [keep.at[2, h * blocks + n] for h, n in pairs],
        [keep.at[0, h * blocks + n] for h, n in pairs],
    )
    for h, n in pairs:
        tri_out[0, h, n] = low(keep[2, h * blocks + n])
    flow.give(*late)


def mixer_advance(heads, span, blocks, me, ins, outs, state):
    gate_in, small_in, kqs, vs, tri_in, rb, hg = ins
    gated, ou_out, s_out = outs
    head = 256
    here = me[0]
    grow, gcol = tile_masks(span)
    tri = jnp.where(grow >= gcol, 1.0, 0.0).astype(f32)
    state[...] = jnp.zeros_like(state)

    def advance(n, carry):
        start = pl.multiple_of(n * span, span)
        row = pl.multiple_of((n ^ here) * span, span)
        betas, running, _ = gates(small_in, rb, start, span, 0, tri)
        for h in range(heads):
            cols = slice(h * head, (h + 1) * head)
            c, b = running[:, h : h + 1], betas[:, heads + h : heads + h + 1]
            d = jnp.exp(c)
            last = c[span - 1 : span, :]
            old = state[h]
            low_old = low(old)
            s_out[h, n] = low_old
            seen = nn(kqs[h, n], low_old)
            u = low(nn(tri_in[0, h, n], low(b * (vs[h, n].astype(f32) - d * seen[:span]))))
            o = d * seen[span:] + nn(tri_in[1, h, n], u)
            ou_out[1, pl.ds(start, span), cols] = u
            ou_out[0, pl.ds(start, span), cols] = low(o)
            weighted = low(kqs[h, n, :span].astype(f32) * jnp.exp(last - c))
            state[h] = jnp.exp(last) * old + tn(weighted, u)
            norm = o * lax.rsqrt(jnp.mean(o * o, 1, keepdims=True) + epsilon) * hg[...]
            gate = gate_in[pl.ds(start, span), cols].astype(f32)
            gated[pl.ds(row, span), cols] = low(norm * (gate * lax.logistic(gate)))
        return carry

    lax.fori_loop(0, blocks, advance, 0)


def project_output(lay, micro, gated, a_out, b_out, w_out, near, single, pair, z_out):
    z_out[...] = low(nt(gated[...], a_out[...]))
    for col in range(0, lay.width, 256):
        value = nn(gated[...], w_out[:, col : col + 256]) + nn(z_out[...], b_out[:, col : col + 256])
        block_out(True, near, single, pair, col, value)


def mixer_output(lay, micro, step, flow, me, gated, a_out, b_out, q0, q1, q2, q3, near, single, pair, z_out, w_out):
    flow.need(7)
    load_w_out(me, step, (q0, q1, q2, q3), w_out)
    flow.give(4)
    project_output(lay, micro, gated, a_out, b_out, w_out, near, single, pair, z_out)


def mixer_backward(lay, micro, heads, span, blocks, windows, flow, me, g0, g1, g2, g3, a_out, b_out, w_out,
                   a_in, b_in, cw, rb, hg, pre, gates_in, small_in, ou_in, s_in, tri_in,
                   z_out, gated, z_in, w_in, h1,
                   ga_gu, g_hidden, gb_down, near, single, pair, send_near, send_single, send_pair,
                   ext, back, dstate, gbranch, dgated, dproj, dsmall, flat):
    head = 256
    here = me[0]
    own = lay.own
    width = lay.width
    flow.need(7)
    rows_of(gbranch, (g0, g1, g2, g3))
    gz_out = low(nt(gbranch[...], b_out[...]))
    for col in range(0, own, 256):
        dgated[:, col : col + 256] = low(
            nt(gbranch[...], w_out[col : col + 256, :]) + nn(gz_out, a_out[:, col : col + 256])
        )
    flow.need(18)
    grow, gcol = tile_masks(span)
    inclusive = grow >= gcol
    strictly = grow > gcol
    tri = jnp.where(inclusive, 1.0, 0.0).astype(f32)
    scale_k = 0.5**0.5
    scale_q = 128 ** (-0.5) * 0.5**0.5
    ext[0:8, :] = jnp.zeros((8, ext.shape[1]), f32)
    ext[8:, :] = pre[...].astype(f32)
    back[...] = jnp.zeros_like(back)
    dstate[...] = jnp.zeros_like(dstate)
    lane = lax.broadcasted_iota(jnp.int32, (span, 128), 1)
    sub = lax.broadcasted_iota(jnp.int32, (span, 128), 0)
    final = lax.broadcasted_iota(jnp.int32, (span, 1), 0) == span - 1

    def step(i, carry):
        n = blocks - 1 - i
        row = pl.multiple_of((n ^ here) * span, span)
        start = pl.multiple_of(n * span, span)
        betas, running, slope = gates(small_in, rb, start, span, 0, tri)
        running_t = running.T
        drunning = jnp.zeros((span, 128), f32)
        by_row = jnp.zeros((span, 128), f32)
        dbetas = jnp.zeros((span, 128), f32)
        for h in range(heads):
            cols = slice(h * head, (h + 1) * head)
            cq = conv_block(ext, cw, start, h * head, span, head)
            ck = conv_block(ext, cw, start, (heads + h) * head, span, head)
            cv = conv_block(ext, cw, start, (2 * heads + h) * head, span, head)
            sq, sk, sv = lax.logistic(cq), lax.logistic(ck), lax.logistic(cv)
            qa, ka, v = cq * sq, ck * sk, cv * sv
            rq, rk = half_rsqrt(qa), half_rsqrt(ka)
            q = qa * (rq * scale_q)
            k = ka * (rk * scale_k)
            kq = jnp.concatenate([low(k), low(q)], 0)
            c = running[:, h : h + 1]
            b = betas[:, heads + h : heads + h + 1]
            d = jnp.exp(c)
            last = c[span - 1 : span, :]
            w = jnp.exp(last - c)
            inv, att = tri_in[0, h, n], tri_in[1, h, n]
            kr = tri_in[2, h, n].astype(f32)
            u = ou_in[1, pl.ds(start, span), cols]
            o = ou_in[0, pl.ds(start, span), cols].astype(f32)
            old = s_in[h, n]
            after = dstate[h]
            gate = gates_in[pl.ds(start, span), cols].astype(f32)
            dy = dgated[pl.ds(row, span), cols].astype(f32)
            sg = lax.logistic(gate)
            r = lax.rsqrt(jnp.mean(o * o, 1, keepdims=True) + epsilon)
            dn = dy * (gate * sg) * hg[...]
            normed = o * r
            dproj[pl.ds(row, span), (3 * heads + h) * head : (3 * heads + h + 1) * head] = low(
                dy * (normed * hg[...]) * (sg * (1.0 + gate * (1.0 - sg)))
            )
            do = r * (dn - normed * jnp.mean(normed * dn, 1, keepdims=True))
            seen = nn(kq, old)
            low_after, low_do = low(after), low(do)
            x = v - d * seen[:span]
            du = tn(att, low_do) + lnn(k * w, low_after)
            datt = jnp.where(inclusive, nt(low_do, u), 0.0)
            dweighted = nt(u, low_after)
            y = ltn(inv, du)
            dlow = jnp.where(strictly, -lnt(y, u), 0.0)
            dx = b * y
            db = jnp.sum(y * x, 1, keepdims=True) + jnp.sum(dlow * kr, 1, keepdims=True)
            dseen = jnp.concatenate([low(-(d * dx)), low(d * do)], 0)
            dstate[h] = jnp.exp(last) * after + tn(kq, dseen)
            dkq = nt(dseen, old)
            dd = jnp.sum(do * seen[span:] - dx * seen[:span], 1, keepdims=True)
            ratio = decay_ratio(c, running_t[h : h + 1, :], inclusive)
            dboth = jnp.concatenate([low(dlow * b * ratio), low(datt * ratio)], 0)
            dkq = dkq + nn(dboth, kq[:span])
            dk = dkq[:span] + tn(dboth, kq) + dweighted * w
            dq = dkq[span:]
            grown = dlow * (b * kr) + datt * att
            dw = jnp.sum(dweighted * k, 1, keepdims=True) * w
            dlast = jnp.exp(last) * jnp.sum(
                jnp.sum(after * old.astype(f32), 1, keepdims=True), 0, keepdims=True
            ) + jnp.sum(dw, 0, keepdims=True)
            dc = jnp.sum(grown, 1, keepdims=True) - dw + dd * d + jnp.where(final, dlast, 0.0)
            drunning = drunning + jnp.where(lane == h, dc, 0.0)
            by_row = by_row + jnp.where(sub == h, jnp.sum(grown, 0, keepdims=True), 0.0)
            dbetas = dbetas + jnp.where(lane == heads + h, db, 0.0)
            dqa = rq * scale_q * dq - qa * (rq * rq * rq * scale_q) * half_sum(qa * dq)
            dka = rk * scale_k * dk - ka * (rk * rk * rk * scale_k) * half_sum(ka * dk)
            for part, grad, sig, act in ((0, dqa, sq, cq), (1, dka, sk, ck), (2, dx, sv, cv)):
                col = (part * heads + h) * head
                through = grad * (sig * (1.0 + act * (1.0 - sig)))
                window = jnp.concatenate([through, back[:, col : col + head]], 0)
                back[:, col : col + head] = through[:8]
                out = None
                for j in range(4):
                    term = shifted_rows(window, span, 3 - j) * cw[j : j + 1, col : col + head]
                    out = term if out is None else out + term
                dproj[pl.ds(row, span), col : col + head] = low(out)
        dlog = tn(tri, drunning - by_row.T, high)
        dsmall[pl.ds(row, span), :] = low(
            -rb[0:1, :] * slope * dlog + dbetas * betas * (1.0 - betas)
        )
        return carry

    lax.fori_loop(0, blocks, step, 0)
    flow.need(26)
    gz_in = low(nt(dproj[...], b_in[...]))
    for col in range(0, width, 256):
        value = (
            nt(dproj[...], w_in[col : col + 256, : 4 * own])
            + nt(dsmall[...], w_in[col : col + 256, 4 * own :])
            + nn(gz_in, a_in[:, col : col + 256])
        )
        block_out(micro == 0, near, single, pair, col, value)
    flow.give(0, 1, 2)
    ga_out = tn(gz_out, gated[...])
    gb_out = tn(z_out[...], gbranch[...])
    flat[...] = jnp.zeros_like(flat)
    ga_in = low(tn(gz_in, h1[...]))
    for p in range(4):
        flat[:, lay.a_in + p * width : lay.a_in + (p + 1) * width] = ga_in[p * RANK : (p + 1) * RANK]
        gb = tn(z_in[...], dproj[:, p * own : (p + 1) * own])
        flat[:, pl.ds(pl.multiple_of(lay.b_in + p * lay.value_width + here * own, 128), own)] = low(
            gb[p * RANK : (p + 1) * RANK]
        )
    flat[:, pl.ds(pl.multiple_of(lay.a_out + here * own, 128), own)] = low(ga_out)
    flat[:, lay.b_out : lay.b_out + width] = low(gb_out)
    for i in range(2):
        flat[:, lay.a_gu + i * width : lay.a_gu + (i + 1) * width] = ga_gu[i * RANK : (i + 1) * RANK, :]
    hidden = lay.hidden
    flat[:, lay.a_down : lay.a_down + hidden] = g_hidden[:RANK, :]
    for i in range(2):
        flat[:, lay.b_gu + i * hidden : lay.b_gu + (i + 1) * hidden] = g_hidden[(i + 1) * RANK : (i + 2) * RANK, :]
    flat[:, lay.b_down : lay.b_down + width] = gb_down[...]
    quarter = send_near.shape[2]
    one, two = block_order(micro == 0)
    sends = {0: send_near, one: send_single, two[0]: send_pair.at[0], two[1]: send_pair.at[1]}
    for k, send in sends.items():
        for f, window in enumerate(windows):
            at = pl.multiple_of(window + (here ^ k) * quarter, 128)
            send[f] = flat[:, pl.ds(at, quarter)]


def feed_forward_blocks(lay, micro, count, flow, table, *refs):
    ins, pieces, rest = refs[:6], refs[6 : 6 + count], refs[6 + count :]
    outs, w_gu, scratch = rest[6:15], rest[15], rest[16:]

    def weights():
        flow.need(6 + count)
        load_w_in(table, pieces, w_gu)
        flow.give(9)

    feed_forward(lay, micro, flow, weights, 12 + count, w_gu, ins, rest[:6], outs, scratch)


def feed_forward_whole(lay, micro, flow, *refs):
    ins, w_gu, rest = refs[:6], refs[6], refs[7:]
    feed_forward(lay, micro, flow, partial(flow.need, 7), 13, w_gu, ins, rest[:6], rest[6:15], rest[15:])


def feed_forward(lay, micro, flow, weights, last_ins, w_gu, ins, more_ins, outs, scratch):
    h0, h1, h2, h3, a_gu, hidden = ins
    g0, g1, g2, g3, b_down, w_down = more_ins
    near, single, pair, gnear, gsingle, gpair, ga_gu, g_own, gb_down = outs
    hs, gs, b_gate, b_up, act, ggate, gup, gates, ups = scratch
    width = lay.width
    wide = act.shape[1]
    flow.need(6)
    rows_of(hs, (h0, h1, h2, h3))
    at = [(3 * micro + i) * RANK for i in range(3)]
    a_down = hidden[at[0] : at[0] + RANK, :]
    b_gate[...] = jnp.zeros_like(b_gate)
    b_up[...] = jnp.zeros_like(b_up)
    b_gate[:RANK, :] = hidden[at[1] : at[1] + RANK, :]
    b_up[RANK:, :] = hidden[at[2] : at[2] + RANK, :]
    z_gu = low(nt(hs[...], a_gu[...]))
    weights()
    for col in range(0, wide, 256):
        cols = slice(col, col + 256)
        gates[:, cols] = nn(hs[...], w_gu[:, cols]) + nn(z_gu, b_gate[:, cols])
        ups[:, cols] = nn(hs[...], w_gu[:, wide + col : wide + col + 256]) + nn(z_gu, b_up[:, cols])
    flow.need(last_ins)
    rows_of(gs, (g0, g1, g2, g3))
    gz_down = low(nt(gs[...], b_down[...]))
    for col in range(0, wide, 256):
        cols = slice(col, col + 256)
        ga, ua = gates[:, cols], ups[:, cols]
        sig = lax.logistic(ga)
        silu = ga * sig
        act[:, cols] = low(silu * ua)
        da = low(nt(gs[...], w_down[cols, :]) + nn(gz_down, a_down[:, cols])).astype(f32)
        ggate[:, cols] = low(da * ua * (sig * (1.0 + ga * (1.0 - sig))))
        gup[:, cols] = low(da * silu)
    gz_gu = low(nt(ggate[...], b_gate[...]) + nt(gup[...], b_up[...]))
    for col in range(0, width, 256):
        cols = slice(col, col + 256)
        value = (
            nt(ggate[...], w_gu[cols, :wide]) + nt(gup[...], w_gu[cols, wide:]) + nn(gz_gu, a_gu[:, cols])
        )
        block_out(micro == 0, gnear, gsingle, gpair, col, value)
    flow.give(3, 4, 5)
    z_down = low(nt(act[...], a_down))
    for col in range(0, width, 256):
        cols = slice(col, col + 256)
        value = nn(act[...], w_down[:, cols]) + nn(z_down, b_down[:, cols])
        block_out(micro == 0, near, single, pair, col, value)
    ga_gu[...] = low(tn(gz_gu, hs[...]))
    gb_down[...] = low(tn(z_down, gs[...]))
    g_own[:RANK, :] = low(tn(gz_down, act[...]))
    g_own[RANK : 2 * RANK, :] = low(tn(z_gu, ggate[...])[:RANK])
    g_own[2 * RANK :, :] = low(tn(z_gu, gup[...])[RANK:])


def adapter_rows(lay, micro_count, windows, flow, me, c0, c1, c2, c3, *refs):
    here = me[0]
    outs, used, flat = refs[:-2], refs[-2], refs[-1]
    width, own, hidden = lay.width, lay.own, lay.hidden
    flat[...] = jnp.zeros_like(flat)
    flow.need(4)
    quarter = c0.shape[2]
    for k, piece in enumerate((c0, c1, c2, c3)):
        for f, window in enumerate(windows):
            cols = pl.ds(pl.multiple_of(window + (here ^ k) * quarter, 128), quarter)
            flat[:, cols] = flat[:, cols] + piece[f]

    def own_columns(rows, at):
        return flat[rows, pl.ds(pl.multiple_of(at + here * own, 128), own)]

    for m in range(micro_count):
        rows = slice(m * RANK, (m + 1) * RANK)
        a_in, b_in, a_gu, a_out, b_out, b_down = outs[6 * m : 6 * (m + 1)]
        b_in[...] = jnp.zeros_like(b_in)
        for p in range(4):
            part = slice(p * RANK, (p + 1) * RANK)
            a_in[part, :] = flat[rows, lay.a_in + p * width : lay.a_in + (p + 1) * width]
            b_in[part, p * own : (p + 1) * own] = own_columns(rows, lay.b_in + p * lay.value_width)
        for i in range(2):
            a_gu[i * RANK : (i + 1) * RANK, :] = flat[rows, lay.a_gu + i * width : lay.a_gu + (i + 1) * width]
        a_out[...] = own_columns(rows, lay.a_out)
        b_out[...] = flat[rows, lay.b_out : lay.b_out + width]
        b_down[...] = flat[rows, lay.b_down : lay.b_down + width]
        for i, at in enumerate((lay.a_down, lay.b_gu, lay.b_gu + hidden)):
            used[(3 * m + i) * RANK : (3 * m + i + 1) * RANK, :] = flat[rows, at : at + hidden]


SMEM = pl.BlockSpec(memory_space=pltpu.SMEM)
VMEM = pl.BlockSpec(memory_space=pltpu.VMEM)


class Flow:
    def __init__(self, stages, far_in, near_in, far_out, near_out, sems):
        self.coming = [
            pltpu.make_async_copy(far, near, sems.at[i]) for i, (far, near) in enumerate(zip(far_in, near_in))
        ]
        at = len(self.coming)
        self.going = [
            pltpu.make_async_copy(near, far, sems.at[at + i]) for i, (far, near) in enumerate(zip(far_out, near_out))
        ]
        self.sent, self.stages = set(), list(stages) + [len(self.coming)]
        self.started = self.ready = 0
        self.start()

    def start(self):
        if self.stages:
            upto = self.stages.pop(0)
            for copy in self.coming[self.started : upto]:
                copy.start()
            self.started = upto

    def need(self, upto):
        while self.ready < upto:
            if self.ready == self.started:
                self.start()
            self.coming[self.ready].wait()
            self.ready += 1
            if self.ready == self.started:
                self.start()

    def give(self, *which):
        for i in which:
            if i not in self.sent:
                self.sent.add(i)
                self.going[i].start()

    def close(self):
        self.need(len(self.coming))
        self.give(*range(len(self.going)))
        for copy in self.going:
            copy.wait()


def flowing(body, stages, scalars, arrays, results, *refs):
    smem, refs = refs[:scalars], refs[scalars:]
    far_in, refs = refs[:arrays], refs[arrays:]
    far_out, refs = refs[:results], refs[results:]
    near_in, refs = refs[:arrays], refs[arrays:]
    near_out, refs = refs[:results], refs[results:]
    sems, scratch = refs[0], refs[1:]
    flow = Flow(stages, far_in, near_in, far_out, near_out, sems)
    body(flow, *smem, *near_in, *near_out, *scratch)
    flow.close()


def kernel_call(body, name, out_shape, scratch, args, scalars=1, flops=0, stages=()):
    size = sum(a.size * a.dtype.itemsize for a in args) + sum(o.size * o.dtype.itemsize for o in out_shape)
    arrays = args[scalars:]
    far = pl.BlockSpec(memory_space=pl.ANY)
    buffers = [pltpu.VMEM(a.shape, a.dtype) for a in (*arrays, *out_shape)]
    return pl.pallas_call(
        partial(flowing, body, stages, scalars, len(arrays), len(out_shape)),
        out_shape=tuple(out_shape),
        in_specs=[SMEM] * scalars + [far] * len(arrays),
        out_specs=tuple([far] * len(out_shape)),
        scratch_shapes=[*buffers, pltpu.SemaphoreType.DMA((len(buffers),)), *scratch],
        compiler_params=pltpu.CompilerParams(vmem_limit_bytes=VMEM_LIMIT),
        cost_estimate=pl.CostEstimate(flops=flops, bytes_accessed=int(size), transcendentals=0),
        name=name,
    )(*args)


class Kernels:
    def __init__(self, lay, heads, head, span, blocks, width, own, wide, windows, quarter, flat, ranks, step):
        shape = jax.ShapeDtypeStruct
        rows = blocks * span
        self.lay, self.sizes = lay, (heads, span, blocks)
        self.windows, self.step = windows, step
        self.blocks = [shape((span, width), f32), shape((span, width), bf16), shape((2, span, width), bf16)]
        send = (ranks, RANK, quarter)
        self.sends = [shape(send, bf16), shape(send, bf16), shape((2, *send), bf16)]
        self.z_out = shape((rows, RANK), bf16)
        self.saved = [
            shape((rows, width), bf16),
            shape((rows, 4 * RANK), bf16),
            shape((rows, 3 * own), bf16),
            shape((rows, own), bf16),
            shape((rows, 128), f32),
            shape((rows, own), bf16),
            shape((2, rows, own), bf16),
            shape((heads, blocks, head, head), bf16),
            shape((3, heads, blocks, span, span), bf16),
        ]
        self.small = [shape((2 * RANK, width), bf16), shape((3 * RANK, wide), bf16), shape((RANK, width), bf16)]
        self.w_gu = shape((width, 2 * wide), bf16)
        self.w_in, self.w_out = shape((width, 4 * own + 128), bf16), shape((own, width), bf16)
        ext = pltpu.VMEM((rows + 8, 3 * own), f32)
        state = pltpu.VMEM((heads, head, head), f32)
        self.kq = shape((heads, blocks, 2 * span, head), bf16)
        self.v = shape((heads, blocks, span, head), bf16)
        keep = pltpu.VMEM((3, heads * blocks, span, span), f32)
        self.state = state
        self.first_scratch = [pltpu.VMEM((8, 128), f32), ext, keep]
        self.forward_scratch = [
            pltpu.VMEM((8, 128), f32),
            ext,
            state,
            pltpu.VMEM(self.kq.shape, bf16),
            pltpu.VMEM(self.v.shape, f32),
            keep,
        ]
        self.feed_scratch = (
            [pltpu.VMEM((rows, width), bf16)] * 2
            + [pltpu.VMEM((2 * RANK, wide), bf16)] * 2
            + [pltpu.VMEM((rows, wide), bf16)] * 3
            + [pltpu.VMEM((rows, wide), f32)] * 2
        )
        self.backward_scratch = [
            ext,
            pltpu.VMEM((8, 3 * own), f32),
            state,
            pltpu.VMEM((rows, width), bf16),
            pltpu.VMEM((rows, own), bf16),
            pltpu.VMEM((rows, 4 * own), bf16),
            pltpu.VMEM((rows, 128), bf16),
            pltpu.VMEM((RANK, flat), bf16),
        ]

    def forward(self, m, me, table, w_in, x, gain, adapters, cw, rb, hg):
        outs = kernel_call(
            partial(mixer_forward, self.lay, *self.sizes, len(w_in)),
            "mixer_forward",
            self.saved + [self.w_in],
            self.forward_scratch,
            (me, table, *x, gain, *adapters, cw, rb, hg, *w_in),
            scalars=2,
            stages=(5,),
            flops=6_000_000_000,
        )
        return outs[:-1], outs[-1]

    def first(self, m, me, w_in, x, gain, adapters, cw, rb):
        return kernel_call(
            partial(mixer_first, self.lay, *self.sizes),
            "mixer_first",
            self.saved[:5] + [self.kq, self.v, self.saved[8]],
            self.first_scratch,
            (me, *x, gain, *adapters, cw, rb, w_in),
            stages=(5,),
            flops=5_000_000_000,
        )

    def second(self, m, me, w_out, done, adapters, rb, hg):
        h1, z_in, pre, gate, small, kq, v, tri = done
        outs = kernel_call(
            partial(mixer_second, self.lay, m, *self.sizes),
            "mixer_second",
            self.blocks + [self.z_out] + self.saved[5:8],
            [self.state],
            (me, kq, v, tri, gate, small, rb, hg, *adapters, w_out),
            flops=3_000_000_000,
        )
        return outs[:3], outs[3], (h1, z_in, pre, gate, small, *outs[4:], tri)

    def output(self, m, me, w_out, gated, adapters):
        outs = kernel_call(
            partial(mixer_output, self.lay, m, self.step),
            "mixer_output",
            self.blocks + [self.z_out, self.w_out],
            [],
            (me, gated, *adapters, *w_out),
            flops=1_000_000_000,
        )
        return outs[:3], outs[3], outs[4]

    def feed(self, m, table, h2, cot, w_gu, w_down, a_gu, b_down, hidden):
        whole = len(w_gu) == 1
        outs = kernel_call(
            partial(feed_forward_whole, self.lay, m) if whole else partial(feed_forward_blocks, self.lay, m, len(w_gu)),
            "feed_forward",
            self.blocks * 2 + self.small + ([] if whole else [self.w_gu]),
            self.feed_scratch,
            (*([] if whole else [table]), *h2, a_gu, hidden, *w_gu, *cot, b_down, w_down),
            scalars=0 if whole else 1,
            stages=(6, 6 + len(w_gu)),
            flops=5_000_000_000,
        )
        return outs[:3], outs[3:6], outs[6:9], w_gu[0] if whole else outs[9]

    def backward(self, m, me, w_in, w_out, g_branch, in_adapters, out_adapters, cw, rb, hg, z_out, saved, small):
        h1, z_in, pre, gates_in, small_in, gated, ou_in, s_in, tri_in = saved
        outs = kernel_call(
            partial(mixer_backward, self.lay, m, *self.sizes, self.windows),
            "mixer_backward",
            self.blocks + self.sends,
            self.backward_scratch,
            (
                me,
                *g_branch,
                *out_adapters,
                w_out,
                *in_adapters,
                cw,
                rb,
                hg,
                pre,
                gates_in,
                small_in,
                ou_in,
                s_in,
                tri_in,
                z_out,
                gated,
                z_in,
                w_in,
                h1,
                *small,
            ),
            stages=(7, 18),
            flops=9_000_000_000,
        )
        return outs[:3], outs[3:]


def rms_norm(inputs, scales):
    return inputs * lax.rsqrt(jnp.mean(inputs * inputs, -1, keepdims=True) + epsilon) * scales


def own_lanes(value, start, size):
    return lax.dynamic_slice_in_dim(value, start, size, axis=value.ndim - 1)


def shards(
    tokens,
    cotangent,
    lengths,
    adapter_index,
    step_count,
    w_in,
    w_out,
    w_gu,
    w_down,
    conv_weight,
    norm_gains,
    head_gain,
    decay_rate,
    decay_bias,
    adapters,
    first_moment,
    second_moment,
):
    micro_count, _, span, width = tokens.shape
    ranks = lax.axis_size("fsdp")
    parts = lax.axis_size("seq")
    here = lax.axis_index("seq")
    place = lax.axis_index("fsdp")
    all_heads = decay_rate.shape[0]
    heads = all_heads // parts
    value_width = conv_weight.shape[1] // 3
    own = value_width // parts
    hidden = w_gu.shape[1] // 2
    piece = w_down.shape[0] // parts
    wide = -(-hidden // parts // 256) * 256
    padded = wide // ranks
    columns = adapters.shape[1]
    shard_rows = adapters.shape[0]
    rows = parts * span
    me = here.astype(jnp.int32).reshape(1)
    lay = Layout(width, value_width, hidden, parts)
    shape = jax.ShapeDtypeStruct

    bits = [1 << i for i in range(ranks.bit_length() - 1)]
    picks = lax.dynamic_update_slice(
        jnp.zeros((ranks, 128), jnp.int32), jnp.pad(adapter_index.T, ((0, 0), (0, 128 - micro_count))), (place, 0)
    )
    picks = butterfly(picks, "fsdp", bits[:1])

    def heads_slice(part):
        return own_lanes(w_in, part * value_width + here * own, own)

    small = jnp.concatenate(
        [
            own_lanes(w_in, 4 * value_width + here * heads, heads),
            own_lanes(w_in, 4 * value_width + all_heads + here * heads, heads),
            jnp.zeros((w_in.shape[0], 128 - 2 * heads), bf16),
        ],
        1,
    )
    in_rows = w_in.shape[0]
    local_out = own_lanes(w_out, here * (width // parts), width // parts)
    local_in = jnp.concatenate(
        [local_out[:in_rows], local_out[in_rows:]] + [heads_slice(p) for p in range(4)] + [small], 1
    )
    ring = RingGather(local_in)

    window = -(-(shard_rows + 127) // (128 * parts)) * 128 * parts
    quarter = window // parts
    windows = [shard_rows * f // 128 * 128 for f in range(ranks)]
    flat_width = windows[-1] + window
    offset = (shard_rows * place) % 128
    framed = lax.dynamic_update_slice(
        jnp.zeros((window, columns), bf16), adapters.astype(bf16), (offset, 0)
    )
    framed = lax.dynamic_slice_in_dim(framed, here * quarter, quarter, 0)
    conv_own = jnp.concatenate(
        [own_lanes(conv_weight, p * value_width + here * own, own) for p in range(3)], 1
    )
    rate_bias = jnp.zeros((8, 128), f32)
    rate_bias = rate_bias.at[0, :heads].set(lax.dynamic_slice(decay_rate, (here * heads,), (heads,)))
    rate_bias = rate_bias.at[1, :heads].set(lax.dynamic_slice(decay_bias, (here * heads,), (heads,)))
    gain_row = head_gain.reshape(1, -1)

    far_tokens = [gather_far(tokens[m, 0]) for m in range(micro_count)]
    positions = here * span + jnp.arange(span)
    cots = [
        cotangent[m, 0].astype(f32) * (positions < lengths[m, 0]).astype(f32)[:, None]
        for m in range(micro_count)
    ]
    picks = butterfly(picks, "fsdp", bits[1:])
    wanted = (picks[:, :micro_count, None] * RANK + jnp.arange(RANK)[None, None, :]).reshape(-1)
    select = (wanted[:, None] == jnp.arange(columns)[None, :]).astype(bf16)
    chosen = nt(select, framed).astype(bf16).reshape(ranks, micro_count * RANK, quarter)
    chosen, conv_own, rate_bias, table, select = ring.advance(chosen, conv_own, rate_bias, ring.table, select)
    chosen = lax.all_to_all(chosen, "fsdp", 0, 0)

    unit = after(jnp.arange(wide), ring.right)
    unit_of = (unit // padded) * w_down.shape[0] + here * piece + unit % padded
    unit_of = jnp.where(unit % padded < piece, unit_of, -1)
    spread = (jnp.arange(hidden)[:, None] == unit_of[None, :]).astype(bf16)
    local_gu = jnp.concatenate(
        [nn(w_gu[:, i * hidden : (i + 1) * hidden], spread).astype(bf16) for i in range(2)], 1
    )
    local_down = jnp.pad(
        lax.dynamic_slice_in_dim(w_down, here * piece, piece, 0), ((0, padded - piece), (0, 0))
    )
    pieces = [gather_near(*far) for far in far_tokens]
    far_cots = [gather_far(low(cot)) for cot in cots]
    (far_tokens,) = ring.advance(far_tokens)

    chosen, local_gu, pieces, far_cots = ring.advance(chosen, local_gu, pieces, far_cots)
    cot_pieces = [gather_near(*far) for far in far_cots]
    chosen, beyond = ring.advance(*gather_far(chosen))
    chosen = gather_near(chosen, beyond)
    while not ring.done():
        ring.advance()
    quarter_width = 2 * (width // parts)
    out_sorted = pl.pallas_call(
        partial(split_out, min(block.shape[0] for block in ring.blocks)),
        grid=(1,),
        out_shape=[shape((width // parts, quarter_width), bf16)] * parts,
        in_specs=[SMEM, SMEM]
        + [pl.BlockSpec((block.shape[0], quarter_width), lambda i: (0, 0)) for block in ring.blocks],
        out_specs=[pl.BlockSpec((width // parts, quarter_width), lambda i: (0, 0))] * parts,
        name="split_out",
    )(me, table, *ring.blocks)
    out_quarters = [swapped(out_sorted[k], k) if k else out_sorted[k] for k in range(parts)]
    per_micro = [
        shape((4 * RANK, width), bf16),
        shape((4 * RANK, 4 * own), bf16),
        shape((2 * RANK, width), bf16),
        shape((RANK, own), bf16),
        shape((RANK, width), bf16),
        shape((RANK, width), bf16),
    ]
    *adapted, used = kernel_call(
        partial(adapter_rows, lay, micro_count, windows),
        "adapter_rows",
        per_micro * micro_count + [shape((3 * micro_count * RANK, hidden), bf16)],
        [pltpu.VMEM((micro_count * RANK, flat_width), bf16)],
        (me, *chosen),
    )
    adapted = [adapted[6 * m : 6 * (m + 1)] for m in range(micro_count)]
    hidden_own = nn(used, spread).astype(bf16)
    second_ring = RingGather(after(local_gu, ring.right))
    full_down = lax.all_gather(after(local_down, ring.right), "fsdp", axis=0, tiled=True)

    first_gain = norm_gains[0].reshape(1, -1)
    micros = range(micro_count)
    inputs = [tokens[m, 0].astype(f32) for m in micros]
    kernels = Kernels(
        lay, heads, head_gain.shape[0], span, parts, width, own, wide, windows, quarter, flat_width, ranks, in_rows
    )

    def feed(m, h2, cot, w_gu):
        return kernels.feed(m, table, h2, cot, w_gu, full_down, adapted[m][2], adapted[m][5], hidden_own)

    def backward(m, g_branch, z_out, saved, small_grads):
        return kernels.backward(
            m,
            me,
            full_in,
            full_out,
            g_branch,
            adapted[m][:2],
            adapted[m][3:5],
            conv_own,
            rate_bias,
            gain_row,
            z_out,
            saved,
            small_grads,
        )

    def second_norm(middle):
        h2, pull = jax.vjp(partial(rms_norm, scales=norm_gains[1]), middle)
        return low(h2), pull

    def input_gradient(m, g_middle, g_h1):
        pull = jax.vjp(partial(rms_norm, scales=norm_gains[0]), inputs[m])[1]
        return low(g_middle + pull(low(g_h1).astype(f32))[0])

    saved0, full_in = kernels.forward(
        0, me, table, ring.blocks, pieces[0], first_gain, adapted[0][:2], conv_own, rate_bias, gain_row
    )
    (saved0,) = second_ring.advance(saved0)
    out0, z_out0, full_out = kernels.output(0, me, out_quarters, saved0[5], adapted[0][3:5])
    got0 = scatter_far(out0[2])
    begun1 = kernels.first(1, me, full_in, pieces[1], first_gain, adapted[1][:2], conv_own, rate_bias)
    got0, begun1 = second_ring.advance(got0, begun1)
    middle0 = inputs[0] + scatter_near(out0[0], out0[1], got0)
    h20, pull0 = second_norm(middle0)
    far0 = gather_far(h20)
    begun1 = held(begun1, h20)
    out1, z_out1, saved1 = kernels.second(1, me, full_out, begun1, adapted[1][3:5], rate_bias, gain_row)
    far0, out1 = second_ring.advance(far0, out1)
    (h20,) = second_ring.advance(gather_near(*far0))
    while not second_ring.done():
        second_ring.advance()
    got1 = scatter_far(out1[2])
    last0, g_out0, grads0, full_gu = feed(0, h20, cot_pieces[0], second_ring.blocks)
    got1, last0, g_out0, grads0 = held((got1, last0, g_out0, grads0))
    middle1 = inputs[1] + scatter_near(out1[0], out1[1], got1)
    h21, pull1 = second_norm(middle1)
    h21 = gather_seq(h21)
    g_out0, h21 = held((g_out0, h21))
    g_got0 = scatter_far(g_out0[2])
    last1, g_out1, grads1, full_gu = feed(1, h21, cot_pieces[1], [full_gu])
    g_got0, last1, g_out1, grads1 = held((g_got0, last1, g_out1, grads1))
    g_h20 = scatter_near(g_out0[0], g_out0[1], g_got0)
    g_middle0 = cots[0] + pull0(low(g_h20).astype(f32))[0]
    branch0 = gather_far(low(g_middle0))
    hidden0, hidden1 = [nt(g[1], spread).astype(bf16) for g in (grads0, grads1)]
    branch0, hidden0, hidden1 = held((branch0, hidden0, hidden1))
    branch0 = gather_near(*branch0)
    g_h21 = after(scatter_seq(*g_out1), branch0[2])
    g_middle1 = cots[1] + pull1(low(g_h21).astype(f32))[0]
    branch0, g_middle1, last0 = held((branch0, g_middle1, last0))
    far1 = gather_far(low(g_middle1))
    last_got0 = scatter_far(last0[2])
    g_in0, sums0 = backward(0, branch0, z_out0, saved0, (grads0[0], hidden0, grads0[2]))
    far1, last_got0, last1, g_in0, sums0 = held((far1, last_got0, last1, g_in0, sums0))
    branch1 = gather_near(*far1)
    mixed0 = low(middle0 + scatter_near(last0[0], last0[1], last_got0))
    sums_got0 = scatter_far(sums0[2])
    g_in_got0 = scatter_far(g_in0[2])
    g_in1, sums1 = backward(1, branch1, z_out1, saved1, (grads1[0], hidden1, grads1[2]))
    sums_got0, g_in_got0, g_in1, sums1 = held((sums_got0, g_in_got0, g_in1, sums1))
    total1 = low(scatter_seq(sums1[0].astype(f32), *sums1[1:]))
    total0 = low(scatter_near(sums0[0].astype(f32), sums0[1], sums_got0))
    total = jnp.concatenate([total0, total1], 1)
    total, g_in1, last1 = held((total, g_in1, last1))
    arrived = lax.all_to_all(total, "fsdp", 0, 0)
    arrived, g_in_got0 = held((arrived, g_in_got0))
    mixed1 = low(middle1 + scatter_seq(*last1))
    grad_tokens0 = input_gradient(0, g_middle0, scatter_near(g_in0[0], g_in0[1], g_in_got0))
    grad_tokens1 = input_gradient(1, g_middle1, scatter_seq(*g_in1))
    mine = tn(arrived.reshape(-1, quarter), select)
    at = here * quarter + jnp.arange(quarter)
    mine = jnp.where(((at >= offset) & (at < offset + shard_rows))[:, None], mine, 0.0)
    squares = jnp.full((8, 128), jnp.sum(mine * mine))
    shard_grad = jnp.concatenate(in_seq_order(gather_seq(low(mine))), 0)
    shard_grad = lax.optimization_barrier(shard_grad)
    squares = total_over(total_over(squares, "seq"), "fsdp")[0, 0]
    shard_grad = lax.dynamic_slice_in_dim(shard_grad, offset, shard_rows, 0).astype(f32)
    norm_value = jnp.sqrt(squares)
    clipped = shard_grad * (CLIP_LIMIT / jnp.maximum(norm_value, CLIP_LIMIT))
    new_first = FIRST_DECAY * first_moment + (1.0 - FIRST_DECAY) * clipped
    new_second = SECOND_DECAY * second_moment + (1.0 - SECOND_DECAY) * clipped * clipped
    counter = step_count[0].astype(f32)
    corrected_first = new_first / (1.0 - jnp.power(FIRST_DECAY, counter))
    corrected_second = new_second / (1.0 - jnp.power(SECOND_DECAY, counter))
    update = -LEARN_RATE * (
        corrected_first / (jnp.sqrt(corrected_second) + ADAM_EPSILON) + WEIGHT_DECAY * adapters
    )
    return (
        jnp.stack([mixed0, mixed1], 0)[:, None],
        jnp.stack([grad_tokens0, grad_tokens1], 0)[:, None],
        update,
        new_first,
        new_second,
        norm_value.reshape(1),
    )


def solution(mesh):
    in_specs = (
        P(None, "fsdp", "seq", None),
        P(None, "fsdp", "seq", None),
        P(None, "fsdp"),
        P(None, "fsdp"),
        P(),
        P("fsdp", None),
        P("fsdp", None),
        P("fsdp", None),
        P("fsdp", None),
        P(),
        P(),
        P(),
        P(),
        P(),
        P("fsdp", None),
        P("fsdp", None),
        P("fsdp", None),
    )
    out_specs = (
        P(None, "fsdp", "seq", None),
        P(None, "fsdp", "seq", None),
        P("fsdp", None),
        P("fsdp", None),
        P("fsdp", None),
        P(),
    )
    return jax.shard_map(shards, mesh=mesh, in_specs=in_specs, out_specs=out_specs, check_vma=False)
```

```python
from functools import partial

import jax
import jax.numpy as jnp
from jax import lax
from jax.experimental import pallas as pl
from jax.experimental.pallas import tpu as pltpu
from jax.sharding import PartitionSpec as P

RANK = 16
epsilon = 1e-06
CLIP_LIMIT = 1.0
LEARN_RATE = 0.01
FIRST_DECAY = 0.9
SECOND_DECAY = 0.999
ADAM_EPSILON = 1e-08
WEIGHT_DECAY = 0.1
VMEM_LIMIT = 56 << 20

f32 = jnp.float32
bf16 = jnp.bfloat16
high = lax.Precision.HIGH


def nn(a, b, precision=None):
    return lax.dot_general(
        a, b, (((1,), (0,)), ((), ())), precision=precision, preferred_element_type=f32
    )


def nt(a, b, precision=None):
    return lax.dot_general(
        a, b, (((1,), (1,)), ((), ())), precision=precision, preferred_element_type=f32
    )


def tn(a, b, precision=None):
    return lax.dot_general(
        a, b, (((0,), (0,)), ((), ())), precision=precision, preferred_element_type=f32
    )


def swapped(value, bit):
    count = lax.axis_size("seq")
    return lax.ppermute(value, "seq", [(i, i ^ bit) for i in range(count)])


def gather_far(value):
    return value, swapped(value, 2)


def gather_near(value, beyond):
    return value, swapped(value, 1), beyond, swapped(beyond, 1)


def gather_seq(value):
    return gather_near(*gather_far(value))


def in_seq_order(blocks):
    here = lax.axis_index("seq")
    for bit in (1, 2):
        flip = here & bit != 0
        blocks = [jnp.where(flip, blocks[k ^ bit], blocks[k]) for k in range(4)]
    return blocks


def scatter_far(far):
    return swapped(far, 2)


def scatter_near(near, beside, got):
    got = got.astype(f32)
    return near + got[0] + swapped((beside.astype(f32) + got[1]).astype(bf16), 1).astype(f32)


def scatter_seq(near, beyond, pair):
    got = swapped(pair, 1).astype(f32)
    return near + got[0] + swapped((beyond.astype(f32) + got[1]).astype(bf16), 2).astype(f32)


def held(values, *others):
    return lax.optimization_barrier((tuple(values), *others))[0]


def ring_order(count):
    return list(range(0, count, 2)) + list(range(count - 1, 0, -2))


def after(value, *others):
    return lax.optimization_barrier((value, *others))[0]


class RingGather:
    def __init__(self, value):
        count, here = lax.axis_size("fsdp"), lax.axis_index("fsdp")
        order = ring_order(count)
        place = [order.index(d) for d in range(count)]
        rows = value.shape[0]
        halves = rows // 2 % 16 == 0
        table = []
        for d in range(count):
            source = [order[(place[d] - k) % count] * rows for k in range(count)]
            at = [source[0]]
            for hop in range(1, count // 2 + 1):
                last = 2 * hop == count
                at.append(source[hop])
                if not last:
                    at.append(source[count - hop])
                elif halves:
                    at.append(source[hop] + rows // 2)
            table.append(at)
        self.count, self.hop, self.rows, self.halves = count, 0, rows, halves
        self.table = jnp.asarray(table, jnp.int32)[here]
        self.ahead = [(order[i], order[(i + 1) % count]) for i in range(count)]
        self.behind = [(b, a) for a, b in self.ahead]
        self.right = self.left = value
        self.blocks = [value]

    def advance(self, *others):
        self.hop += 1
        right, left = self.right, self.left
        half = self.rows // 2
        last = 2 * self.hop == self.count
        if last and self.halves:
            right, left = right[:half], left[half:]
        right = lax.ppermute(right, "fsdp", self.ahead)
        if not last or self.halves:
            left = lax.ppermute(left, "fsdp", self.behind)
        self.right, self.left, *others = lax.optimization_barrier((right, left, *others))
        self.blocks.append(self.right)
        if not last or self.halves:
            self.blocks.append(self.left)
        return others

    def done(self):
        return 2 * self.hop >= self.count


def butterfly(value, axis, bits=None):
    count = lax.axis_size(axis)
    for bit in [1 << i for i in range(count.bit_length() - 1)] if bits is None else bits:
        value = value + lax.ppermute(value, axis, [(i, i ^ bit) for i in range(count)])
    return value


def total_over(value, axis):
    count = lax.axis_size(axis)
    bit = 1
    if (count.bit_length() - 1) % 2:
        value = value + lax.ppermute(value, axis, [(i, i ^ bit) for i in range(count)])
        bit = 2
    while bit < count:
        one, two, three = [
            lax.ppermute(value, axis, [(i, i ^ k) for i in range(count)]) for k in (bit, 2 * bit, 3 * bit)
        ]
        value = (value + one) + (two + three)
        bit *= 4
    return value


def low(x):
    return x.astype(bf16)


def lnn(a, b):
    return nn(low(a), low(b))


def lnt(a, b):
    return nt(low(a), low(b))


def ltn(a, b):
    return tn(low(a), low(b))


def load_w_in(table, pieces, at, w_in):
    for i, piece in enumerate(pieces):
        w_in[pl.ds(pl.multiple_of(table[i], 16), piece.shape[0]), :] = piece[:, at : at + w_in.shape[1]]


def split_out(step, me, table, *refs):
    pieces, outs = refs[:-4], refs[-4:]
    span = outs[0].shape[0]
    for i, piece in enumerate(pieces):
        row = table[i]
        for k, out in enumerate(outs):

            @pl.when((row // span) ^ me[0] == k)
            def _():
                out[pl.ds(pl.multiple_of(row % span, step), piece.shape[0]), :] = piece[...]


def load_w_down(table, pieces, rows, at, w_down):
    step = rows // 4
    wide = w_down.shape[1] // 4 * 3
    third = wide // 3
    for i, piece in enumerate(pieces):
        base = table[i] // rows * (3 * step)
        skip = rows // 2 if i == len(pieces) - 1 and piece.shape[0] < rows else 0
        for k in range(piece.shape[0] // step):
            block = piece[k * step : (k + 1) * step, at : at + wide]
            row = k + skip // step
            if row < 3:
                w_down[pl.ds(pl.multiple_of(base + row * step, step), step), :wide] = block
            else:
                for j in range(3):
                    w_down[pl.ds(pl.multiple_of(base + j * step, step), step), wide:] = block[
                        :, j * third : (j + 1) * third
                    ]


def load_w_out(me, step, quarters, w_out):
    wide = quarters[0].shape[1] // 2
    for k, quarter in enumerate(quarters):
        cols = pl.ds(pl.multiple_of((me[0] ^ k) * wide, 128), wide)
        for j in range(0, quarter.shape[0], step):
            for i in range(2):
                w_out[2 * j + i * step : 2 * j + (i + 1) * step, cols] = quarter[j : j + step, i * wide : (i + 1) * wide]


def rows_of(ref, pieces):
    span = pieces[0].shape[0]
    for k, piece in enumerate(pieces):
        ref[k * span : (k + 1) * span, :] = piece[...].astype(ref.dtype)


def block_order(far_first):
    return (1, (2, 3)) if far_first else (2, (1, 3))


def block_out(far_first, near, single, pair, col, value):
    span = near.shape[0]
    cols = slice(col, col + value.shape[1])
    one, two = block_order(far_first)
    near[:, cols] = value[:span]
    single[:, cols] = low(value[one * span : (one + 1) * span])
    for i, k in enumerate(two):
        pair[i, :, cols] = low(value[k * span : (k + 1) * span])


def tile_masks(size):
    rows = lax.broadcasted_iota(jnp.int32, (size, size), 0)
    columns = lax.broadcasted_iota(jnp.int32, (size, size), 1)
    return rows, columns


def unit_lower_inverses(lowers, inverses, keep):
    size = keep[0].shape[0]
    rows, columns = tile_masks(size)
    eye = jnp.where(rows == columns, 1.0, 0.0).astype(f32)
    block = 1
    while block < size:
        wide = 2 * block
        inside = (rows // wide == columns // wide) & (rows // block != columns // block)
        if block == 1:
            for lower, inverse in zip(lowers, inverses):
                inverse[...] = eye - jnp.where(inside, lower[...], 0.0)
        else:
            for lower, inverse, right in zip(lowers, inverses, keep):
                right[...] = nn(jnp.where(inside, lower[...], 0.0), inverse[...], high)
            for inverse, right in zip(inverses, keep):
                inverse[...] = inverse[...] - nn(inverse[...], right[...], high)
        block = wide


def shifted_rows(value, count, offset):
    if offset == 0:
        return value[:count]
    if offset % 8 == 0:
        return value[offset : offset + count]
    return pltpu.roll(value, value.shape[0] - offset, 0)[:count]


def half_sum(x):
    half = x.shape[1] // 2
    left = jnp.sum(x[:, :half], 1, keepdims=True)
    right = jnp.sum(x[:, half:], 1, keepdims=True)
    lane = lax.broadcasted_iota(jnp.int32, x.shape, 1)
    return jnp.where(lane < half, left, right)


def half_rsqrt(x):
    half = x.shape[1] // 2
    sq = x * x
    left = lax.rsqrt(jnp.sum(sq[:, :half], 1, keepdims=True) + epsilon)
    right = lax.rsqrt(jnp.sum(sq[:, half:], 1, keepdims=True) + epsilon)
    lane = lax.broadcasted_iota(jnp.int32, x.shape, 1)
    return jnp.where(lane < half, left, right)


def conv_block(ext, cw, start, col, span, width):
    window = ext[pl.ds(start, span + 8), col : col + width]
    out = None
    for j in range(4):
        term = shifted_rows(window, span, 5 + j) * cw[j : j + 1, col : col + width]
        out = term if out is None else out + term
    return out


def gates(gs, rb, start, span, col, tri):
    z = gs[pl.ds(start, span), col : col + 128]
    moved = z + rb[1:2, :]
    soft = jnp.maximum(moved, 0.0) + jnp.log(1.0 + jnp.exp(-jnp.abs(moved)))
    return lax.logistic(z), nn(tri, -rb[0:1, :] * soft, high), lax.logistic(moved)


def decay_ratio(c, c_row, inclusive):
    return jnp.where(inclusive, jnp.exp(jnp.where(inclusive, c - c_row, 0.0)), 0.0)


class Layout:
    def __init__(self, width, value_width, hidden, parts):
        counts = [4 * width, 2 * width, value_width, hidden, 4 * value_width, width, 2 * hidden, width]
        at = [sum(counts[:i]) for i in range(8)]
        self.a_in, self.a_gu, self.a_out, self.a_down, self.b_in, self.b_out, self.b_gu, self.b_down = at
        self.total = sum(counts)
        self.width, self.value_width, self.hidden = width, value_width, hidden
        self.own = value_width // parts


def mixer_forward(lay, heads, span, blocks, count, flow, me, table, *refs):
    (x0, x1, x2, x3, gain, a_in, b_in, cw, rb, hg), refs = refs[:10], refs[10:]
    pieces, refs = refs[:count], refs[count:]
    (h1, z_in, pre, gate_out, small_out, gated, ou_out, s_out, tri_out, w_in), scratch = refs[:10], refs[10:]
    gs, ext, state, kqs, vs, keep = scratch

    def weights():
        flow.need(10 + count)
        load_w_in(table, pieces, pieces[0].shape[1] - w_in.shape[1], w_in)
        flow.give(9)

    mixer_prepare(
        lay, heads, span, blocks, flow, me, weights, w_in, (x0, x1, x2, x3, gain, a_in, b_in, cw, rb),
        (h1, z_in, pre, gate_out, small_out, kqs, vs, tri_out), (gs, ext, keep), 10, (0, 1, 2, 3, 4), (8,)
    )
    mixer_advance(heads, span, blocks, me, (gate_out, small_out, kqs, vs, tri_out, rb, hg), (gated, ou_out, s_out), state)


def mixer_first(lay, heads, span, blocks, flow, me, x0, x1, x2, x3, gain, a_in, b_in, cw, rb, w_in,
                h1, z_in, pre, gate_out, small_out, kqs, vs, tri_out, gs, ext, keep):
    mixer_prepare(
        lay, heads, span, blocks, flow, me, partial(flow.need, 10), w_in, (x0, x1, x2, x3, gain, a_in, b_in, cw, rb),
        (h1, z_in, pre, gate_out, small_out, kqs, vs, tri_out), (gs, ext, keep), 9, (0, 1, 2, 3, 4), (5, 6, 7)
    )


def mixer_second(lay, micro, heads, span, blocks, flow, me, kqs, vs, tri, gate_in, small_in, rb, hg, a_out, b_out, w_out,
                 near, single, pair, z_out, gated, ou_out, s_out, state):
    flow.need(7)
    mixer_advance(heads, span, blocks, me, (gate_in, small_in, kqs, vs, tri, rb, hg), (gated, ou_out, s_out), state)
    flow.give(4, 5, 6)
    flow.need(10)
    project_output(lay, micro, gated, a_out, b_out, w_out, near, single, pair, z_out)


def mixer_prepare(lay, heads, span, blocks, flow, me, weights, w_in, ins, outs, scratch, small_ins, early, late):
    x0, x1, x2, x3, gain, a_in, b_in, cw, rb = ins
    h1, z_in, pre, gate_out, small_out, kqs, vs, tri_out = outs
    gs, ext, keep = scratch
    head = 256
    here = me[0]
    own = lay.own
    flow.need(5)
    for k, piece in enumerate((x0, x1, x2, x3)):
        x = piece[...].astype(f32)
        h1[k * span : (k + 1) * span, :] = low(
            x * lax.rsqrt(jnp.mean(x * x, 1, keepdims=True) + epsilon) * gain[...]
        )
    flow.need(small_ins)
    z_in[...] = low(nt(h1[...], a_in[...]))
    weights()
    ext[0:8, :] = jnp.zeros((8, ext.shape[1]), f32)
    for col in range(0, 4 * own + 128, 256):
        wide = min(256, 4 * own + 128 - col)
        value = nn(h1[...], w_in[:, col : col + wide])
        if col < 4 * own:
            value = value + nn(z_in[...], b_in[:, col : col + wide])
        for k in range(blocks):
            part = value[k * span : (k + 1) * span]
            start = pl.multiple_of((k ^ here) * span, span)
            if col < 3 * own:
                part = low(part)
                pre[pl.ds(start, span), col : col + wide] = part
                ext[pl.ds(start + 8, span), col : col + wide] = part.astype(f32)
            else:
                at = col - 3 * own
                if at < own:
                    gate_out[pl.ds(start, span), at : at + wide] = low(part)
                else:
                    small_out[pl.ds(start, span), :] = part
    flow.give(*early)
    grow, gcol = tile_masks(span)
    inclusive = grow >= gcol
    strictly = grow > gcol
    tri = jnp.where(inclusive, 1.0, 0.0).astype(f32)
    scale_k = 0.5**0.5
    scale_q = 128 ** (-0.5) * 0.5**0.5

    def prepare(n, carry):
        start = pl.multiple_of(n * span, span)
        betas, running, _ = gates(small_out, rb, start, span, 0, tri)
        running_t = running.T
        for h in range(heads):
            q = conv_block(ext, cw, start, h * head, span, head)
            k = conv_block(ext, cw, start, (heads + h) * head, span, head)
            v = conv_block(ext, cw, start, (2 * heads + h) * head, span, head)
            q = q * lax.logistic(q)
            k = k * lax.logistic(k)
            vs[h, n] = (v * lax.logistic(v)).astype(vs.dtype)
            q = low(q * (half_rsqrt(q) * scale_q))
            k = low(k * (half_rsqrt(k) * scale_k))
            kqs[h, n, :span] = k
            kqs[h, n, span:] = q
            both = nt(kqs[h, n], k)
            ratio = decay_ratio(running[:, h : h + 1], running_t[h : h + 1, :], inclusive)
            kr = jnp.where(strictly, ratio * both[:span], 0.0)
            tri_out[2, h, n] = low(kr)
            tri_out[1, h, n] = low(both[span:] * ratio)
            keep[1, h * blocks + n] = kr * betas[:, heads + h : heads + h + 1]
        return carry

    lax.fori_loop(0, blocks, prepare, 0)
    pairs = [(h, n) for h in range(heads) for n in range(blocks)]
    unit_lower_inverses(
        [keep.at[1, h * blocks + n] for h, n in pairs],
        [keep.at[2, h * blocks + n] for h, n in pairs],
        [keep.at[0, h * blocks + n] for h, n in pairs],
    )
    for h, n in pairs:
        tri_out[0, h, n] = low(keep[2, h * blocks + n])
    flow.give(*late)


def mixer_advance(heads, span, blocks, me, ins, outs, state):
    gate_in, small_in, kqs, vs, tri_in, rb, hg = ins
    gated, ou_out, s_out = outs
    head = 256
    here = me[0]
    grow, gcol = tile_masks(span)
    tri = jnp.where(grow >= gcol, 1.0, 0.0).astype(f32)
    state[...] = jnp.zeros_like(state)

    def advance(n, carry):
        start = pl.multiple_of(n * span, span)
        row = pl.multiple_of((n ^ here) * span, span)
        betas, running, _ = gates(small_in, rb, start, span, 0, tri)
        for h in range(heads):
            cols = slice(h * head, (h + 1) * head)
            c, b = running[:, h : h + 1], betas[:, heads + h : heads + h + 1]
            d = jnp.exp(c)
            last = c[span - 1 : span, :]
            old = state[h]
            low_old = low(old)
            s_out[h, n] = low_old
            seen = nn(kqs[h, n], low_old)
            u = low(nn(tri_in[0, h, n], low(b * (vs[h, n].astype(f32) - d * seen[:span]))))
            o = d * seen[span:] + nn(tri_in[1, h, n], u)
            ou_out[1, pl.ds(start, span), cols] = u
            ou_out[0, pl.ds(start, span), cols] = low(o)
            weighted = low(kqs[h, n, :span].astype(f32) * jnp.exp(last - c))
            state[h] = jnp.exp(last) * old + tn(weighted, u)
            norm = o * lax.rsqrt(jnp.mean(o * o, 1, keepdims=True) + epsilon) * hg[...]
            gate = gate_in[pl.ds(start, span), cols].astype(f32)
            gated[pl.ds(row, span), cols] = low(norm * (gate * lax.logistic(gate)))
        return carry

    lax.fori_loop(0, blocks, advance, 0)


def project_output(lay, micro, gated, a_out, b_out, w_out, near, single, pair, z_out):
    z_out[...] = low(nt(gated[...], a_out[...]))
    for col in range(0, lay.width, 256):
        value = nn(gated[...], w_out[:, col : col + 256]) + nn(z_out[...], b_out[:, col : col + 256])
        block_out(True, near, single, pair, col, value)


def mixer_output(lay, micro, step, flow, me, gated, a_out, b_out, q0, q1, q2, q3, near, single, pair, z_out, w_out):
    flow.need(7)
    load_w_out(me, step, (q0, q1, q2, q3), w_out)
    flow.give(4)
    project_output(lay, micro, gated, a_out, b_out, w_out, near, single, pair, z_out)


def mixer_backward(lay, micro, heads, span, blocks, windows, flow, me, g0, g1, g2, g3, a_out, b_out, w_out,
                   a_in, b_in, cw, rb, hg, pre, gates_in, small_in, ou_in, s_in, tri_in,
                   z_out, gated, z_in, w_in, h1,
                   ga_gu, g_hidden, gb_down, near, single, pair, send_near, send_single, send_pair,
                   ext, back, dstate, gbranch, dgated, dproj, dsmall, flat):
    head = 256
    here = me[0]
    own = lay.own
    width = lay.width
    flow.need(7)
    rows_of(gbranch, (g0, g1, g2, g3))
    gz_out = low(nt(gbranch[...], b_out[...]))
    for col in range(0, own, 256):
        dgated[:, col : col + 256] = low(
            nt(gbranch[...], w_out[col : col + 256, :]) + nn(gz_out, a_out[:, col : col + 256])
        )
    flow.need(18)
    grow, gcol = tile_masks(span)
    inclusive = grow >= gcol
    strictly = grow > gcol
    tri = jnp.where(inclusive, 1.0, 0.0).astype(f32)
    scale_k = 0.5**0.5
    scale_q = 128 ** (-0.5) * 0.5**0.5
    ext[0:8, :] = jnp.zeros((8, ext.shape[1]), f32)
    ext[8:, :] = pre[...].astype(f32)
    back[...] = jnp.zeros_like(back)
    dstate[...] = jnp.zeros_like(dstate)
    lane = lax.broadcasted_iota(jnp.int32, (span, 128), 1)
    sub = lax.broadcasted_iota(jnp.int32, (span, 128), 0)
    final = lax.broadcasted_iota(jnp.int32, (span, 1), 0) == span - 1

    def step(i, carry):
        n = blocks - 1 - i
        row = pl.multiple_of((n ^ here) * span, span)
        start = pl.multiple_of(n * span, span)
        betas, running, slope = gates(small_in, rb, start, span, 0, tri)
        running_t = running.T
        drunning = jnp.zeros((span, 128), f32)
        by_row = jnp.zeros((span, 128), f32)
        dbetas = jnp.zeros((span, 128), f32)
        for h in range(heads):
            cols = slice(h * head, (h + 1) * head)
            cq = conv_block(ext, cw, start, h * head, span, head)
            ck = conv_block(ext, cw, start, (heads + h) * head, span, head)
            cv = conv_block(ext, cw, start, (2 * heads + h) * head, span, head)
            sq, sk, sv = lax.logistic(cq), lax.logistic(ck), lax.logistic(cv)
            qa, ka, v = cq * sq, ck * sk, cv * sv
            rq, rk = half_rsqrt(qa), half_rsqrt(ka)
            q = qa * (rq * scale_q)
            k = ka * (rk * scale_k)
            kq = jnp.concatenate([low(k), low(q)], 0)
            c = running[:, h : h + 1]
            b = betas[:, heads + h : heads + h + 1]
            d = jnp.exp(c)
            last = c[span - 1 : span, :]
            w = jnp.exp(last - c)
            inv, att = tri_in[0, h, n], tri_in[1, h, n]
            kr = tri_in[2, h, n].astype(f32)
            u = ou_in[1, pl.ds(start, span), cols]
            o = ou_in[0, pl.ds(start, span), cols].astype(f32)
            old = s_in[h, n]
            after = dstate[h]
            gate = gates_in[pl.ds(start, span), cols].astype(f32)
            dy = dgated[pl.ds(row, span), cols].astype(f32)
            sg = lax.logistic(gate)
            r = lax.rsqrt(jnp.mean(o * o, 1, keepdims=True) + epsilon)
            dn = dy * (gate * sg) * hg[...]
            normed = o * r
            dproj[pl.ds(row, span), (3 * heads + h) * head : (3 * heads + h + 1) * head] = low(
                dy * (normed * hg[...]) * (sg * (1.0 + gate * (1.0 - sg)))
            )
            do = r * (dn - normed * jnp.mean(normed * dn, 1, keepdims=True))
            seen = nn(kq, old)
            low_after, low_do = low(after), low(do)
            x = v - d * seen[:span]
            du = tn(att, low_do) + lnn(k * w, low_after)
            datt = jnp.where(inclusive, nt(low_do, u), 0.0)
            dweighted = nt(u, low_after)
            y = ltn(inv, du)
            dlow = jnp.where(strictly, -lnt(y, u), 0.0)
            dx = b * y
            db = jnp.sum(y * x, 1, keepdims=True) + jnp.sum(dlow * kr, 1, keepdims=True)
            dseen = jnp.concatenate([low(-(d * dx)), low(d * do)], 0)
            dstate[h] = jnp.exp(last) * after + tn(kq, dseen)
            dkq = nt(dseen, old)
            dd = jnp.sum(do * seen[span:] - dx * seen[:span], 1, keepdims=True)
            ratio = decay_ratio(c, running_t[h : h + 1, :], inclusive)
            dboth = jnp.concatenate([low(dlow * b * ratio), low(datt * ratio)], 0)
            dkq = dkq + nn(dboth, kq[:span])
            dk = dkq[:span] + tn(dboth, kq) + dweighted * w
            dq = dkq[span:]
            grown = dlow * (b * kr) + datt * att
            dw = jnp.sum(dweighted * k, 1, keepdims=True) * w
            dlast = jnp.exp(last) * jnp.sum(
                jnp.sum(after * old.astype(f32), 1, keepdims=True), 0, keepdims=True
            ) + jnp.sum(dw, 0, keepdims=True)
            dc = jnp.sum(grown, 1, keepdims=True) - dw + dd * d + jnp.where(final, dlast, 0.0)
            drunning = drunning + jnp.where(lane == h, dc, 0.0)
            by_row = by_row + jnp.where(sub == h, jnp.sum(grown, 0, keepdims=True), 0.0)
            dbetas = dbetas + jnp.where(lane == heads + h, db, 0.0)
            dqa = rq * scale_q * dq - qa * (rq * rq * rq * scale_q) * half_sum(qa * dq)
            dka = rk * scale_k * dk - ka * (rk * rk * rk * scale_k) * half_sum(ka * dk)
            for part, grad, sig, act in ((0, dqa, sq, cq), (1, dka, sk, ck), (2, dx, sv, cv)):
                col = (part * heads + h) * head
                through = grad * (sig * (1.0 + act * (1.0 - sig)))
                window = jnp.concatenate([through, back[:, col : col + head]], 0)
                back[:, col : col + head] = through[:8]
                out = None
                for j in range(4):
                    term = shifted_rows(window, span, 3 - j) * cw[j : j + 1, col : col + head]
                    out = term if out is None else out + term
                dproj[pl.ds(row, span), col : col + head] = low(out)
        dlog = tn(tri, drunning - by_row.T, high)
        dsmall[pl.ds(row, span), :] = low(
            -rb[0:1, :] * slope * dlog + dbetas * betas * (1.0 - betas)
        )
        return carry

    lax.fori_loop(0, blocks, step, 0)
    flow.need(26)
    gz_in = low(nt(dproj[...], b_in[...]))
    for col in range(0, width, 256):
        value = (
            nt(dproj[...], w_in[col : col + 256, : 4 * own])
            + nt(dsmall[...], w_in[col : col + 256, 4 * own :])
            + nn(gz_in, a_in[:, col : col + 256])
        )
        block_out(micro == 0, near, single, pair, col, value)
    flow.give(0, 1, 2)
    ga_out = tn(gz_out, gated[...])
    gb_out = tn(z_out[...], gbranch[...])
    flat[...] = jnp.zeros_like(flat)
    ga_in = low(tn(gz_in, h1[...]))
    for p in range(4):
        flat[:, lay.a_in + p * width : lay.a_in + (p + 1) * width] = ga_in[p * RANK : (p + 1) * RANK]
        gb = tn(z_in[...], dproj[:, p * own : (p + 1) * own])
        flat[:, pl.ds(pl.multiple_of(lay.b_in + p * lay.value_width + here * own, 128), own)] = low(
            gb[p * RANK : (p + 1) * RANK]
        )
    flat[:, pl.ds(pl.multiple_of(lay.a_out + here * own, 128), own)] = low(ga_out)
    flat[:, lay.b_out : lay.b_out + width] = low(gb_out)
    for i in range(2):
        flat[:, lay.a_gu + i * width : lay.a_gu + (i + 1) * width] = ga_gu[i * RANK : (i + 1) * RANK, :]
    hidden = lay.hidden
    flat[:, lay.a_down : lay.a_down + hidden] = g_hidden[:RANK, :]
    for i in range(2):
        flat[:, lay.b_gu + i * hidden : lay.b_gu + (i + 1) * hidden] = g_hidden[(i + 1) * RANK : (i + 2) * RANK, :]
    flat[:, lay.b_down : lay.b_down + width] = gb_down[...]
    quarter = send_near.shape[2]
    one, two = block_order(micro == 0)
    sends = {0: send_near, one: send_single, two[0]: send_pair.at[0], two[1]: send_pair.at[1]}
    for k, send in sends.items():
        for f, window in enumerate(windows):
            at = pl.multiple_of(window + (here ^ k) * quarter, 128)
            send[f] = flat[:, pl.ds(at, quarter)]


def feed_forward_blocks(lay, micro, count, packed, flow, table, *refs):
    ins, pieces, rest = refs[:6], refs[6 : 6 + count], refs[6 + count :]
    more = 5 if packed else 6
    outs, w_gu = rest[more : more + 9], rest[more + 9]
    if packed:
        w_down, scratch = rest[more + 10], rest[more + 11 :]
    else:
        w_down, scratch = rest[5], rest[more + 10 :]

    def weights():
        flow.need(6 + count)
        load_w_in(table, pieces, 0, w_gu)
        flow.give(9)
        if packed:
            load_w_down(table, pieces, packed, w_gu.shape[1], w_down)
            flow.give(10)

    feed_forward(lay, micro, flow, weights, 6 + count + more, w_gu, ins, (*rest[:5], w_down), outs, scratch)


def feed_forward_whole(lay, micro, flow, *refs):
    ins, w_gu, rest = refs[:6], refs[6], refs[7:]
    feed_forward(lay, micro, flow, partial(flow.need, 7), 13, w_gu, ins, rest[:6], rest[6:15], rest[15:])


def feed_forward(lay, micro, flow, weights, last_ins, w_gu, ins, more_ins, outs, scratch):
    h0, h1, h2, h3, a_gu, hidden = ins
    g0, g1, g2, g3, b_down, w_down = more_ins
    near, single, pair, gnear, gsingle, gpair, ga_gu, g_own, gb_down = outs
    hs, gs, b_gate, b_up, act, ggate, gup, gates, ups = scratch
    width = lay.width
    wide = act.shape[1]
    flow.need(6)
    rows_of(hs, (h0, h1, h2, h3))
    at = [(3 * micro + i) * RANK for i in range(3)]
    a_down = hidden[at[0] : at[0] + RANK, :]
    b_gate[...] = jnp.zeros_like(b_gate)
    b_up[...] = jnp.zeros_like(b_up)
    b_gate[:RANK, :] = hidden[at[1] : at[1] + RANK, :]
    b_up[RANK:, :] = hidden[at[2] : at[2] + RANK, :]
    z_gu = low(nt(hs[...], a_gu[...]))
    weights()
    for col in range(0, wide, 256):
        cols = slice(col, col + 256)
        gates[:, cols] = nn(hs[...], w_gu[:, cols]) + nn(z_gu, b_gate[:, cols])
        ups[:, cols] = nn(hs[...], w_gu[:, wide + col : wide + col + 256]) + nn(z_gu, b_up[:, cols])
    flow.need(last_ins)
    rows_of(gs, (g0, g1, g2, g3))
    gz_down = low(nt(gs[...], b_down[...]))
    for col in range(0, wide, 256):
        cols = slice(col, col + 256)
        ga, ua = gates[:, cols], ups[:, cols]
        sig = lax.logistic(ga)
        silu = ga * sig
        act[:, cols] = low(silu * ua)
        da = low(nt(gs[...], w_down[cols, :]) + nn(gz_down, a_down[:, cols])).astype(f32)
        ggate[:, cols] = low(da * ua * (sig * (1.0 + ga * (1.0 - sig))))
        gup[:, cols] = low(da * silu)
    gz_gu = low(nt(ggate[...], b_gate[...]) + nt(gup[...], b_up[...]))
    for col in range(0, width, 256):
        cols = slice(col, col + 256)
        value = (
            nt(ggate[...], w_gu[cols, :wide]) + nt(gup[...], w_gu[cols, wide:]) + nn(gz_gu, a_gu[:, cols])
        )
        block_out(micro == 0, gnear, gsingle, gpair, col, value)
    flow.give(3, 4, 5)
    z_down = low(nt(act[...], a_down))
    for col in range(0, width, 256):
        cols = slice(col, col + 256)
        value = nn(act[...], w_down[:, cols]) + nn(z_down, b_down[:, cols])
        block_out(micro == 0, near, single, pair, col, value)
    ga_gu[...] = low(tn(gz_gu, hs[...]))
    gb_down[...] = low(tn(z_down, gs[...]))
    g_own[:RANK, :] = low(tn(gz_down, act[...]))
    g_own[RANK : 2 * RANK, :] = low(tn(z_gu, ggate[...])[:RANK])
    g_own[2 * RANK :, :] = low(tn(z_gu, gup[...])[RANK:])


def adapter_rows(lay, micro_count, windows, flow, me, c0, c1, c2, c3, *refs):
    here = me[0]
    outs, used, flat = refs[:-2], refs[-2], refs[-1]
    width, own, hidden = lay.width, lay.own, lay.hidden
    flat[...] = jnp.zeros_like(flat)
    flow.need(4)
    quarter = c0.shape[2]
    for k, piece in enumerate((c0, c1, c2, c3)):
        for f, window in enumerate(windows):
            cols = pl.ds(pl.multiple_of(window + (here ^ k) * quarter, 128), quarter)
            flat[:, cols] = flat[:, cols] + piece[f]

    def own_columns(rows, at):
        return flat[rows, pl.ds(pl.multiple_of(at + here * own, 128), own)]

    for m in range(micro_count):
        rows = slice(m * RANK, (m + 1) * RANK)
        a_in, b_in, a_gu, a_out, b_out, b_down = outs[6 * m : 6 * (m + 1)]
        b_in[...] = jnp.zeros_like(b_in)
        for p in range(4):
            part = slice(p * RANK, (p + 1) * RANK)
            a_in[part, :] = flat[rows, lay.a_in + p * width : lay.a_in + (p + 1) * width]
            b_in[part, p * own : (p + 1) * own] = own_columns(rows, lay.b_in + p * lay.value_width)
        for i in range(2):
            a_gu[i * RANK : (i + 1) * RANK, :] = flat[rows, lay.a_gu + i * width : lay.a_gu + (i + 1) * width]
        a_out[...] = own_columns(rows, lay.a_out)
        b_out[...] = flat[rows, lay.b_out : lay.b_out + width]
        b_down[...] = flat[rows, lay.b_down : lay.b_down + width]
        for i, at in enumerate((lay.a_down, lay.b_gu, lay.b_gu + hidden)):
            used[(3 * m + i) * RANK : (3 * m + i + 1) * RANK, :] = flat[rows, at : at + hidden]


SMEM = pl.BlockSpec(memory_space=pltpu.SMEM)
VMEM = pl.BlockSpec(memory_space=pltpu.VMEM)


class Flow:
    def __init__(self, stages, far_in, near_in, far_out, near_out, sems):
        self.coming = [
            pltpu.make_async_copy(far, near, sems.at[i]) for i, (far, near) in enumerate(zip(far_in, near_in))
        ]
        at = len(self.coming)
        self.going = [
            pltpu.make_async_copy(near, far, sems.at[at + i]) for i, (far, near) in enumerate(zip(far_out, near_out))
        ]
        self.sent, self.stages = set(), list(stages) + [len(self.coming)]
        self.started = self.ready = 0
        self.start()

    def start(self):
        if self.stages:
            upto = self.stages.pop(0)
            for copy in self.coming[self.started : upto]:
                copy.start()
            self.started = upto

    def need(self, upto):
        while self.ready < upto:
            if self.ready == self.started:
                self.start()
            self.coming[self.ready].wait()
            self.ready += 1
            if self.ready == self.started:
                self.start()

    def give(self, *which):
        for i in which:
            if i not in self.sent:
                self.sent.add(i)
                self.going[i].start()

    def close(self):
        self.need(len(self.coming))
        self.give(*range(len(self.going)))
        for copy in self.going:
            copy.wait()


def flowing(body, stages, scalars, arrays, results, *refs):
    smem, refs = refs[:scalars], refs[scalars:]
    far_in, refs = refs[:arrays], refs[arrays:]
    far_out, refs = refs[:results], refs[results:]
    near_in, refs = refs[:arrays], refs[arrays:]
    near_out, refs = refs[:results], refs[results:]
    sems, scratch = refs[0], refs[1:]
    flow = Flow(stages, far_in, near_in, far_out, near_out, sems)
    body(flow, *smem, *near_in, *near_out, *scratch)
    flow.close()


def kernel_call(body, name, out_shape, scratch, args, scalars=1, flops=0, stages=()):
    size = sum(a.size * a.dtype.itemsize for a in args) + sum(o.size * o.dtype.itemsize for o in out_shape)
    arrays = args[scalars:]
    far = pl.BlockSpec(memory_space=pl.ANY)
    buffers = [pltpu.VMEM(a.shape, a.dtype) for a in (*arrays, *out_shape)]
    return pl.pallas_call(
        partial(flowing, body, stages, scalars, len(arrays), len(out_shape)),
        out_shape=tuple(out_shape),
        in_specs=[SMEM] * scalars + [far] * len(arrays),
        out_specs=tuple([far] * len(out_shape)),
        scratch_shapes=[*buffers, pltpu.SemaphoreType.DMA((len(buffers),)), *scratch],
        compiler_params=pltpu.CompilerParams(vmem_limit_bytes=VMEM_LIMIT),
        cost_estimate=pl.CostEstimate(flops=flops, bytes_accessed=int(size), transcendentals=0),
        name=name,
    )(*args)


class Kernels:
    def __init__(self, lay, heads, head, span, blocks, width, own, wide, windows, quarter, flat, ranks, step):
        shape = jax.ShapeDtypeStruct
        rows = blocks * span
        self.lay, self.sizes = lay, (heads, span, blocks)
        self.windows, self.step = windows, step
        self.blocks = [shape((span, width), f32), shape((span, width), bf16), shape((2, span, width), bf16)]
        send = (ranks, RANK, quarter)
        self.sends = [shape(send, bf16), shape(send, bf16), shape((2, *send), bf16)]
        self.z_out = shape((rows, RANK), bf16)
        self.saved = [
            shape((rows, width), bf16),
            shape((rows, 4 * RANK), bf16),
            shape((rows, 3 * own), bf16),
            shape((rows, own), bf16),
            shape((rows, 128), f32),
            shape((rows, own), bf16),
            shape((2, rows, own), bf16),
            shape((heads, blocks, head, head), bf16),
            shape((3, heads, blocks, span, span), bf16),
        ]
        self.small = [shape((2 * RANK, width), bf16), shape((3 * RANK, wide), bf16), shape((RANK, width), bf16)]
        self.w_gu, self.w_down = shape((width, 2 * wide), bf16), shape((wide, width), bf16)
        self.w_in, self.w_out = shape((width, 4 * own + 128), bf16), shape((own, width), bf16)
        ext = pltpu.VMEM((rows + 8, 3 * own), f32)
        state = pltpu.VMEM((heads, head, head), f32)
        self.kq = shape((heads, blocks, 2 * span, head), bf16)
        self.v = shape((heads, blocks, span, head), bf16)
        keep = pltpu.VMEM((3, heads * blocks, span, span), f32)
        self.state = state
        self.first_scratch = [pltpu.VMEM((8, 128), f32), ext, keep]
        self.forward_scratch = [
            pltpu.VMEM((8, 128), f32),
            ext,
            state,
            pltpu.VMEM(self.kq.shape, bf16),
            pltpu.VMEM(self.v.shape, f32),
            keep,
        ]
        self.feed_scratch = (
            [pltpu.VMEM((rows, width), bf16)] * 2
            + [pltpu.VMEM((2 * RANK, wide), bf16)] * 2
            + [pltpu.VMEM((rows, wide), bf16)] * 3
            + [pltpu.VMEM((rows, wide), f32)] * 2
        )
        self.backward_scratch = [
            ext,
            pltpu.VMEM((8, 3 * own), f32),
            state,
            pltpu.VMEM((rows, width), bf16),
            pltpu.VMEM((rows, own), bf16),
            pltpu.VMEM((rows, 4 * own), bf16),
            pltpu.VMEM((rows, 128), bf16),
            pltpu.VMEM((RANK, flat), bf16),
        ]

    def forward(self, m, me, table, w_in, x, gain, adapters, cw, rb, hg):
        outs = kernel_call(
            partial(mixer_forward, self.lay, *self.sizes, len(w_in)),
            "mixer_forward",
            self.saved + [self.w_in],
            self.forward_scratch,
            (me, table, *x, gain, *adapters, cw, rb, hg, *w_in),
            scalars=2,
            stages=(5,),
            flops=6_000_000_000,
        )
        return outs[:-1], outs[-1]

    def first(self, m, me, w_in, x, gain, adapters, cw, rb):
        return kernel_call(
            partial(mixer_first, self.lay, *self.sizes),
            "mixer_first",
            self.saved[:5] + [self.kq, self.v, self.saved[8]],
            self.first_scratch,
            (me, *x, gain, *adapters, cw, rb, w_in),
            stages=(5,),
            flops=5_000_000_000,
        )

    def second(self, m, me, w_out, done, adapters, rb, hg):
        h1, z_in, pre, gate, small, kq, v, tri = done
        outs = kernel_call(
            partial(mixer_second, self.lay, m, *self.sizes),
            "mixer_second",
            self.blocks + [self.z_out] + self.saved[5:8],
            [self.state],
            (me, kq, v, tri, gate, small, rb, hg, *adapters, w_out),
            flops=3_000_000_000,
        )
        return outs[:3], outs[3], (h1, z_in, pre, gate, small, *outs[4:], tri)

    def output(self, m, me, w_out, gated, adapters):
        outs = kernel_call(
            partial(mixer_output, self.lay, m, self.step),
            "mixer_output",
            self.blocks + [self.z_out, self.w_out],
            [],
            (me, gated, *adapters, *w_out),
            flops=1_000_000_000,
        )
        return outs[:3], outs[3], outs[4]

    def feed(self, m, table, h2, cot, w_gu, w_down, a_gu, b_down, hidden):
        whole, packed = len(w_gu) == 1, w_down is None
        if whole:
            body = partial(feed_forward_whole, self.lay, m)
        else:
            body = partial(feed_forward_blocks, self.lay, m, len(w_gu), w_gu[0].shape[0] if packed else 0)
        more = [] if whole else [self.w_gu] + ([self.w_down] if packed else [])
        outs = kernel_call(
            body,
            "feed_forward",
            self.blocks * 2 + self.small + more,
            self.feed_scratch,
            (*([] if whole else [table]), *h2, a_gu, hidden, *w_gu, *cot, b_down, *([] if packed else [w_down])),
            scalars=0 if whole else 1,
            stages=(6, 6 + len(w_gu)),
            flops=5_000_000_000,
        )
        full = w_gu[0] if whole else outs[9]
        return outs[:3], outs[3:6], outs[6:9], full, outs[10] if packed else w_down

    def backward(self, m, me, w_in, w_out, g_branch, in_adapters, out_adapters, cw, rb, hg, z_out, saved, small):
        h1, z_in, pre, gates_in, small_in, gated, ou_in, s_in, tri_in = saved
        outs = kernel_call(
            partial(mixer_backward, self.lay, m, *self.sizes, self.windows),
            "mixer_backward",
            self.blocks + self.sends,
            self.backward_scratch,
            (
                me,
                *g_branch,
                *out_adapters,
                w_out,
                *in_adapters,
                cw,
                rb,
                hg,
                pre,
                gates_in,
                small_in,
                ou_in,
                s_in,
                tri_in,
                z_out,
                gated,
                z_in,
                w_in,
                h1,
                *small,
            ),
            stages=(7, 18),
            flops=9_000_000_000,
        )
        return outs[:3], outs[3:]


def rms_norm(inputs, scales):
    return inputs * lax.rsqrt(jnp.mean(inputs * inputs, -1, keepdims=True) + epsilon) * scales


def own_lanes(value, start, size):
    return lax.dynamic_slice_in_dim(value, start, size, axis=value.ndim - 1)


def shards(
    tokens,
    cotangent,
    lengths,
    adapter_index,
    step_count,
    w_in,
    w_out,
    w_gu,
    w_down,
    conv_weight,
    norm_gains,
    head_gain,
    decay_rate,
    decay_bias,
    adapters,
    first_moment,
    second_moment,
):
    micro_count, _, span, width = tokens.shape
    ranks = lax.axis_size("fsdp")
    parts = lax.axis_size("seq")
    here = lax.axis_index("seq")
    place = lax.axis_index("fsdp")
    all_heads = decay_rate.shape[0]
    heads = all_heads // parts
    value_width = conv_weight.shape[1] // 3
    own = value_width // parts
    hidden = w_gu.shape[1] // 2
    piece = w_down.shape[0] // parts
    wide = -(-hidden // parts // 256) * 256
    padded = wide // ranks
    columns = adapters.shape[1]
    shard_rows = adapters.shape[0]
    rows = parts * span
    me = here.astype(jnp.int32).reshape(1)
    lay = Layout(width, value_width, hidden, parts)
    shape = jax.ShapeDtypeStruct

    bits = [1 << i for i in range(ranks.bit_length() - 1)]
    picks = lax.dynamic_update_slice(
        jnp.zeros((ranks, 128), jnp.int32), jnp.pad(adapter_index.T, ((0, 0), (0, 128 - micro_count))), (place, 0)
    )
    picks = butterfly(picks, "fsdp", bits[:1])

    def heads_slice(part):
        return own_lanes(w_in, part * value_width + here * own, own)

    small = jnp.concatenate(
        [
            own_lanes(w_in, 4 * value_width + here * heads, heads),
            own_lanes(w_in, 4 * value_width + all_heads + here * heads, heads),
            jnp.zeros((w_in.shape[0], 128 - 2 * heads), bf16),
        ],
        1,
    )
    in_rows = w_in.shape[0]
    local_out = own_lanes(w_out, here * (width // parts), width // parts)
    local_in = jnp.concatenate(
        [local_out[:in_rows], local_out[in_rows:]] + [heads_slice(p) for p in range(4)] + [small], 1
    )
    ring = RingGather(local_in)

    window = -(-(shard_rows + 127) // (128 * parts)) * 128 * parts
    quarter = window // parts
    windows = [shard_rows * f // 128 * 128 for f in range(ranks)]
    flat_width = windows[-1] + window
    offset = (shard_rows * place) % 128
    framed = lax.dynamic_update_slice(
        jnp.zeros((window, columns), bf16), adapters.astype(bf16), (offset, 0)
    )
    framed = lax.dynamic_slice_in_dim(framed, here * quarter, quarter, 0)
    conv_own = jnp.concatenate(
        [own_lanes(conv_weight, p * value_width + here * own, own) for p in range(3)], 1
    )
    rate_bias = jnp.zeros((8, 128), f32)
    rate_bias = rate_bias.at[0, :heads].set(lax.dynamic_slice(decay_rate, (here * heads,), (heads,)))
    rate_bias = rate_bias.at[1, :heads].set(lax.dynamic_slice(decay_bias, (here * heads,), (heads,)))
    gain_row = head_gain.reshape(1, -1)

    far_tokens = [gather_far(tokens[m, 0]) for m in range(micro_count)]
    positions = here * span + jnp.arange(span)
    cots = [
        cotangent[m, 0].astype(f32) * (positions < lengths[m, 0]).astype(f32)[:, None]
        for m in range(micro_count)
    ]
    picks = butterfly(picks, "fsdp", bits[1:])
    wanted = (picks[:, :micro_count, None] * RANK + jnp.arange(RANK)[None, None, :]).reshape(-1)
    select = (wanted[:, None] == jnp.arange(columns)[None, :]).astype(bf16)
    chosen = nt(select, framed).astype(bf16).reshape(ranks, micro_count * RANK, quarter)
    chosen, conv_own, rate_bias, table, select = ring.advance(chosen, conv_own, rate_bias, ring.table, select)
    chosen = lax.all_to_all(chosen, "fsdp", 0, 0)

    unit = after(jnp.arange(wide), ring.right)
    unit_of = (unit // padded) * w_down.shape[0] + here * piece + unit % padded
    unit_of = jnp.where(unit % padded < piece, unit_of, -1)
    spread = (jnp.arange(hidden)[:, None] == unit_of[None, :]).astype(bf16)
    local_gu = jnp.concatenate(
        [nn(w_gu[:, i * hidden : (i + 1) * hidden], spread).astype(bf16) for i in range(2)], 1
    )
    local_down = jnp.pad(
        lax.dynamic_slice_in_dim(w_down, here * piece, piece, 0), ((0, padded - piece), (0, 0))
    )
    if in_rows % 128 == 0 and 4 * padded == 3 * in_rows:
        split, step = width // 4 * 3, in_rows // 4
        thirds = [local_down[i * step : (i + 1) * step, split:] for i in range(3)]
        packed = jnp.concatenate([local_down[:, :split], jnp.concatenate(thirds, 1)], 0)
        local_gu = jnp.concatenate([local_gu, packed], 1)
    pieces = [gather_near(*far) for far in far_tokens]
    far_cots = [gather_far(low(cot)) for cot in cots]
    (far_tokens,) = ring.advance(far_tokens)

    chosen, local_gu, pieces, far_cots = ring.advance(chosen, local_gu, pieces, far_cots)
    cot_pieces = [gather_near(*far) for far in far_cots]
    chosen, beyond = ring.advance(*gather_far(chosen))
    chosen = gather_near(chosen, beyond)
    while not ring.done():
        ring.advance()
    quarter_width = 2 * (width // parts)
    out_sorted = pl.pallas_call(
        partial(split_out, min(block.shape[0] for block in ring.blocks)),
        grid=(1,),
        out_shape=[shape((width // parts, quarter_width), bf16)] * parts,
        in_specs=[SMEM, SMEM]
        + [pl.BlockSpec((block.shape[0], quarter_width), lambda i: (0, 0)) for block in ring.blocks],
        out_specs=[pl.BlockSpec((width // parts, quarter_width), lambda i: (0, 0))] * parts,
        name="split_out",
    )(me, table, *ring.blocks)
    out_quarters = [swapped(out_sorted[k], k) if k else out_sorted[k] for k in range(parts)]
    per_micro = [
        shape((4 * RANK, width), bf16),
        shape((4 * RANK, 4 * own), bf16),
        shape((2 * RANK, width), bf16),
        shape((RANK, own), bf16),
        shape((RANK, width), bf16),
        shape((RANK, width), bf16),
    ]
    *adapted, used = kernel_call(
        partial(adapter_rows, lay, micro_count, windows),
        "adapter_rows",
        per_micro * micro_count + [shape((3 * micro_count * RANK, hidden), bf16)],
        [pltpu.VMEM((micro_count * RANK, flat_width), bf16)],
        (me, *chosen),
    )
    adapted = [adapted[6 * m : 6 * (m + 1)] for m in range(micro_count)]
    hidden_own = nn(used, spread).astype(bf16)
    second_ring = RingGather(after(local_gu, ring.right))
    if in_rows % 128 == 0 and 4 * padded == 3 * in_rows:
        full_down = None
    else:
        full_down = lax.all_gather(after(local_down, ring.right), "fsdp", axis=0, tiled=True)

    first_gain = norm_gains[0].reshape(1, -1)
    micros = range(micro_count)
    inputs = [tokens[m, 0].astype(f32) for m in micros]
    kernels = Kernels(
        lay, heads, head_gain.shape[0], span, parts, width, own, wide, windows, quarter, flat_width, ranks, in_rows
    )

    def feed(m, h2, cot, w_gu, w_down):
        return kernels.feed(m, table, h2, cot, w_gu, w_down, adapted[m][2], adapted[m][5], hidden_own)

    def backward(m, g_branch, z_out, saved, small_grads):
        return kernels.backward(
            m,
            me,
            full_in,
            full_out,
            g_branch,
            adapted[m][:2],
            adapted[m][3:5],
            conv_own,
            rate_bias,
            gain_row,
            z_out,
            saved,
            small_grads,
        )

    def second_norm(middle):
        h2, pull = jax.vjp(partial(rms_norm, scales=norm_gains[1]), middle)
        return low(h2), pull

    def input_gradient(m, g_middle, g_h1):
        pull = jax.vjp(partial(rms_norm, scales=norm_gains[0]), inputs[m])[1]
        return low(g_middle + pull(low(g_h1).astype(f32))[0])

    saved0, full_in = kernels.forward(
        0, me, table, ring.blocks, pieces[0], first_gain, adapted[0][:2], conv_own, rate_bias, gain_row
    )
    (saved0,) = second_ring.advance(saved0)
    out0, z_out0, full_out = kernels.output(0, me, out_quarters, saved0[5], adapted[0][3:5])
    got0 = scatter_far(out0[2])
    begun1 = kernels.first(1, me, full_in, pieces[1], first_gain, adapted[1][:2], conv_own, rate_bias)
    got0, begun1 = second_ring.advance(got0, begun1)
    middle0 = inputs[0] + scatter_near(out0[0], out0[1], got0)
    h20, pull0 = second_norm(middle0)
    far0 = gather_far(h20)
    begun1 = held(begun1, h20)
    out1, z_out1, saved1 = kernels.second(1, me, full_out, begun1, adapted[1][3:5], rate_bias, gain_row)
    far0, out1 = second_ring.advance(far0, out1)
    h20, hidden_own = second_ring.advance(gather_near(*far0), hidden_own)
    while not second_ring.done():
        second_ring.advance()
    got1 = scatter_far(out1[2])
    last0, g_out0, grads0, full_gu, full_down = feed(0, h20, cot_pieces[0], second_ring.blocks, full_down)
    got1, last0, g_out0, grads0 = held((got1, last0, g_out0, grads0))
    middle1 = inputs[1] + scatter_near(out1[0], out1[1], got1)
    h21, pull1 = second_norm(middle1)
    h21 = gather_seq(h21)
    g_out0, h21 = held((g_out0, h21))
    g_got0 = scatter_far(g_out0[2])
    last1, g_out1, grads1, full_gu, full_down = feed(1, h21, cot_pieces[1], [full_gu], full_down)
    g_got0, last1, g_out1, grads1 = held((g_got0, last1, g_out1, grads1))
    g_h20 = scatter_near(g_out0[0], g_out0[1], g_got0)
    g_middle0 = cots[0] + pull0(low(g_h20).astype(f32))[0]
    branch0 = gather_far(low(g_middle0))
    hidden0, hidden1 = [nt(g[1], spread).astype(bf16) for g in (grads0, grads1)]
    branch0, hidden0, hidden1 = held((branch0, hidden0, hidden1))
    branch0 = gather_near(*branch0)
    g_h21 = after(scatter_seq(*g_out1), branch0[2])
    g_middle1 = cots[1] + pull1(low(g_h21).astype(f32))[0]
    branch0, g_middle1, last0 = held((branch0, g_middle1, last0))
    far1 = gather_far(low(g_middle1))
    last_got0 = scatter_far(last0[2])
    g_in0, sums0 = backward(0, branch0, z_out0, saved0, (grads0[0], hidden0, grads0[2]))
    far1, last_got0, last1, g_in0, sums0 = held((far1, last_got0, last1, g_in0, sums0))
    branch1 = gather_near(*far1)
    mixed0 = low(middle0 + scatter_near(last0[0], last0[1], last_got0))
    sums_got0 = scatter_far(sums0[2])
    g_in_got0 = scatter_far(g_in0[2])
    g_in1, sums1 = backward(1, branch1, z_out1, saved1, (grads1[0], hidden1, grads1[2]))
    sums_got0, g_in_got0, g_in1, sums1 = held((sums_got0, g_in_got0, g_in1, sums1))
    total1 = low(scatter_seq(sums1[0].astype(f32), *sums1[1:]))
    total0 = low(scatter_near(sums0[0].astype(f32), sums0[1], sums_got0))
    total = jnp.concatenate([total0, total1], 1)
    total, g_in1, last1 = held((total, g_in1, last1))
    arrived = lax.all_to_all(total, "fsdp", 0, 0)
    arrived, g_in_got0 = held((arrived, g_in_got0))
    mixed1 = low(middle1 + scatter_seq(*last1))
    grad_tokens0 = input_gradient(0, g_middle0, scatter_near(g_in0[0], g_in0[1], g_in_got0))
    grad_tokens1 = input_gradient(1, g_middle1, scatter_seq(*g_in1))
    mine = tn(arrived.reshape(-1, quarter), select)
    at = here * quarter + jnp.arange(quarter)
    mine = jnp.where(((at >= offset) & (at < offset + shard_rows))[:, None], mine, 0.0)
    squares = jnp.full((8, 128), jnp.sum(mine * mine))
    shard_grad = jnp.concatenate(in_seq_order(gather_seq(low(mine))), 0)
    shard_grad = lax.optimization_barrier(shard_grad)
    squares = total_over(total_over(squares, "seq"), "fsdp")[0, 0]
    shard_grad = lax.dynamic_slice_in_dim(shard_grad, offset, shard_rows, 0).astype(f32)
    norm_value = jnp.sqrt(squares)
    clipped = shard_grad * (CLIP_LIMIT / jnp.maximum(norm_value, CLIP_LIMIT))
    new_first = FIRST_DECAY * first_moment + (1.0 - FIRST_DECAY) * clipped
    new_second = SECOND_DECAY * second_moment + (1.0 - SECOND_DECAY) * clipped * clipped
    counter = step_count[0].astype(f32)
    corrected_first = new_first / (1.0 - jnp.power(FIRST_DECAY, counter))
    corrected_second = new_second / (1.0 - jnp.power(SECOND_DECAY, counter))
    update = -LEARN_RATE * (
        corrected_first / (jnp.sqrt(corrected_second) + ADAM_EPSILON) + WEIGHT_DECAY * adapters
    )
    return (
        jnp.stack([mixed0, mixed1], 0)[:, None],
        jnp.stack([grad_tokens0, grad_tokens1], 0)[:, None],
        update,
        new_first,
        new_second,
        norm_value.reshape(1),
    )


def solution(mesh):
    in_specs = (
        P(None, "fsdp", "seq", None),
        P(None, "fsdp", "seq", None),
        P(None, "fsdp"),
        P(None, "fsdp"),
        P(),
        P("fsdp", None),
        P("fsdp", None),
        P("fsdp", None),
        P("fsdp", None),
        P(),
        P(),
        P(),
        P(),
        P(),
        P("fsdp", None),
        P("fsdp", None),
        P("fsdp", None),
    )
    out_specs = (
        P(None, "fsdp", "seq", None),
        P(None, "fsdp", "seq", None),
        P("fsdp", None),
        P("fsdp", None),
        P("fsdp", None),
        P(),
    )
    return jax.shard_map(shards, mesh=mesh, in_specs=in_specs, out_specs=out_specs, check_vma=False)
```

```python
from functools import partial

import jax
import jax.numpy as jnp
from jax import lax
from jax.experimental import pallas as pl
from jax.experimental.pallas import tpu as pltpu
from jax.sharding import PartitionSpec as P

RANK = 16
epsilon = 1e-06
CLIP_LIMIT = 1.0
LEARN_RATE = 0.01
FIRST_DECAY = 0.9
SECOND_DECAY = 0.999
ADAM_EPSILON = 1e-08
WEIGHT_DECAY = 0.1
VMEM_LIMIT = 56 << 20

f32 = jnp.float32
bf16 = jnp.bfloat16
high = lax.Precision.HIGH


def nn(a, b, precision=None):
    return lax.dot_general(
        a, b, (((1,), (0,)), ((), ())), precision=precision, preferred_element_type=f32
    )


def nt(a, b, precision=None):
    return lax.dot_general(
        a, b, (((1,), (1,)), ((), ())), precision=precision, preferred_element_type=f32
    )


def tn(a, b, precision=None):
    return lax.dot_general(
        a, b, (((0,), (0,)), ((), ())), precision=precision, preferred_element_type=f32
    )


def swapped(value, bit):
    count = lax.axis_size("seq")
    return lax.ppermute(value, "seq", [(i, i ^ bit) for i in range(count)])


def gather_far(value):
    return value, swapped(value, 2)


def gather_near(value, beyond):
    return value, swapped(value, 1), beyond, swapped(beyond, 1)


def gather_seq(value):
    return gather_near(*gather_far(value))


def in_seq_order(blocks):
    here = lax.axis_index("seq")
    for bit in (1, 2):
        flip = here & bit != 0
        blocks = [jnp.where(flip, blocks[k ^ bit], blocks[k]) for k in range(4)]
    return blocks


def scatter_far(far):
    return swapped(far, 2)


def scatter_near(near, beside, got):
    got = got.astype(f32)
    return near + got[0] + swapped((beside.astype(f32) + got[1]).astype(bf16), 1).astype(f32)


def scatter_seq(near, beyond, pair):
    got = swapped(pair, 1).astype(f32)
    return near + got[0] + swapped((beyond.astype(f32) + got[1]).astype(bf16), 2).astype(f32)


def held(values, *others):
    return lax.optimization_barrier((tuple(values), *others))[0]


def ring_order(count):
    return list(range(0, count, 2)) + list(range(count - 1, 0, -2))


def after(value, *others):
    return lax.optimization_barrier((value, *others))[0]


class RingGather:
    def __init__(self, value):
        count, here = lax.axis_size("fsdp"), lax.axis_index("fsdp")
        order = ring_order(count)
        place = [order.index(d) for d in range(count)]
        rows = value.shape[0]
        halves = rows // 2 % 16 == 0
        table = []
        for d in range(count):
            source = [order[(place[d] - k) % count] * rows for k in range(count)]
            at = [source[0]]
            for hop in range(1, count // 2 + 1):
                last = 2 * hop == count
                at.append(source[hop])
                if not last:
                    at.append(source[count - hop])
                elif halves:
                    at.append(source[hop] + rows // 2)
            table.append(at)
        self.count, self.hop, self.rows, self.halves = count, 0, rows, halves
        self.table = jnp.asarray(table, jnp.int32)[here]
        self.ahead = [(order[i], order[(i + 1) % count]) for i in range(count)]
        self.behind = [(b, a) for a, b in self.ahead]
        self.right = self.left = value
        self.blocks = [value]

    def advance(self, *others):
        self.hop += 1
        right, left = self.right, self.left
        half = self.rows // 2
        last = 2 * self.hop == self.count
        if last and self.halves:
            right, left = right[:half], left[half:]
        right = lax.ppermute(right, "fsdp", self.ahead)
        if not last or self.halves:
            left = lax.ppermute(left, "fsdp", self.behind)
        self.right, self.left, *others = lax.optimization_barrier((right, left, *others))
        self.blocks.append(self.right)
        if not last or self.halves:
            self.blocks.append(self.left)
        return others

    def done(self):
        return 2 * self.hop >= self.count


def butterfly(value, axis, bits=None):
    count = lax.axis_size(axis)
    for bit in [1 << i for i in range(count.bit_length() - 1)] if bits is None else bits:
        value = value + lax.ppermute(value, axis, [(i, i ^ bit) for i in range(count)])
    return value


def total_over(value, axis):
    count = lax.axis_size(axis)
    bit = 1
    if (count.bit_length() - 1) % 2:
        value = value + lax.ppermute(value, axis, [(i, i ^ bit) for i in range(count)])
        bit = 2
    while bit < count:
        one, two, three = [
            lax.ppermute(value, axis, [(i, i ^ k) for i in range(count)]) for k in (bit, 2 * bit, 3 * bit)
        ]
        value = (value + one) + (two + three)
        bit *= 4
    return value


def low(x):
    return x.astype(bf16)


def lnn(a, b):
    return nn(low(a), low(b))


def lnt(a, b):
    return nt(low(a), low(b))


def ltn(a, b):
    return tn(low(a), low(b))


def load_w_in(table, pieces, at, w_in):
    for i, piece in enumerate(pieces):
        w_in[pl.ds(pl.multiple_of(table[i], 16), piece.shape[0]), :] = piece[:, at : at + w_in.shape[1]]


def split_out(step, me, table, *refs):
    pieces, outs = refs[:-4], refs[-4:]
    span = outs[0].shape[0]
    for i, piece in enumerate(pieces):
        row = table[i]
        for k, out in enumerate(outs):

            @pl.when((row // span) ^ me[0] == k)
            def _():
                out[pl.ds(pl.multiple_of(row % span, step), piece.shape[0]), :] = piece[...]


def load_w_down(table, pieces, rows, at, w_down):
    step = rows // 4
    wide = w_down.shape[1] // 4 * 3
    third = wide // 3
    for i, piece in enumerate(pieces):
        base = table[i] // rows * (3 * step)
        skip = rows // 2 if i == len(pieces) - 1 and piece.shape[0] < rows else 0
        for k in range(piece.shape[0] // step):
            block = piece[k * step : (k + 1) * step, at : at + wide]
            row = k + skip // step
            if row < 3:
                w_down[pl.ds(pl.multiple_of(base + row * step, step), step), :wide] = block
            else:
                for j in range(3):
                    w_down[pl.ds(pl.multiple_of(base + j * step, step), step), wide:] = block[
                        :, j * third : (j + 1) * third
                    ]


def load_w_out(me, step, quarters, w_out):
    wide = quarters[0].shape[1] // 2
    for k, quarter in enumerate(quarters):
        cols = pl.ds(pl.multiple_of((me[0] ^ k) * wide, 128), wide)
        for j in range(0, quarter.shape[0], step):
            for i in range(2):
                w_out[2 * j + i * step : 2 * j + (i + 1) * step, cols] = quarter[j : j + step, i * wide : (i + 1) * wide]


def rows_of(ref, pieces):
    span = pieces[0].shape[0]
    for k, piece in enumerate(pieces):
        ref[k * span : (k + 1) * span, :] = piece[...].astype(ref.dtype)


def block_order(far_first):
    return (1, (2, 3)) if far_first else (2, (1, 3))


def block_out(far_first, near, single, pair, col, value):
    span = near.shape[0]
    cols = slice(col, col + value.shape[1])
    one, two = block_order(far_first)
    near[:, cols] = value[:span]
    single[:, cols] = low(value[one * span : (one + 1) * span])
    for i, k in enumerate(two):
        pair[i, :, cols] = low(value[k * span : (k + 1) * span])


def tile_masks(size):
    rows = lax.broadcasted_iota(jnp.int32, (size, size), 0)
    columns = lax.broadcasted_iota(jnp.int32, (size, size), 1)
    return rows, columns


def unit_lower_inverses(lowers, inverses, keep):
    size = keep[0].shape[0]
    rows, columns = tile_masks(size)
    eye = jnp.where(rows == columns, 1.0, 0.0).astype(f32)
    block = 1
    while block < size:
        wide = 2 * block
        inside = (rows // wide == columns // wide) & (rows // block != columns // block)
        if block == 1:
            for lower, inverse in zip(lowers, inverses):
                inverse[...] = eye - jnp.where(inside, lower[...], 0.0)
        else:
            for lower, inverse, right in zip(lowers, inverses, keep):
                right[...] = nn(jnp.where(inside, lower[...], 0.0), inverse[...], high)
            for inverse, right in zip(inverses, keep):
                inverse[...] = inverse[...] - nn(inverse[...], right[...], high)
        block = wide


def shifted_rows(value, count, offset):
    if offset == 0:
        return value[:count]
    if offset % 8 == 0:
        return value[offset : offset + count]
    return pltpu.roll(value, value.shape[0] - offset, 0)[:count]


def half_sum(x):
    half = x.shape[1] // 2
    left = jnp.sum(x[:, :half], 1, keepdims=True)
    right = jnp.sum(x[:, half:], 1, keepdims=True)
    lane = lax.broadcasted_iota(jnp.int32, x.shape, 1)
    return jnp.where(lane < half, left, right)


def half_rsqrt(x):
    half = x.shape[1] // 2
    sq = x * x
    left = lax.rsqrt(jnp.sum(sq[:, :half], 1, keepdims=True) + epsilon)
    right = lax.rsqrt(jnp.sum(sq[:, half:], 1, keepdims=True) + epsilon)
    lane = lax.broadcasted_iota(jnp.int32, x.shape, 1)
    return jnp.where(lane < half, left, right)


def conv_block(ext, cw, start, col, span, width):
    window = ext[pl.ds(start, span + 8), col : col + width]
    out = None
    for j in range(4):
        term = shifted_rows(window, span, 5 + j) * cw[j : j + 1, col : col + width]
        out = term if out is None else out + term
    return out


def gates(gs, rb, start, span, col, tri):
    z = gs[pl.ds(start, span), col : col + 128]
    moved = z + rb[1:2, :]
    soft = jnp.maximum(moved, 0.0) + jnp.log(1.0 + jnp.exp(-jnp.abs(moved)))
    return lax.logistic(z), nn(tri, -rb[0:1, :] * soft, high), lax.logistic(moved)


def decay_ratio(c, c_row, inclusive):
    return jnp.where(inclusive, jnp.exp(jnp.where(inclusive, c - c_row, 0.0)), 0.0)


class Layout:
    def __init__(self, width, value_width, hidden, parts):
        counts = [4 * width, 2 * width, value_width, hidden, 4 * value_width, width, 2 * hidden, width]
        at = [sum(counts[:i]) for i in range(8)]
        self.a_in, self.a_gu, self.a_out, self.a_down, self.b_in, self.b_out, self.b_gu, self.b_down = at
        self.total = sum(counts)
        self.width, self.value_width, self.hidden = width, value_width, hidden
        self.own = value_width // parts


def mixer_forward(lay, heads, span, blocks, count, flow, me, table, *refs):
    (x0, x1, x2, x3, gain, a_in, b_in, cw, rb, hg), refs = refs[:10], refs[10:]
    pieces, refs = refs[:count], refs[count:]
    (h1, z_in, pre, gate_out, small_out, gated, ou_out, s_out, tri_out, w_in), scratch = refs[:10], refs[10:]
    gs, ext, state, kqs, vs, keep = scratch

    def weights():
        flow.need(10 + count)
        load_w_in(table, pieces, pieces[0].shape[1] - w_in.shape[1], w_in)
        flow.give(9)

    mixer_prepare(
        lay, heads, span, blocks, flow, me, weights, w_in, (x0, x1, x2, x3, gain, a_in, b_in, cw, rb),
        (h1, z_in, pre, gate_out, small_out, kqs, vs, tri_out), (gs, ext, keep), 10, (0, 1, 2, 3, 4), (8,)
    )
    mixer_advance(heads, span, blocks, me, (gate_out, small_out, kqs, vs, tri_out, rb, hg), (gated, ou_out, s_out), state)


def mixer_first(lay, heads, span, blocks, flow, me, x0, x1, x2, x3, gain, a_in, b_in, cw, rb, w_in,
                h1, z_in, pre, gate_out, small_out, kqs, vs, tri_out, gs, ext, keep):
    mixer_prepare(
        lay, heads, span, blocks, flow, me, partial(flow.need, 10), w_in, (x0, x1, x2, x3, gain, a_in, b_in, cw, rb),
        (h1, z_in, pre, gate_out, small_out, kqs, vs, tri_out), (gs, ext, keep), 9, (0, 1, 2, 3, 4), (5, 6, 7)
    )


def mixer_second(lay, micro, heads, span, blocks, flow, me, kqs, vs, tri, gate_in, small_in, rb, hg, a_out, b_out, w_out,
                 near, single, pair, z_out, gated, ou_out, s_out, state):
    flow.need(7)
    mixer_advance(heads, span, blocks, me, (gate_in, small_in, kqs, vs, tri, rb, hg), (gated, ou_out, s_out), state)
    flow.give(4, 5, 6)
    flow.need(10)
    project_output(lay, micro, gated, a_out, b_out, w_out, near, single, pair, z_out)


def mixer_prepare(lay, heads, span, blocks, flow, me, weights, w_in, ins, outs, scratch, small_ins, early, late):
    x0, x1, x2, x3, gain, a_in, b_in, cw, rb = ins
    h1, z_in, pre, gate_out, small_out, kqs, vs, tri_out = outs
    gs, ext, keep = scratch
    head = 256
    here = me[0]
    own = lay.own
    flow.need(5)
    for k, piece in enumerate((x0, x1, x2, x3)):
        x = piece[...].astype(f32)
        h1[k * span : (k + 1) * span, :] = low(
            x * lax.rsqrt(jnp.mean(x * x, 1, keepdims=True) + epsilon) * gain[...]
        )
    flow.need(small_ins)
    z_in[...] = low(nt(h1[...], a_in[...]))
    weights()
    ext[0:8, :] = jnp.zeros((8, ext.shape[1]), f32)
    for col in range(0, 4 * own + 128, 256):
        wide = min(256, 4 * own + 128 - col)
        value = nn(h1[...], w_in[:, col : col + wide])
        if col < 4 * own:
            value = value + nn(z_in[...], b_in[:, col : col + wide])
        for k in range(blocks):
            part = value[k * span : (k + 1) * span]
            start = pl.multiple_of((k ^ here) * span, span)
            if col < 3 * own:
                part = low(part)
                pre[pl.ds(start, span), col : col + wide] = part
                ext[pl.ds(start + 8, span), col : col + wide] = part.astype(f32)
            else:
                at = col - 3 * own
                if at < own:
                    gate_out[pl.ds(start, span), at : at + wide] = low(part)
                else:
                    small_out[pl.ds(start, span), :] = part
    flow.give(*early)
    grow, gcol = tile_masks(span)
    inclusive = grow >= gcol
    strictly = grow > gcol
    tri = jnp.where(inclusive, 1.0, 0.0).astype(f32)
    scale_k = 0.5**0.5
    scale_q = 128 ** (-0.5) * 0.5**0.5

    def prepare(n, carry):
        start = pl.multiple_of(n * span, span)
        betas, running, _ = gates(small_out, rb, start, span, 0, tri)
        running_t = running.T
        for h in range(heads):
            q = conv_block(ext, cw, start, h * head, span, head)
            k = conv_block(ext, cw, start, (heads + h) * head, span, head)
            v = conv_block(ext, cw, start, (2 * heads + h) * head, span, head)
            q = q * lax.logistic(q)
            k = k * lax.logistic(k)
            vs[h, n] = (v * lax.logistic(v)).astype(vs.dtype)
            q = low(q * (half_rsqrt(q) * scale_q))
            k = low(k * (half_rsqrt(k) * scale_k))
            kqs[h, n, :span] = k
            kqs[h, n, span:] = q
            both = nt(kqs[h, n], k)
            ratio = decay_ratio(running[:, h : h + 1], running_t[h : h + 1, :], inclusive)
            kr = jnp.where(strictly, ratio * both[:span], 0.0)
            tri_out[2, h, n] = low(kr)
            tri_out[1, h, n] = low(both[span:] * ratio)
            keep[1, h * blocks + n] = kr * betas[:, heads + h : heads + h + 1]
        return carry

    lax.fori_loop(0, blocks, prepare, 0)
    pairs = [(h, n) for h in range(heads) for n in range(blocks)]
    unit_lower_inverses(
        [keep.at[1, h * blocks + n] for h, n in pairs],
        [keep.at[2, h * blocks + n] for h, n in pairs],
        [keep.at[0, h * blocks + n] for h, n in pairs],
    )
    for h, n in pairs:
        tri_out[0, h, n] = low(keep[2, h * blocks + n])
    flow.give(*late)


def mixer_advance(heads, span, blocks, me, ins, outs, state):
    gate_in, small_in, kqs, vs, tri_in, rb, hg = ins
    gated, ou_out, s_out = outs
    head = 256
    here = me[0]
    grow, gcol = tile_masks(span)
    tri = jnp.where(grow >= gcol, 1.0, 0.0).astype(f32)
    state[...] = jnp.zeros_like(state)

    def advance(n, carry):
        start = pl.multiple_of(n * span, span)
        row = pl.multiple_of((n ^ here) * span, span)
        betas, running, _ = gates(small_in, rb, start, span, 0, tri)
        for h in range(heads):
            cols = slice(h * head, (h + 1) * head)
            c, b = running[:, h : h + 1], betas[:, heads + h : heads + h + 1]
            d = jnp.exp(c)
            last = c[span - 1 : span, :]
            old = state[h]
            low_old = low(old)
            s_out[h, n] = low_old
            seen = nn(kqs[h, n], low_old)
            u = low(nn(tri_in[0, h, n], low(b * (vs[h, n].astype(f32) - d * seen[:span]))))
            o = d * seen[span:] + nn(tri_in[1, h, n], u)
            ou_out[1, pl.ds(start, span), cols] = u
            ou_out[0, pl.ds(start, span), cols] = low(o)
            weighted = low(kqs[h, n, :span].astype(f32) * jnp.exp(last - c))
            state[h] = jnp.exp(last) * old + tn(weighted, u)
            norm = o * lax.rsqrt(jnp.mean(o * o, 1, keepdims=True) + epsilon) * hg[...]
            gate = gate_in[pl.ds(start, span), cols].astype(f32)
            gated[pl.ds(row, span), cols] = low(norm * (gate * lax.logistic(gate)))
        return carry

    lax.fori_loop(0, blocks, advance, 0)


def project_output(lay, micro, gated, a_out, b_out, w_out, near, single, pair, z_out):
    z_out[...] = low(nt(gated[...], a_out[...]))
    for col in range(0, lay.width, 256):
        value = nn(gated[...], w_out[:, col : col + 256]) + nn(z_out[...], b_out[:, col : col + 256])
        block_out(True, near, single, pair, col, value)


def mixer_output(lay, micro, step, flow, me, gated, a_out, b_out, q0, q1, q2, q3, near, single, pair, z_out, w_out):
    flow.need(7)
    load_w_out(me, step, (q0, q1, q2, q3), w_out)
    flow.give(4)
    project_output(lay, micro, gated, a_out, b_out, w_out, near, single, pair, z_out)


def mixer_backward(lay, micro, heads, span, blocks, windows, flow, me, g0, g1, g2, g3, a_out, b_out, w_out,
                   a_in, b_in, cw, rb, hg, pre, gates_in, small_in, ou_in, s_in, tri_in,
                   z_out, gated, z_in, w_in, h1,
                   ga_gu, g_hidden, gb_down, near, single, pair, send_near, send_single, send_pair,
                   ext, back, dstate, gbranch, dgated, dproj, dsmall, flat):
    head = 256
    here = me[0]
    own = lay.own
    width = lay.width
    flow.need(7)
    rows_of(gbranch, (g0, g1, g2, g3))
    gz_out = low(nt(gbranch[...], b_out[...]))
    for col in range(0, own, 256):
        dgated[:, col : col + 256] = low(
            nt(gbranch[...], w_out[col : col + 256, :]) + nn(gz_out, a_out[:, col : col + 256])
        )
    flow.need(18)
    grow, gcol = tile_masks(span)
    inclusive = grow >= gcol
    strictly = grow > gcol
    tri = jnp.where(inclusive, 1.0, 0.0).astype(f32)
    scale_k = 0.5**0.5
    scale_q = 128 ** (-0.5) * 0.5**0.5
    ext[0:8, :] = jnp.zeros((8, ext.shape[1]), f32)
    ext[8:, :] = pre[...].astype(f32)
    back[...] = jnp.zeros_like(back)
    dstate[...] = jnp.zeros_like(dstate)
    lane = lax.broadcasted_iota(jnp.int32, (span, 128), 1)
    sub = lax.broadcasted_iota(jnp.int32, (span, 128), 0)
    final = lax.broadcasted_iota(jnp.int32, (span, 1), 0) == span - 1

    def step(i, carry):
        n = blocks - 1 - i
        row = pl.multiple_of((n ^ here) * span, span)
        start = pl.multiple_of(n * span, span)
        betas, running, slope = gates(small_in, rb, start, span, 0, tri)
        running_t = running.T
        drunning = jnp.zeros((span, 128), f32)
        by_row = jnp.zeros((span, 128), f32)
        dbetas = jnp.zeros((span, 128), f32)
        for h in range(heads):
            cols = slice(h * head, (h + 1) * head)
            cq = conv_block(ext, cw, start, h * head, span, head)
            ck = conv_block(ext, cw, start, (heads + h) * head, span, head)
            cv = conv_block(ext, cw, start, (2 * heads + h) * head, span, head)
            sq, sk, sv = lax.logistic(cq), lax.logistic(ck), lax.logistic(cv)
            qa, ka, v = cq * sq, ck * sk, cv * sv
            rq, rk = half_rsqrt(qa), half_rsqrt(ka)
            q = qa * (rq * scale_q)
            k = ka * (rk * scale_k)
            kq = jnp.concatenate([low(k), low(q)], 0)
            c = running[:, h : h + 1]
            b = betas[:, heads + h : heads + h + 1]
            d = jnp.exp(c)
            last = c[span - 1 : span, :]
            w = jnp.exp(last - c)
            inv, att = tri_in[0, h, n], tri_in[1, h, n]
            kr = tri_in[2, h, n].astype(f32)
            u = ou_in[1, pl.ds(start, span), cols]
            o = ou_in[0, pl.ds(start, span), cols].astype(f32)
            old = s_in[h, n]
            after = dstate[h]
            gate = gates_in[pl.ds(start, span), cols].astype(f32)
            dy = dgated[pl.ds(row, span), cols].astype(f32)
            sg = lax.logistic(gate)
            r = lax.rsqrt(jnp.mean(o * o, 1, keepdims=True) + epsilon)
            dn = dy * (gate * sg) * hg[...]
            normed = o * r
            dproj[pl.ds(row, span), (3 * heads + h) * head : (3 * heads + h + 1) * head] = low(
                dy * (normed * hg[...]) * (sg * (1.0 + gate * (1.0 - sg)))
            )
            do = r * (dn - normed * jnp.mean(normed * dn, 1, keepdims=True))
            seen = nn(kq, old)
            low_after, low_do = low(after), low(do)
            x = v - d * seen[:span]
            du = tn(att, low_do) + lnn(k * w, low_after)
            datt = jnp.where(inclusive, nt(low_do, u), 0.0)
            dweighted = nt(u, low_after)
            y = ltn(inv, du)
            dlow = jnp.where(strictly, -lnt(y, u), 0.0)
            dx = b * y
            db = jnp.sum(y * x, 1, keepdims=True) + jnp.sum(dlow * kr, 1, keepdims=True)
            dseen = jnp.concatenate([low(-(d * dx)), low(d * do)], 0)
            dstate[h] = jnp.exp(last) * after + tn(kq, dseen)
            dkq = nt(dseen, old)
            dd = jnp.sum(do * seen[span:] - dx * seen[:span], 1, keepdims=True)
            ratio = decay_ratio(c, running_t[h : h + 1, :], inclusive)
            dboth = jnp.concatenate([low(dlow * b * ratio), low(datt * ratio)], 0)
            dkq = dkq + nn(dboth, kq[:span])
            dk = dkq[:span] + tn(dboth, kq) + dweighted * w
            dq = dkq[span:]
            grown = dlow * (b * kr) + datt * att
            dw = jnp.sum(dweighted * k, 1, keepdims=True) * w
            dlast = jnp.exp(last) * jnp.sum(
                jnp.sum(after * old.astype(f32), 1, keepdims=True), 0, keepdims=True
            ) + jnp.sum(dw, 0, keepdims=True)
            dc = jnp.sum(grown, 1, keepdims=True) - dw + dd * d + jnp.where(final, dlast, 0.0)
            drunning = drunning + jnp.where(lane == h, dc, 0.0)
            by_row = by_row + jnp.where(sub == h, jnp.sum(grown, 0, keepdims=True), 0.0)
            dbetas = dbetas + jnp.where(lane == heads + h, db, 0.0)
            dqa = rq * scale_q * dq - qa * (rq * rq * rq * scale_q) * half_sum(qa * dq)
            dka = rk * scale_k * dk - ka * (rk * rk * rk * scale_k) * half_sum(ka * dk)
            for part, grad, sig, act in ((0, dqa, sq, cq), (1, dka, sk, ck), (2, dx, sv, cv)):
                col = (part * heads + h) * head
                through = grad * (sig * (1.0 + act * (1.0 - sig)))
                window = jnp.concatenate([through, back[:, col : col + head]], 0)
                back[:, col : col + head] = through[:8]
                out = None
                for j in range(4):
                    term = shifted_rows(window, span, 3 - j) * cw[j : j + 1, col : col + head]
                    out = term if out is None else out + term
                dproj[pl.ds(row, span), col : col + head] = low(out)
        dlog = tn(tri, drunning - by_row.T, high)
        dsmall[pl.ds(row, span), :] = low(
            -rb[0:1, :] * slope * dlog + dbetas * betas * (1.0 - betas)
        )
        return carry

    lax.fori_loop(0, blocks, step, 0)
    flow.need(26)
    gz_in = low(nt(dproj[...], b_in[...]))
    for col in range(0, width, 256):
        value = (
            nt(dproj[...], w_in[col : col + 256, : 4 * own])
            + nt(dsmall[...], w_in[col : col + 256, 4 * own :])
            + nn(gz_in, a_in[:, col : col + 256])
        )
        block_out(micro == 0, near, single, pair, col, value)
    flow.give(0, 1, 2)
    ga_out = tn(gz_out, gated[...])
    gb_out = tn(z_out[...], gbranch[...])
    flat[...] = jnp.zeros_like(flat)
    ga_in = low(tn(gz_in, h1[...]))
    for p in range(4):
        flat[:, lay.a_in + p * width : lay.a_in + (p + 1) * width] = ga_in[p * RANK : (p + 1) * RANK]
        gb = tn(z_in[...], dproj[:, p * own : (p + 1) * own])
        flat[:, pl.ds(pl.multiple_of(lay.b_in + p * lay.value_width + here * own, 128), own)] = low(
            gb[p * RANK : (p + 1) * RANK]
        )
    flat[:, pl.ds(pl.multiple_of(lay.a_out + here * own, 128), own)] = low(ga_out)
    flat[:, lay.b_out : lay.b_out + width] = low(gb_out)
    for i in range(2):
        flat[:, lay.a_gu + i * width : lay.a_gu + (i + 1) * width] = ga_gu[i * RANK : (i + 1) * RANK, :]
    hidden = lay.hidden
    flat[:, lay.a_down : lay.a_down + hidden] = g_hidden[:RANK, :]
    for i in range(2):
        flat[:, lay.b_gu + i * hidden : lay.b_gu + (i + 1) * hidden] = g_hidden[(i + 1) * RANK : (i + 2) * RANK, :]
    flat[:, lay.b_down : lay.b_down + width] = gb_down[...]
    quarter = send_near.shape[2]
    one, two = block_order(micro == 0)
    sends = {0: send_near, one: send_single, two[0]: send_pair.at[0], two[1]: send_pair.at[1]}
    for k, send in sends.items():
        for f, window in enumerate(windows):
            at = pl.multiple_of(window + (here ^ k) * quarter, 128)
            send[f] = flat[:, pl.ds(at, quarter)]


def feed_forward_blocks(lay, micro, count, packed, flow, table, *refs):
    ins, pieces, rest = refs[:6], refs[6 : 6 + count], refs[6 + count :]
    more = 5 if packed else 6
    outs, w_gu = rest[more : more + 9], rest[more + 9]
    if packed:
        w_down, scratch = rest[more + 10], rest[more + 11 :]
    else:
        w_down, scratch = rest[5], rest[more + 10 :]

    def weights():
        flow.need(6 + count)
        load_w_in(table, pieces, 0, w_gu)
        flow.give(9)
        if packed:
            load_w_down(table, pieces, packed, w_gu.shape[1], w_down)
            flow.give(10)

    feed_forward(lay, micro, flow, weights, 6 + count + more, w_gu, ins, (*rest[:5], w_down), outs, scratch)


def feed_forward_whole(lay, micro, flow, *refs):
    ins, w_gu, rest = refs[:6], refs[6], refs[7:]
    feed_forward(lay, micro, flow, partial(flow.need, 7), 13, w_gu, ins, rest[:6], rest[6:15], rest[15:])


def feed_forward(lay, micro, flow, weights, last_ins, w_gu, ins, more_ins, outs, scratch):
    h0, h1, h2, h3, a_gu, hidden = ins
    g0, g1, g2, g3, b_down, w_down = more_ins
    near, single, pair, gnear, gsingle, gpair, ga_gu, g_own, gb_down = outs
    hs, gs, b_gate, b_up, act, ggate, gup, gates, ups = scratch
    width = lay.width
    wide = act.shape[1]
    flow.need(6)
    rows_of(hs, (h0, h1, h2, h3))
    at = [(3 * micro + i) * RANK for i in range(3)]
    a_down = hidden[at[0] : at[0] + RANK, :]
    b_gate[...] = jnp.zeros_like(b_gate)
    b_up[...] = jnp.zeros_like(b_up)
    b_gate[:RANK, :] = hidden[at[1] : at[1] + RANK, :]
    b_up[RANK:, :] = hidden[at[2] : at[2] + RANK, :]
    z_gu = low(nt(hs[...], a_gu[...]))
    weights()
    for col in range(0, wide, 256):
        cols = slice(col, col + 256)
        gates[:, cols] = nn(hs[...], w_gu[:, cols]) + nn(z_gu, b_gate[:, cols])
        ups[:, cols] = nn(hs[...], w_gu[:, wide + col : wide + col + 256]) + nn(z_gu, b_up[:, cols])
    flow.need(last_ins)
    rows_of(gs, (g0, g1, g2, g3))
    gz_down = low(nt(gs[...], b_down[...]))
    for col in range(0, wide, 256):
        cols = slice(col, col + 256)
        ga, ua = gates[:, cols], ups[:, cols]
        sig = lax.logistic(ga)
        silu = ga * sig
        act[:, cols] = low(silu * ua)
        da = low(nt(gs[...], w_down[cols, :]) + nn(gz_down, a_down[:, cols])).astype(f32)
        ggate[:, cols] = low(da * ua * (sig * (1.0 + ga * (1.0 - sig))))
        gup[:, cols] = low(da * silu)
    gz_gu = low(nt(ggate[...], b_gate[...]) + nt(gup[...], b_up[...]))
    for col in range(0, width, 256):
        cols = slice(col, col + 256)
        value = (
            nt(ggate[...], w_gu[cols, :wide]) + nt(gup[...], w_gu[cols, wide:]) + nn(gz_gu, a_gu[:, cols])
        )
        block_out(micro == 0, gnear, gsingle, gpair, col, value)
    flow.give(3, 4, 5)
    z_down = low(nt(act[...], a_down))
    for col in range(0, width, 256):
        cols = slice(col, col + 256)
        value = nn(act[...], w_down[:, cols]) + nn(z_down, b_down[:, cols])
        block_out(micro == 0, near, single, pair, col, value)
    ga_gu[...] = low(tn(gz_gu, hs[...]))
    gb_down[...] = low(tn(z_down, gs[...]))
    g_own[:RANK, :] = low(tn(gz_down, act[...]))
    g_own[RANK : 2 * RANK, :] = low(tn(z_gu, ggate[...])[:RANK])
    g_own[2 * RANK :, :] = low(tn(z_gu, gup[...])[RANK:])


def adapter_rows(lay, micro_count, windows, flow, me, c0, c1, c2, c3, *refs):
    here = me[0]
    outs, used, flat = refs[:-2], refs[-2], refs[-1]
    width, own, hidden = lay.width, lay.own, lay.hidden
    flat[...] = jnp.zeros_like(flat)
    flow.need(4)
    quarter = c0.shape[2]
    for k, piece in enumerate((c0, c1, c2, c3)):
        for f, window in enumerate(windows):
            cols = pl.ds(pl.multiple_of(window + (here ^ k) * quarter, 128), quarter)
            flat[:, cols] = flat[:, cols] + piece[f]

    def own_columns(rows, at):
        return flat[rows, pl.ds(pl.multiple_of(at + here * own, 128), own)]

    for m in range(micro_count):
        rows = slice(m * RANK, (m + 1) * RANK)
        a_in, b_in, a_gu, a_out, b_out, b_down = outs[6 * m : 6 * (m + 1)]
        b_in[...] = jnp.zeros_like(b_in)
        for p in range(4):
            part = slice(p * RANK, (p + 1) * RANK)
            a_in[part, :] = flat[rows, lay.a_in + p * width : lay.a_in + (p + 1) * width]
            b_in[part, p * own : (p + 1) * own] = own_columns(rows, lay.b_in + p * lay.value_width)
        for i in range(2):
            a_gu[i * RANK : (i + 1) * RANK, :] = flat[rows, lay.a_gu + i * width : lay.a_gu + (i + 1) * width]
        a_out[...] = own_columns(rows, lay.a_out)
        b_out[...] = flat[rows, lay.b_out : lay.b_out + width]
        b_down[...] = flat[rows, lay.b_down : lay.b_down + width]
        for i, at in enumerate((lay.a_down, lay.b_gu, lay.b_gu + hidden)):
            used[(3 * m + i) * RANK : (3 * m + i + 1) * RANK, :] = flat[rows, at : at + hidden]


SMEM = pl.BlockSpec(memory_space=pltpu.SMEM)
VMEM = pl.BlockSpec(memory_space=pltpu.VMEM)


class Flow:
    def __init__(self, stages, far_in, near_in, far_out, near_out, sems):
        self.coming = [
            pltpu.make_async_copy(far, near, sems.at[i]) for i, (far, near) in enumerate(zip(far_in, near_in))
        ]
        at = len(self.coming)
        self.going = [
            pltpu.make_async_copy(near, far, sems.at[at + i]) for i, (far, near) in enumerate(zip(far_out, near_out))
        ]
        self.sent, self.stages = set(), list(stages) + [len(self.coming)]
        self.started = self.ready = 0
        self.start()

    def start(self):
        if self.stages:
            upto = self.stages.pop(0)
            for copy in self.coming[self.started : upto]:
                copy.start()
            self.started = upto

    def need(self, upto):
        while self.ready < upto:
            if self.ready == self.started:
                self.start()
            self.coming[self.ready].wait()
            self.ready += 1
            if self.ready == self.started:
                self.start()

    def give(self, *which):
        for i in which:
            if i not in self.sent:
                self.sent.add(i)
                self.going[i].start()

    def close(self):
        self.need(len(self.coming))
        self.give(*range(len(self.going)))
        for copy in self.going:
            copy.wait()


def flowing(body, stages, scalars, arrays, results, *refs):
    smem, refs = refs[:scalars], refs[scalars:]
    far_in, refs = refs[:arrays], refs[arrays:]
    far_out, refs = refs[:results], refs[results:]
    near_in, refs = refs[:arrays], refs[arrays:]
    near_out, refs = refs[:results], refs[results:]
    sems, scratch = refs[0], refs[1:]
    flow = Flow(stages, far_in, near_in, far_out, near_out, sems)
    body(flow, *smem, *near_in, *near_out, *scratch)
    flow.close()


def kernel_call(body, name, out_shape, scratch, args, scalars=1, flops=0, stages=()):
    size = sum(a.size * a.dtype.itemsize for a in args) + sum(o.size * o.dtype.itemsize for o in out_shape)
    arrays = args[scalars:]
    far = pl.BlockSpec(memory_space=pl.ANY)
    buffers = [pltpu.VMEM(a.shape, a.dtype) for a in (*arrays, *out_shape)]
    return pl.pallas_call(
        partial(flowing, body, stages, scalars, len(arrays), len(out_shape)),
        out_shape=tuple(out_shape),
        in_specs=[SMEM] * scalars + [far] * len(arrays),
        out_specs=tuple([far] * len(out_shape)),
        scratch_shapes=[*buffers, pltpu.SemaphoreType.DMA((len(buffers),)), *scratch],
        compiler_params=pltpu.CompilerParams(vmem_limit_bytes=VMEM_LIMIT),
        cost_estimate=pl.CostEstimate(flops=flops, bytes_accessed=int(size), transcendentals=0),
        name=name,
    )(*args)


class Kernels:
    def __init__(self, lay, heads, head, span, blocks, width, own, wide, windows, quarter, flat, ranks, step):
        shape = jax.ShapeDtypeStruct
        rows = blocks * span
        self.lay, self.sizes = lay, (heads, span, blocks)
        self.windows, self.step = windows, step
        self.blocks = [shape((span, width), f32), shape((span, width), bf16), shape((2, span, width), bf16)]
        send = (ranks, RANK, quarter)
        self.sends = [shape(send, bf16), shape(send, bf16), shape((2, *send), bf16)]
        self.z_out = shape((rows, RANK), bf16)
        self.saved = [
            shape((rows, width), bf16),
            shape((rows, 4 * RANK), bf16),
            shape((rows, 3 * own), bf16),
            shape((rows, own), bf16),
            shape((rows, 128), f32),
            shape((rows, own), bf16),
            shape((2, rows, own), bf16),
            shape((heads, blocks, head, head), bf16),
            shape((3, heads, blocks, span, span), bf16),
        ]
        self.small = [shape((2 * RANK, width), bf16), shape((3 * RANK, wide), bf16), shape((RANK, width), bf16)]
        self.w_gu, self.w_down = shape((width, 2 * wide), bf16), shape((wide, width), bf16)
        self.w_in, self.w_out = shape((width, 4 * own + 128), bf16), shape((own, width), bf16)
        ext = pltpu.VMEM((rows + 8, 3 * own), f32)
        state = pltpu.VMEM((heads, head, head), f32)
        self.kq = shape((heads, blocks, 2 * span, head), bf16)
        self.v = shape((heads, blocks, span, head), bf16)
        keep = pltpu.VMEM((3, heads * blocks, span, span), f32)
        self.state = state
        self.first_scratch = [pltpu.VMEM((8, 128), f32), ext, keep]
        self.forward_scratch = [
            pltpu.VMEM((8, 128), f32),
            ext,
            state,
            pltpu.VMEM(self.kq.shape, bf16),
            pltpu.VMEM(self.v.shape, f32),
            keep,
        ]
        self.feed_scratch = (
            [pltpu.VMEM((rows, width), bf16)] * 2
            + [pltpu.VMEM((2 * RANK, wide), bf16)] * 2
            + [pltpu.VMEM((rows, wide), bf16)] * 3
            + [pltpu.VMEM((rows, wide), f32)] * 2
        )
        self.backward_scratch = [
            ext,
            pltpu.VMEM((8, 3 * own), f32),
            state,
            pltpu.VMEM((rows, width), bf16),
            pltpu.VMEM((rows, own), bf16),
            pltpu.VMEM((rows, 4 * own), bf16),
            pltpu.VMEM((rows, 128), bf16),
            pltpu.VMEM((RANK, flat), bf16),
        ]

    def forward(self, m, me, table, w_in, x, gain, adapters, cw, rb, hg):
        outs = kernel_call(
            partial(mixer_forward, self.lay, *self.sizes, len(w_in)),
            "mixer_forward",
            self.saved + [self.w_in],
            self.forward_scratch,
            (me, table, *x, gain, *adapters, cw, rb, hg, *w_in),
            scalars=2,
            stages=(),
            flops=6_000_000_000,
        )
        return outs[:-1], outs[-1]

    def first(self, m, me, w_in, x, gain, adapters, cw, rb):
        return kernel_call(
            partial(mixer_first, self.lay, *self.sizes),
            "mixer_first",
            self.saved[:5] + [self.kq, self.v, self.saved[8]],
            self.first_scratch,
            (me, *x, gain, *adapters, cw, rb, w_in),
            stages=(),
            flops=5_000_000_000,
        )

    def second(self, m, me, w_out, done, adapters, rb, hg):
        h1, z_in, pre, gate, small, kq, v, tri = done
        outs = kernel_call(
            partial(mixer_second, self.lay, m, *self.sizes),
            "mixer_second",
            self.blocks + [self.z_out] + self.saved[5:8],
            [self.state],
            (me, kq, v, tri, gate, small, rb, hg, *adapters, w_out),
            flops=3_000_000_000,
        )
        return outs[:3], outs[3], (h1, z_in, pre, gate, small, *outs[4:], tri)

    def output(self, m, me, w_out, gated, adapters):
        outs = kernel_call(
            partial(mixer_output, self.lay, m, self.step),
            "mixer_output",
            self.blocks + [self.z_out, self.w_out],
            [],
            (me, gated, *adapters, *w_out),
            flops=1_000_000_000,
        )
        return outs[:3], outs[3], outs[4]

    def feed(self, m, table, h2, cot, w_gu, w_down, a_gu, b_down, hidden):
        whole, packed = len(w_gu) == 1, w_down is None
        if whole:
            body = partial(feed_forward_whole, self.lay, m)
        else:
            body = partial(feed_forward_blocks, self.lay, m, len(w_gu), w_gu[0].shape[0] if packed else 0)
        more = [] if whole else [self.w_gu] + ([self.w_down] if packed else [])
        outs = kernel_call(
            body,
            "feed_forward",
            self.blocks * 2 + self.small + more,
            self.feed_scratch,
            (*([] if whole else [table]), *h2, a_gu, hidden, *w_gu, *cot, b_down, *([] if packed else [w_down])),
            scalars=0 if whole else 1,
            stages=(6 + len(w_gu),),
            flops=5_000_000_000,
        )
        full = w_gu[0] if whole else outs[9]
        return outs[:3], outs[3:6], outs[6:9], full, outs[10] if packed else w_down

    def backward(self, m, me, w_in, w_out, g_branch, in_adapters, out_adapters, cw, rb, hg, z_out, saved, small):
        h1, z_in, pre, gates_in, small_in, gated, ou_in, s_in, tri_in = saved
        outs = kernel_call(
            partial(mixer_backward, self.lay, m, *self.sizes, self.windows),
            "mixer_backward",
            self.blocks + self.sends,
            self.backward_scratch,
            (
                me,
                *g_branch,
                *out_adapters,
                w_out,
                *in_adapters,
                cw,
                rb,
                hg,
                pre,
                gates_in,
                small_in,
                ou_in,
                s_in,
                tri_in,
                z_out,
                gated,
                z_in,
                w_in,
                h1,
                *small,
            ),
            stages=(18,),
            flops=9_000_000_000,
        )
        return outs[:3], outs[3:]


def rms_norm(inputs, scales):
    return inputs * lax.rsqrt(jnp.mean(inputs * inputs, -1, keepdims=True) + epsilon) * scales


def own_lanes(value, start, size):
    return lax.dynamic_slice_in_dim(value, start, size, axis=value.ndim - 1)


def shards(
    tokens,
    cotangent,
    lengths,
    adapter_index,
    step_count,
    w_in,
    w_out,
    w_gu,
    w_down,
    conv_weight,
    norm_gains,
    head_gain,
    decay_rate,
    decay_bias,
    adapters,
    first_moment,
    second_moment,
):
    micro_count, _, span, width = tokens.shape
    ranks = lax.axis_size("fsdp")
    parts = lax.axis_size("seq")
    here = lax.axis_index("seq")
    place = lax.axis_index("fsdp")
    all_heads = decay_rate.shape[0]
    heads = all_heads // parts
    value_width = conv_weight.shape[1] // 3
    own = value_width // parts
    hidden = w_gu.shape[1] // 2
    piece = w_down.shape[0] // parts
    wide = -(-hidden // parts // 256) * 256
    padded = wide // ranks
    columns = adapters.shape[1]
    shard_rows = adapters.shape[0]
    rows = parts * span
    me = here.astype(jnp.int32).reshape(1)
    lay = Layout(width, value_width, hidden, parts)
    shape = jax.ShapeDtypeStruct

    bits = [1 << i for i in range(ranks.bit_length() - 1)]
    picks = lax.dynamic_update_slice(
        jnp.zeros((ranks, 128), jnp.int32), jnp.pad(adapter_index.T, ((0, 0), (0, 128 - micro_count))), (place, 0)
    )
    picks = butterfly(picks, "fsdp", bits[:1])

    def heads_slice(part):
        return own_lanes(w_in, part * value_width + here * own, own)

    small = jnp.concatenate(
        [
            own_lanes(w_in, 4 * value_width + here * heads, heads),
            own_lanes(w_in, 4 * value_width + all_heads + here * heads, heads),
            jnp.zeros((w_in.shape[0], 128 - 2 * heads), bf16),
        ],
        1,
    )
    in_rows = w_in.shape[0]
    local_out = own_lanes(w_out, here * (width // parts), width // parts)
    local_in = jnp.concatenate(
        [local_out[:in_rows], local_out[in_rows:]] + [heads_slice(p) for p in range(4)] + [small], 1
    )
    ring = RingGather(local_in)

    window = -(-(shard_rows + 127) // (128 * parts)) * 128 * parts
    quarter = window // parts
    windows = [shard_rows * f // 128 * 128 for f in range(ranks)]
    flat_width = windows[-1] + window
    offset = (shard_rows * place) % 128
    framed = lax.dynamic_update_slice(
        jnp.zeros((window, columns), bf16), adapters.astype(bf16), (offset, 0)
    )
    framed = lax.dynamic_slice_in_dim(framed, here * quarter, quarter, 0)
    conv_own = jnp.concatenate(
        [own_lanes(conv_weight, p * value_width + here * own, own) for p in range(3)], 1
    )
    rate_bias = jnp.zeros((8, 128), f32)
    rate_bias = rate_bias.at[0, :heads].set(lax.dynamic_slice(decay_rate, (here * heads,), (heads,)))
    rate_bias = rate_bias.at[1, :heads].set(lax.dynamic_slice(decay_bias, (here * heads,), (heads,)))
    gain_row = head_gain.reshape(1, -1)

    far_tokens = [gather_far(tokens[m, 0]) for m in range(micro_count)]
    positions = here * span + jnp.arange(span)
    cots = [
        cotangent[m, 0].astype(f32) * (positions < lengths[m, 0]).astype(f32)[:, None]
        for m in range(micro_count)
    ]
    picks = butterfly(picks, "fsdp", bits[1:])
    wanted = (picks[:, :micro_count, None] * RANK + jnp.arange(RANK)[None, None, :]).reshape(-1)
    select = (wanted[:, None] == jnp.arange(columns)[None, :]).astype(bf16)
    chosen = nt(select, framed).astype(bf16).reshape(ranks, micro_count * RANK, quarter)
    conv_own, rate_bias, table = ring.advance(conv_own, rate_bias, ring.table)
    chosen = lax.all_to_all(chosen, "fsdp", 0, 0)

    unit = after(jnp.arange(wide), ring.right)
    unit_of = (unit // padded) * w_down.shape[0] + here * piece + unit % padded
    unit_of = jnp.where(unit % padded < piece, unit_of, -1)
    spread = (jnp.arange(hidden)[:, None] == unit_of[None, :]).astype(bf16)
    local_gu = jnp.concatenate(
        [nn(w_gu[:, i * hidden : (i + 1) * hidden], spread).astype(bf16) for i in range(2)], 1
    )
    local_down = jnp.pad(
        lax.dynamic_slice_in_dim(w_down, here * piece, piece, 0), ((0, padded - piece), (0, 0))
    )
    if in_rows % 128 == 0 and 4 * padded == 3 * in_rows:
        split, step = width // 4 * 3, in_rows // 4
        thirds = [local_down[i * step : (i + 1) * step, split:] for i in range(3)]
        packed = jnp.concatenate([local_down[:, :split], jnp.concatenate(thirds, 1)], 0)
        local_gu = jnp.concatenate([local_gu, packed], 1)
    pieces = [gather_near(*far) for far in far_tokens]
    far_cots = [gather_far(low(cot)) for cot in cots]
    (far_tokens,) = ring.advance(far_tokens)

    chosen, local_gu, pieces, far_cots = ring.advance(chosen, local_gu, pieces, far_cots)
    cot_pieces = [gather_near(*far) for far in far_cots]
    chosen, beyond = ring.advance(*gather_far(chosen))
    chosen = gather_near(chosen, beyond)
    while not ring.done():
        ring.advance()
    quarter_width = 2 * (width // parts)
    out_sorted = pl.pallas_call(
        partial(split_out, min(block.shape[0] for block in ring.blocks)),
        grid=(1,),
        out_shape=[shape((width // parts, quarter_width), bf16)] * parts,
        in_specs=[SMEM, SMEM]
        + [pl.BlockSpec((block.shape[0], quarter_width), lambda i: (0, 0)) for block in ring.blocks],
        out_specs=[pl.BlockSpec((width // parts, quarter_width), lambda i: (0, 0))] * parts,
        name="split_out",
    )(me, table, *ring.blocks)
    out_quarters = [swapped(out_sorted[k], k) if k else out_sorted[k] for k in range(parts)]
    per_micro = [
        shape((4 * RANK, width), bf16),
        shape((4 * RANK, 4 * own), bf16),
        shape((2 * RANK, width), bf16),
        shape((RANK, own), bf16),
        shape((RANK, width), bf16),
        shape((RANK, width), bf16),
    ]
    *adapted, used = kernel_call(
        partial(adapter_rows, lay, micro_count, windows),
        "adapter_rows",
        per_micro * micro_count + [shape((3 * micro_count * RANK, hidden), bf16)],
        [pltpu.VMEM((micro_count * RANK, flat_width), bf16)],
        (me, *chosen),
    )
    adapted = [adapted[6 * m : 6 * (m + 1)] for m in range(micro_count)]
    hidden_own = nn(used, spread).astype(bf16)
    second_ring = RingGather(after(local_gu, ring.right))
    if in_rows % 128 == 0 and 4 * padded == 3 * in_rows:
        full_down = None
    else:
        full_down = lax.all_gather(after(local_down, ring.right), "fsdp", axis=0, tiled=True)

    first_gain = norm_gains[0].reshape(1, -1)
    micros = range(micro_count)
    inputs = [tokens[m, 0].astype(f32) for m in micros]
    kernels = Kernels(
        lay, heads, head_gain.shape[0], span, parts, width, own, wide, windows, quarter, flat_width, ranks, in_rows
    )

    def feed(m, h2, cot, w_gu, w_down):
        return kernels.feed(m, table, h2, cot, w_gu, w_down, adapted[m][2], adapted[m][5], hidden_own)

    def backward(m, g_branch, z_out, saved, small_grads):
        return kernels.backward(
            m,
            me,
            full_in,
            full_out,
            g_branch,
            adapted[m][:2],
            adapted[m][3:5],
            conv_own,
            rate_bias,
            gain_row,
            z_out,
            saved,
            small_grads,
        )

    def second_norm(middle):
        h2, pull = jax.vjp(partial(rms_norm, scales=norm_gains[1]), middle)
        return low(h2), pull

    def input_gradient(m, g_middle, g_h1):
        pull = jax.vjp(partial(rms_norm, scales=norm_gains[0]), inputs[m])[1]
        return low(g_middle + pull(low(g_h1).astype(f32))[0])

    saved0, full_in = kernels.forward(
        0, me, table, ring.blocks, pieces[0], first_gain, adapted[0][:2], conv_own, rate_bias, gain_row
    )
    (saved0,) = second_ring.advance(saved0)
    out0, z_out0, full_out = kernels.output(0, me, out_quarters, saved0[5], adapted[0][3:5])
    got0 = scatter_far(out0[2])
    begun1 = kernels.first(1, me, full_in, pieces[1], first_gain, adapted[1][:2], conv_own, rate_bias)
    got0, begun1 = second_ring.advance(got0, begun1)
    middle0 = inputs[0] + scatter_near(out0[0], out0[1], got0)
    h20, pull0 = second_norm(middle0)
    far0 = gather_far(h20)
    begun1 = held(begun1, h20)
    out1, z_out1, saved1 = kernels.second(1, me, full_out, begun1, adapted[1][3:5], rate_bias, gain_row)
    far0, out1 = second_ring.advance(far0, out1)
    h20, hidden_own = second_ring.advance(gather_near(*far0), hidden_own)
    while not second_ring.done():
        second_ring.advance()
    got1 = scatter_far(out1[2])
    last0, g_out0, grads0, full_gu, full_down = feed(0, h20, cot_pieces[0], second_ring.blocks, full_down)
    got1, last0, g_out0, grads0 = held((got1, last0, g_out0, grads0))
    middle1 = inputs[1] + scatter_near(out1[0], out1[1], got1)
    h21, pull1 = second_norm(middle1)
    h21 = gather_seq(h21)
    g_out0, h21 = held((g_out0, h21))
    g_got0 = scatter_far(g_out0[2])
    last1, g_out1, grads1, full_gu, full_down = feed(1, h21, cot_pieces[1], [full_gu], full_down)
    g_got0, last1, g_out1, grads1 = held((g_got0, last1, g_out1, grads1))
    g_h20 = scatter_near(g_out0[0], g_out0[1], g_got0)
    g_middle0 = cots[0] + pull0(low(g_h20).astype(f32))[0]
    branch0 = gather_far(low(g_middle0))
    hidden0, hidden1 = [nt(g[1], spread).astype(bf16) for g in (grads0, grads1)]
    branch0, hidden0, hidden1 = held((branch0, hidden0, hidden1))
    branch0 = gather_near(*branch0)
    g_h21 = after(scatter_seq(*g_out1), branch0[2])
    g_middle1 = cots[1] + pull1(low(g_h21).astype(f32))[0]
    branch0, g_middle1, last0 = held((branch0, g_middle1, last0))
    far1 = gather_far(low(g_middle1))
    last_got0 = scatter_far(last0[2])
    g_in0, sums0 = backward(0, branch0, z_out0, saved0, (grads0[0], hidden0, grads0[2]))
    far1, last_got0, last1, g_in0, sums0 = held((far1, last_got0, last1, g_in0, sums0))
    branch1 = gather_near(*far1)
    mixed0 = low(middle0 + scatter_near(last0[0], last0[1], last_got0))
    sums_got0 = scatter_far(sums0[2])
    g_in_got0 = scatter_far(g_in0[2])
    g_in1, sums1 = backward(1, branch1, z_out1, saved1, (grads1[0], hidden1, grads1[2]))
    sums_got0, g_in_got0, g_in1, sums1 = held((sums_got0, g_in_got0, g_in1, sums1))
    total1 = low(scatter_seq(sums1[0].astype(f32), *sums1[1:]))
    total0 = low(scatter_near(sums0[0].astype(f32), sums0[1], sums_got0))
    total = jnp.concatenate([total0, total1], 1)
    total, g_in1, last1 = held((total, g_in1, last1))
    arrived = lax.all_to_all(total, "fsdp", 0, 0)
    arrived, g_in_got0 = held((arrived, g_in_got0))
    mixed1 = low(middle1 + scatter_seq(*last1))
    grad_tokens0 = input_gradient(0, g_middle0, scatter_near(g_in0[0], g_in0[1], g_in_got0))
    grad_tokens1 = input_gradient(1, g_middle1, scatter_seq(*g_in1))
    mine = tn(arrived.reshape(-1, quarter), select)
    at = here * quarter + jnp.arange(quarter)
    mine = jnp.where(((at >= offset) & (at < offset + shard_rows))[:, None], mine, 0.0)
    squares = jnp.full((8, 128), jnp.sum(mine * mine))
    shard_grad = jnp.concatenate(in_seq_order(gather_seq(low(mine))), 0)
    shard_grad = lax.optimization_barrier(shard_grad)
    squares = total_over(total_over(squares, "seq"), "fsdp")[0, 0]
    shard_grad = lax.dynamic_slice_in_dim(shard_grad, offset, shard_rows, 0).astype(f32)
    norm_value = jnp.sqrt(squares)
    clipped = shard_grad * (CLIP_LIMIT / jnp.maximum(norm_value, CLIP_LIMIT))
    new_first = FIRST_DECAY * first_moment + (1.0 - FIRST_DECAY) * clipped
    new_second = SECOND_DECAY * second_moment + (1.0 - SECOND_DECAY) * clipped * clipped
    counter = step_count[0].astype(f32)
    corrected_first = new_first / (1.0 - jnp.power(FIRST_DECAY, counter))
    corrected_second = new_second / (1.0 - jnp.power(SECOND_DECAY, counter))
    update = -LEARN_RATE * (
        corrected_first / (jnp.sqrt(corrected_second) + ADAM_EPSILON) + WEIGHT_DECAY * adapters
    )
    return (
        jnp.stack([mixed0, mixed1], 0)[:, None],
        jnp.stack([grad_tokens0, grad_tokens1], 0)[:, None],
        update,
        new_first,
        new_second,
        norm_value.reshape(1),
    )


def solution(mesh):
    in_specs = (
        P(None, "fsdp", "seq", None),
        P(None, "fsdp", "seq", None),
        P(None, "fsdp"),
        P(None, "fsdp"),
        P(),
        P("fsdp", None),
        P("fsdp", None),
        P("fsdp", None),
        P("fsdp", None),
        P(),
        P(),
        P(),
        P(),
        P(),
        P("fsdp", None),
        P("fsdp", None),
        P("fsdp", None),
    )
    out_specs = (
        P(None, "fsdp", "seq", None),
        P(None, "fsdp", "seq", None),
        P("fsdp", None),
        P("fsdp", None),
        P("fsdp", None),
        P(),
    )
    return jax.shard_map(shards, mesh=mesh, in_specs=in_specs, out_specs=out_specs, check_vma=False)
```

```python
from functools import partial

import jax
import jax.numpy as jnp
from jax import lax
from jax.experimental import pallas as pl
from jax.experimental.pallas import tpu as pltpu
from jax.sharding import PartitionSpec as P

RANK = 16
epsilon = 1e-06
CLIP_LIMIT = 1.0
LEARN_RATE = 0.01
FIRST_DECAY = 0.9
SECOND_DECAY = 0.999
ADAM_EPSILON = 1e-08
WEIGHT_DECAY = 0.1
VMEM_LIMIT = 50 << 20

f32 = jnp.float32
bf16 = jnp.bfloat16
high = lax.Precision.HIGH


def nn(a, b, precision=None):
    return lax.dot_general(
        a, b, (((1,), (0,)), ((), ())), precision=precision, preferred_element_type=f32
    )


def nt(a, b, precision=None):
    return lax.dot_general(
        a, b, (((1,), (1,)), ((), ())), precision=precision, preferred_element_type=f32
    )


def tn(a, b, precision=None):
    return lax.dot_general(
        a, b, (((0,), (0,)), ((), ())), precision=precision, preferred_element_type=f32
    )


def swapped(value, bit):
    count = lax.axis_size("seq")
    return lax.ppermute(value, "seq", [(i, i ^ bit) for i in range(count)])


def gather_far(value):
    return value, swapped(value, 2)


def gather_near(value, beyond):
    return value, swapped(value, 1), beyond, swapped(beyond, 1)


def gather_seq(value):
    return gather_near(*gather_far(value))


def in_seq_order(blocks):
    here = lax.axis_index("seq")
    for bit in (1, 2):
        flip = here & bit != 0
        blocks = [jnp.where(flip, blocks[k ^ bit], blocks[k]) for k in range(4)]
    return blocks


def scatter_far(far):
    return swapped(far, 2)


def scatter_near(near, beside, got):
    got = got.astype(f32)
    return near + got[0] + swapped((beside.astype(f32) + got[1]).astype(bf16), 1).astype(f32)


def scatter_seq(near, beyond, pair):
    got = swapped(pair, 1).astype(f32)
    return near + got[0] + swapped((beyond.astype(f32) + got[1]).astype(bf16), 2).astype(f32)


def held(values, *others):
    return lax.optimization_barrier((tuple(values), *others))[0]


def ring_order(count):
    return list(range(0, count, 2)) + list(range(count - 1, 0, -2))


def after(value, *others):
    return lax.optimization_barrier((value, *others))[0]


class RingGather:
    def __init__(self, value):
        count, here = lax.axis_size("fsdp"), lax.axis_index("fsdp")
        order = ring_order(count)
        place = [order.index(d) for d in range(count)]
        rows = value.shape[0]
        halves = rows // 2 % 16 == 0
        table = []
        for d in range(count):
            source = [order[(place[d] - k) % count] * rows for k in range(count)]
            at = [source[0]]
            for hop in range(1, count // 2 + 1):
                last = 2 * hop == count
                at.append(source[hop])
                if not last:
                    at.append(source[count - hop])
                elif halves:
                    at.append(source[hop] + rows // 2)
            table.append(at)
        self.count, self.hop, self.rows, self.halves = count, 0, rows, halves
        self.table = jnp.asarray(table, jnp.int32)[here]
        self.ahead = [(order[i], order[(i + 1) % count]) for i in range(count)]
        self.behind = [(b, a) for a, b in self.ahead]
        self.right = self.left = value
        self.blocks = [value]

    def advance(self, *others):
        self.hop += 1
        right, left = self.right, self.left
        half = self.rows // 2
        last = 2 * self.hop == self.count
        if last and self.halves:
            right, left = right[:half], left[half:]
        right = lax.ppermute(right, "fsdp", self.ahead)
        if not last or self.halves:
            left = lax.ppermute(left, "fsdp", self.behind)
        self.right, self.left, *others = lax.optimization_barrier((right, left, *others))
        self.blocks.append(self.right)
        if not last or self.halves:
            self.blocks.append(self.left)
        return others

    def done(self):
        return 2 * self.hop >= self.count


def butterfly(value, axis, bits=None):
    count = lax.axis_size(axis)
    for bit in [1 << i for i in range(count.bit_length() - 1)] if bits is None else bits:
        value = value + lax.ppermute(value, axis, [(i, i ^ bit) for i in range(count)])
    return value


def total_over(value, axis):
    count = lax.axis_size(axis)
    bit = 1
    if (count.bit_length() - 1) % 2:
        value = value + lax.ppermute(value, axis, [(i, i ^ bit) for i in range(count)])
        bit = 2
    while bit < count:
        one, two, three = [
            lax.ppermute(value, axis, [(i, i ^ k) for i in range(count)]) for k in (bit, 2 * bit, 3 * bit)
        ]
        value = (value + one) + (two + three)
        bit *= 4
    return value


def low(x):
    return x.astype(bf16)


def lnn(a, b):
    return nn(low(a), low(b))


def lnt(a, b):
    return nt(low(a), low(b))


def ltn(a, b):
    return tn(low(a), low(b))


def load_w_in(table, pieces, at, w_in):
    for i, piece in enumerate(pieces):
        w_in[pl.ds(pl.multiple_of(table[i], 16), piece.shape[0]), :] = piece[:, at : at + w_in.shape[1]]


def split_out(step, me, table, *refs):
    pieces, outs = refs[:-4], refs[-4:]
    span = outs[0].shape[0]
    for i, piece in enumerate(pieces):
        row = table[i]
        for k, out in enumerate(outs):

            @pl.when((row // span) ^ me[0] == k)
            def _():
                out[pl.ds(pl.multiple_of(row % span, step), piece.shape[0]), :] = piece[...]


def load_w_down(table, pieces, rows, at, w_down):
    step = rows // 4
    wide = w_down.shape[1] // 4 * 3
    third = wide // 3
    for i, piece in enumerate(pieces):
        base = table[i] // rows * (3 * step)
        skip = rows // 2 if i == len(pieces) - 1 and piece.shape[0] < rows else 0
        for k in range(piece.shape[0] // step):
            block = piece[k * step : (k + 1) * step, at : at + wide]
            row = k + skip // step
            if row < 3:
                w_down[pl.ds(pl.multiple_of(base + row * step, step), step), :wide] = block
            else:
                for j in range(3):
                    w_down[pl.ds(pl.multiple_of(base + j * step, step), step), wide:] = block[
                        :, j * third : (j + 1) * third
                    ]


def load_w_out(me, step, quarters, w_out):
    wide = quarters[0].shape[1] // 2
    for k, quarter in enumerate(quarters):
        cols = pl.ds(pl.multiple_of((me[0] ^ k) * wide, 128), wide)
        for j in range(0, quarter.shape[0], step):
            for i in range(2):
                w_out[2 * j + i * step : 2 * j + (i + 1) * step, cols] = quarter[j : j + step, i * wide : (i + 1) * wide]


def rows_of(ref, pieces):
    span = pieces[0].shape[0]
    for k, piece in enumerate(pieces):
        ref[k * span : (k + 1) * span, :] = piece[...].astype(ref.dtype)


def block_order(far_first):
    return (1, (2, 3)) if far_first else (2, (1, 3))


def block_out(far_first, near, single, pair, col, value):
    span = near.shape[0]
    cols = slice(col, col + value.shape[1])
    one, two = block_order(far_first)
    near[:, cols] = value[:span]
    single[:, cols] = low(value[one * span : (one + 1) * span])
    for i, k in enumerate(two):
        pair[i, :, cols] = low(value[k * span : (k + 1) * span])


def tile_masks(size):
    rows = lax.broadcasted_iota(jnp.int32, (size, size), 0)
    columns = lax.broadcasted_iota(jnp.int32, (size, size), 1)
    return rows, columns


def unit_lower_inverses(lowers, inverses, keep):
    size = keep[0].shape[0]
    rows, columns = tile_masks(size)
    eye = jnp.where(rows == columns, 1.0, 0.0).astype(f32)
    block = 1
    while block < size:
        wide = 2 * block
        inside = (rows // wide == columns // wide) & (rows // block != columns // block)
        if block == 1:
            for lower, inverse in zip(lowers, inverses):
                inverse[...] = eye - jnp.where(inside, lower[...], 0.0)
        else:
            for lower, inverse, right in zip(lowers, inverses, keep):
                right[...] = nn(jnp.where(inside, lower[...], 0.0), inverse[...], high)
            for inverse, right in zip(inverses, keep):
                inverse[...] = inverse[...] - nn(inverse[...], right[...], high)
        block = wide


def shifted_rows(value, count, offset):
    if offset == 0:
        return value[:count]
    if offset % 8 == 0:
        return value[offset : offset + count]
    return pltpu.roll(value, value.shape[0] - offset, 0)[:count]


def half_sum(x):
    half = x.shape[1] // 2
    left = jnp.sum(x[:, :half], 1, keepdims=True)
    right = jnp.sum(x[:, half:], 1, keepdims=True)
    lane = lax.broadcasted_iota(jnp.int32, x.shape, 1)
    return jnp.where(lane < half, left, right)


def half_rsqrt(x):
    half = x.shape[1] // 2
    sq = x * x
    left = lax.rsqrt(jnp.sum(sq[:, :half], 1, keepdims=True) + epsilon)
    right = lax.rsqrt(jnp.sum(sq[:, half:], 1, keepdims=True) + epsilon)
    lane = lax.broadcasted_iota(jnp.int32, x.shape, 1)
    return jnp.where(lane < half, left, right)


def conv_block(ext, cw, start, col, span, width):
    window = ext[pl.ds(start, span + 8), col : col + width]
    out = None
    for j in range(4):
        term = shifted_rows(window, span, 5 + j) * cw[j : j + 1, col : col + width]
        out = term if out is None else out + term
    return out


def gates(gs, rb, start, span, col, tri):
    z = gs[pl.ds(start, span), col : col + 128]
    moved = z + rb[1:2, :]
    soft = jnp.maximum(moved, 0.0) + jnp.log(1.0 + jnp.exp(-jnp.abs(moved)))
    return lax.logistic(z), nn(tri, -rb[0:1, :] * soft, high), lax.logistic(moved)


def decay_ratio(c, c_row, inclusive):
    return jnp.where(inclusive, jnp.exp(jnp.where(inclusive, c - c_row, 0.0)), 0.0)


class Layout:
    def __init__(self, width, value_width, hidden, parts):
        counts = [4 * width, 2 * width, value_width, hidden, 4 * value_width, width, 2 * hidden, width]
        at = [sum(counts[:i]) for i in range(8)]
        self.a_in, self.a_gu, self.a_out, self.a_down, self.b_in, self.b_out, self.b_gu, self.b_down = at
        self.total = sum(counts)
        self.width, self.value_width, self.hidden = width, value_width, hidden
        self.own = value_width // parts


def mixer_forward(lay, heads, span, blocks, count, flow, me, table, *refs):
    (x0, x1, x2, x3, gain, a_in, b_in, cw, rb, hg), refs = refs[:10], refs[10:]
    pieces, refs = refs[:count], refs[count:]
    (h1, z_in, pre, gate_out, small_out, gated, ou_out, s_out, tri_out, w_in), scratch = refs[:10], refs[10:]
    gs, ext, state, kqs, vs, keep = scratch

    def weights():
        flow.need(10 + count)
        load_w_in(table, pieces, pieces[0].shape[1] - w_in.shape[1], w_in)
        flow.give(9)

    mixer_prepare(
        lay, heads, span, blocks, flow, me, weights, w_in, (x0, x1, x2, x3, gain, a_in, b_in, cw, rb),
        (h1, z_in, pre, gate_out, small_out, kqs, vs, tri_out), (gs, ext, keep), 10, (0, 1, 2, 3, 4), (8,)
    )
    mixer_advance(heads, span, blocks, me, (gate_out, small_out, kqs, vs, tri_out, rb, hg), (gated, ou_out, s_out), state)


def mixer_first(lay, heads, span, blocks, flow, me, x0, x1, x2, x3, gain, a_in, b_in, cw, rb, w_in,
                h1, z_in, pre, gate_out, small_out, kqs, vs, tri_out, gs, ext, keep):
    mixer_prepare(
        lay, heads, span, blocks, flow, me, partial(flow.need, 10), w_in, (x0, x1, x2, x3, gain, a_in, b_in, cw, rb),
        (h1, z_in, pre, gate_out, small_out, kqs, vs, tri_out), (gs, ext, keep), 9, (0, 1, 2, 3, 4), (5, 6, 7)
    )


def mixer_second(lay, micro, heads, span, blocks, flow, me, kqs, vs, tri, gate_in, small_in, rb, hg, a_out, b_out, w_out,
                 near, single, pair, z_out, gated, ou_out, s_out, state):
    flow.need(7)
    mixer_advance(heads, span, blocks, me, (gate_in, small_in, kqs, vs, tri, rb, hg), (gated, ou_out, s_out), state)
    flow.give(4, 5, 6)
    flow.need(10)
    project_output(lay, micro, gated, a_out, b_out, w_out, near, single, pair, z_out)


def mixer_prepare(lay, heads, span, blocks, flow, me, weights, w_in, ins, outs, scratch, small_ins, early, late):
    x0, x1, x2, x3, gain, a_in, b_in, cw, rb = ins
    h1, z_in, pre, gate_out, small_out, kqs, vs, tri_out = outs
    gs, ext, keep = scratch
    head = 256
    here = me[0]
    own = lay.own
    flow.need(5)
    for k, piece in enumerate((x0, x1, x2, x3)):
        x = piece[...].astype(f32)
        h1[k * span : (k + 1) * span, :] = low(
            x * lax.rsqrt(jnp.mean(x * x, 1, keepdims=True) + epsilon) * gain[...]
        )
    flow.need(small_ins)
    z_in[...] = low(nt(h1[...], a_in[...]))
    weights()
    ext[0:8, :] = jnp.zeros((8, ext.shape[1]), f32)
    for col in range(0, 4 * own + 128, 256):
        wide = min(256, 4 * own + 128 - col)
        value = nn(h1[...], w_in[:, col : col + wide])
        if col < 4 * own:
            value = value + nn(z_in[...], b_in[:, col : col + wide])
        for k in range(blocks):
            part = value[k * span : (k + 1) * span]
            start = pl.multiple_of((k ^ here) * span, span)
            if col < 3 * own:
                part = low(part)
                pre[pl.ds(start, span), col : col + wide] = part
                ext[pl.ds(start + 8, span), col : col + wide] = part.astype(f32)
            else:
                at = col - 3 * own
                if at < own:
                    gate_out[pl.ds(start, span), at : at + wide] = low(part)
                else:
                    small_out[pl.ds(start, span), :] = part
    flow.give(*early)
    grow, gcol = tile_masks(span)
    inclusive = grow >= gcol
    strictly = grow > gcol
    tri = jnp.where(inclusive, 1.0, 0.0).astype(f32)
    scale_k = 0.5**0.5
    scale_q = 128 ** (-0.5) * 0.5**0.5

    def prepare(n, carry):
        start = pl.multiple_of(n * span, span)
        betas, running, _ = gates(small_out, rb, start, span, 0, tri)
        running_t = running.T
        for h in range(heads):
            q = conv_block(ext, cw, start, h * head, span, head)
            k = conv_block(ext, cw, start, (heads + h) * head, span, head)
            v = conv_block(ext, cw, start, (2 * heads + h) * head, span, head)
            q = q * lax.logistic(q)
            k = k * lax.logistic(k)
            vs[h, n] = (v * lax.logistic(v)).astype(vs.dtype)
            q = low(q * (half_rsqrt(q) * scale_q))
            k = low(k * (half_rsqrt(k) * scale_k))
            kqs[h, n, :span] = k
            kqs[h, n, span:] = q
            both = nt(kqs[h, n], k)
            ratio = decay_ratio(running[:, h : h + 1], running_t[h : h + 1, :], inclusive)
            kr = jnp.where(strictly, ratio * both[:span], 0.0)
            tri_out[2, h, n] = low(kr)
            tri_out[1, h, n] = low(both[span:] * ratio)
            keep[1, h * blocks + n] = kr * betas[:, heads + h : heads + h + 1]
        return carry

    lax.fori_loop(0, blocks, prepare, 0)
    pairs = [(h, n) for h in range(heads) for n in range(blocks)]
    unit_lower_inverses(
        [keep.at[1, h * blocks + n] for h, n in pairs],
        [keep.at[2, h * blocks + n] for h, n in pairs],
        [keep.at[0, h * blocks + n] for h, n in pairs],
    )
    for h, n in pairs:
        tri_out[0, h, n] = low(keep[2, h * blocks + n])
    flow.give(*late)


def mixer_advance(heads, span, blocks, me, ins, outs, state):
    gate_in, small_in, kqs, vs, tri_in, rb, hg = ins
    gated, ou_out, s_out = outs
    head = 256
    here = me[0]
    grow, gcol = tile_masks(span)
    tri = jnp.where(grow >= gcol, 1.0, 0.0).astype(f32)
    state[...] = jnp.zeros_like(state)

    def advance(n, carry):
        start = pl.multiple_of(n * span, span)
        row = pl.multiple_of((n ^ here) * span, span)
        betas, running, _ = gates(small_in, rb, start, span, 0, tri)
        for h in range(heads):
            cols = slice(h * head, (h + 1) * head)
            c, b = running[:, h : h + 1], betas[:, heads + h : heads + h + 1]
            d = jnp.exp(c)
            last = c[span - 1 : span, :]
            old = state[h]
            low_old = low(old)
            s_out[h, n] = low_old
            seen = nn(kqs[h, n], low_old)
            u = low(nn(tri_in[0, h, n], low(b * (vs[h, n].astype(f32) - d * seen[:span]))))
            o = d * seen[span:] + nn(tri_in[1, h, n], u)
            ou_out[1, pl.ds(start, span), cols] = u
            ou_out[0, pl.ds(start, span), cols] = low(o)
            weighted = low(kqs[h, n, :span].astype(f32) * jnp.exp(last - c))
            state[h] = jnp.exp(last) * old + tn(weighted, u)
            norm = o * lax.rsqrt(jnp.mean(o * o, 1, keepdims=True) + epsilon) * hg[...]
            gate = gate_in[pl.ds(start, span), cols].astype(f32)
            gated[pl.ds(row, span), cols] = low(norm * (gate * lax.logistic(gate)))
        return carry

    lax.fori_loop(0, blocks, advance, 0)


def project_output(lay, micro, gated, a_out, b_out, w_out, near, single, pair, z_out):
    z_out[...] = low(nt(gated[...], a_out[...]))
    for col in range(0, lay.width, 256):
        value = nn(gated[...], w_out[:, col : col + 256]) + nn(z_out[...], b_out[:, col : col + 256])
        block_out(True, near, single, pair, col, value)


def mixer_output(lay, micro, step, flow, me, gated, a_out, b_out, q0, q1, q2, q3, near, single, pair, z_out, w_out):
    flow.need(7)
    load_w_out(me, step, (q0, q1, q2, q3), w_out)
    flow.give(4)
    project_output(lay, micro, gated, a_out, b_out, w_out, near, single, pair, z_out)


def mixer_backward(lay, micro, heads, span, blocks, windows, flow, me, g0, g1, g2, g3, a_out, b_out, w_out,
                   a_in, b_in, cw, rb, hg, pre, gates_in, small_in, ou_in, s_in, tri_in,
                   z_out, gated, z_in, w_in, h1,
                   ga_gu, g_hidden, gb_down, near, single, pair, send_near, send_single, send_pair,
                   ext, back, dstate, gbranch, dgated, dproj, dsmall, flat):
    head = 256
    here = me[0]
    own = lay.own
    width = lay.width
    flow.need(7)
    rows_of(gbranch, (g0, g1, g2, g3))
    gz_out = low(nt(gbranch[...], b_out[...]))
    for col in range(0, own, 256):
        dgated[:, col : col + 256] = low(
            nt(gbranch[...], w_out[col : col + 256, :]) + nn(gz_out, a_out[:, col : col + 256])
        )
    flow.need(18)
    grow, gcol = tile_masks(span)
    inclusive = grow >= gcol
    strictly = grow > gcol
    tri = jnp.where(inclusive, 1.0, 0.0).astype(f32)
    scale_k = 0.5**0.5
    scale_q = 128 ** (-0.5) * 0.5**0.5
    ext[0:8, :] = jnp.zeros((8, ext.shape[1]), f32)
    ext[8:, :] = pre[...].astype(f32)
    back[...] = jnp.zeros_like(back)
    dstate[...] = jnp.zeros_like(dstate)
    lane = lax.broadcasted_iota(jnp.int32, (span, 128), 1)
    sub = lax.broadcasted_iota(jnp.int32, (span, 128), 0)
    final = lax.broadcasted_iota(jnp.int32, (span, 1), 0) == span - 1

    def step(i, carry):
        n = blocks - 1 - i
        row = pl.multiple_of((n ^ here) * span, span)
        start = pl.multiple_of(n * span, span)
        betas, running, slope = gates(small_in, rb, start, span, 0, tri)
        running_t = running.T
        drunning = jnp.zeros((span, 128), f32)
        by_row = jnp.zeros((span, 128), f32)
        dbetas = jnp.zeros((span, 128), f32)
        for h in range(heads):
            cols = slice(h * head, (h + 1) * head)
            cq = conv_block(ext, cw, start, h * head, span, head)
            ck = conv_block(ext, cw, start, (heads + h) * head, span, head)
            cv = conv_block(ext, cw, start, (2 * heads + h) * head, span, head)
            sq, sk, sv = lax.logistic(cq), lax.logistic(ck), lax.logistic(cv)
            qa, ka, v = cq * sq, ck * sk, cv * sv
            rq, rk = half_rsqrt(qa), half_rsqrt(ka)
            q = qa * (rq * scale_q)
            k = ka * (rk * scale_k)
            kq = jnp.concatenate([low(k), low(q)], 0)
            c = running[:, h : h + 1]
            b = betas[:, heads + h : heads + h + 1]
            d = jnp.exp(c)
            last = c[span - 1 : span, :]
            w = jnp.exp(last - c)
            inv, att = tri_in[0, h, n], tri_in[1, h, n]
            kr = tri_in[2, h, n].astype(f32)
            u = ou_in[1, pl.ds(start, span), cols]
            o = ou_in[0, pl.ds(start, span), cols].astype(f32)
            old = s_in[h, n]
            after = dstate[h]
            gate = gates_in[pl.ds(start, span), cols].astype(f32)
            dy = dgated[pl.ds(row, span), cols].astype(f32)
            sg = lax.logistic(gate)
            r = lax.rsqrt(jnp.mean(o * o, 1, keepdims=True) + epsilon)
            dn = dy * (gate * sg) * hg[...]
            normed = o * r
            dproj[pl.ds(row, span), (3 * heads + h) * head : (3 * heads + h + 1) * head] = low(
                dy * (normed * hg[...]) * (sg * (1.0 + gate * (1.0 - sg)))
            )
            do = r * (dn - normed * jnp.mean(normed * dn, 1, keepdims=True))
            seen = nn(kq, old)
            low_after, low_do = low(after), low(do)
            x = v - d * seen[:span]
            du = tn(att, low_do) + lnn(k * w, low_after)
            datt = jnp.where(inclusive, nt(low_do, u), 0.0)
            dweighted = nt(u, low_after)
            y = ltn(inv, du)
            dlow = jnp.where(strictly, -lnt(y, u), 0.0)
            dx = b * y
            db = jnp.sum(y * x, 1, keepdims=True) + jnp.sum(dlow * kr, 1, keepdims=True)
            dseen = jnp.concatenate([low(-(d * dx)), low(d * do)], 0)
            dstate[h] = jnp.exp(last) * after + tn(kq, dseen)
            dkq = nt(dseen, old)
            dd = jnp.sum(do * seen[span:] - dx * seen[:span], 1, keepdims=True)
            ratio = decay_ratio(c, running_t[h : h + 1, :], inclusive)
            dboth = jnp.concatenate([low(dlow * b * ratio), low(datt * ratio)], 0)
            dkq = dkq + nn(dboth, kq[:span])
            dk = dkq[:span] + tn(dboth, kq) + dweighted * w
            dq = dkq[span:]
            grown = dlow * (b * kr) + datt * att
            dw = jnp.sum(dweighted * k, 1, keepdims=True) * w
            dlast = jnp.exp(last) * jnp.sum(
                jnp.sum(after * old.astype(f32), 1, keepdims=True), 0, keepdims=True
            ) + jnp.sum(dw, 0, keepdims=True)
            dc = jnp.sum(grown, 1, keepdims=True) - dw + dd * d + jnp.where(final, dlast, 0.0)
            drunning = drunning + jnp.where(lane == h, dc, 0.0)
            by_row = by_row + jnp.where(sub == h, jnp.sum(grown, 0, keepdims=True), 0.0)
            dbetas = dbetas + jnp.where(lane == heads + h, db, 0.0)
            dqa = rq * scale_q * dq - qa * (rq * rq * rq * scale_q) * half_sum(qa * dq)
            dka = rk * scale_k * dk - ka * (rk * rk * rk * scale_k) * half_sum(ka * dk)
            for part, grad, sig, act in ((0, dqa, sq, cq), (1, dka, sk, ck), (2, dx, sv, cv)):
                col = (part * heads + h) * head
                through = grad * (sig * (1.0 + act * (1.0 - sig)))
                window = jnp.concatenate([through, back[:, col : col + head]], 0)
                back[:, col : col + head] = through[:8]
                out = None
                for j in range(4):
                    term = shifted_rows(window, span, 3 - j) * cw[j : j + 1, col : col + head]
                    out = term if out is None else out + term
                dproj[pl.ds(row, span), col : col + head] = low(out)
        dlog = tn(tri, drunning - by_row.T, high)
        dsmall[pl.ds(row, span), :] = low(
            -rb[0:1, :] * slope * dlog + dbetas * betas * (1.0 - betas)
        )
        return carry

    lax.fori_loop(0, blocks, step, 0)
    flow.need(26)
    gz_in = low(nt(dproj[...], b_in[...]))
    for col in range(0, width, 256):
        value = (
            nt(dproj[...], w_in[col : col + 256, : 4 * own])
            + nt(dsmall[...], w_in[col : col + 256, 4 * own :])
            + nn(gz_in, a_in[:, col : col + 256])
        )
        block_out(micro == 0, near, single, pair, col, value)
    flow.give(0, 1, 2)
    ga_out = tn(gz_out, gated[...])
    gb_out = tn(z_out[...], gbranch[...])
    flat[...] = jnp.zeros_like(flat)
    ga_in = low(tn(gz_in, h1[...]))
    for p in range(4):
        flat[:, lay.a_in + p * width : lay.a_in + (p + 1) * width] = ga_in[p * RANK : (p + 1) * RANK]
        gb = tn(z_in[...], dproj[:, p * own : (p + 1) * own])
        flat[:, pl.ds(pl.multiple_of(lay.b_in + p * lay.value_width + here * own, 128), own)] = low(
            gb[p * RANK : (p + 1) * RANK]
        )
    flat[:, pl.ds(pl.multiple_of(lay.a_out + here * own, 128), own)] = low(ga_out)
    flat[:, lay.b_out : lay.b_out + width] = low(gb_out)
    for i in range(2):
        flat[:, lay.a_gu + i * width : lay.a_gu + (i + 1) * width] = ga_gu[i * RANK : (i + 1) * RANK, :]
    hidden = lay.hidden
    flat[:, lay.a_down : lay.a_down + hidden] = g_hidden[:RANK, :]
    for i in range(2):
        flat[:, lay.b_gu + i * hidden : lay.b_gu + (i + 1) * hidden] = g_hidden[(i + 1) * RANK : (i + 2) * RANK, :]
    flat[:, lay.b_down : lay.b_down + width] = gb_down[...]
    quarter = send_near.shape[2]
    one, two = block_order(micro == 0)
    sends = {0: send_near, one: send_single, two[0]: send_pair.at[0], two[1]: send_pair.at[1]}
    for k, send in sends.items():
        for f, window in enumerate(windows):
            at = pl.multiple_of(window + (here ^ k) * quarter, 128)
            send[f] = flat[:, pl.ds(at, quarter)]


def feed_forward_blocks(lay, micro, count, packed, flow, table, *refs):
    ins, pieces, rest = refs[:6], refs[6 : 6 + count], refs[6 + count :]
    more = 5 if packed else 6
    outs, w_gu = rest[more : more + 9], rest[more + 9]
    if packed:
        w_down, scratch = rest[more + 10], rest[more + 11 :]
    else:
        w_down, scratch = rest[5], rest[more + 10 :]

    def weights():
        flow.need(6 + count)
        load_w_in(table, pieces, 0, w_gu)
        flow.give(9)
        if packed:
            load_w_down(table, pieces, packed, w_gu.shape[1], w_down)
            flow.give(10)

    feed_forward(lay, micro, flow, weights, 6 + count + more, w_gu, ins, (*rest[:5], w_down), outs, scratch)


def feed_forward_whole(lay, micro, flow, *refs):
    ins, w_gu, rest = refs[:6], refs[6], refs[7:]
    feed_forward(lay, micro, flow, partial(flow.need, 7), 13, w_gu, ins, rest[:6], rest[6:15], rest[15:])


def feed_forward(lay, micro, flow, weights, last_ins, w_gu, ins, more_ins, outs, scratch):
    h0, h1, h2, h3, a_gu, hidden = ins
    g0, g1, g2, g3, b_down, w_down = more_ins
    near, single, pair, gnear, gsingle, gpair, ga_gu, g_own, gb_down = outs
    hs, gs, b_gate, b_up, act, ggate, gup, gates, ups = scratch
    width = lay.width
    wide = act.shape[1]
    flow.need(6)
    rows_of(hs, (h0, h1, h2, h3))
    at = [(3 * micro + i) * RANK for i in range(3)]
    a_down = hidden[at[0] : at[0] + RANK, :]
    b_gate[...] = jnp.zeros_like(b_gate)
    b_up[...] = jnp.zeros_like(b_up)
    b_gate[:RANK, :] = hidden[at[1] : at[1] + RANK, :]
    b_up[RANK:, :] = hidden[at[2] : at[2] + RANK, :]
    z_gu = low(nt(hs[...], a_gu[...]))
    weights()
    for col in range(0, wide, 256):
        cols = slice(col, col + 256)
        gates[:, cols] = nn(hs[...], w_gu[:, cols]) + nn(z_gu, b_gate[:, cols])
        ups[:, cols] = nn(hs[...], w_gu[:, wide + col : wide + col + 256]) + nn(z_gu, b_up[:, cols])
    flow.need(last_ins)
    rows_of(gs, (g0, g1, g2, g3))
    gz_down = low(nt(gs[...], b_down[...]))
    for col in range(0, wide, 256):
        cols = slice(col, col + 256)
        ga, ua = gates[:, cols], ups[:, cols]
        sig = lax.logistic(ga)
        silu = ga * sig
        act[:, cols] = low(silu * ua)
        da = low(nt(gs[...], w_down[cols, :]) + nn(gz_down, a_down[:, cols])).astype(f32)
        ggate[:, cols] = low(da * ua * (sig * (1.0 + ga * (1.0 - sig))))
        gup[:, cols] = low(da * silu)
    gz_gu = low(nt(ggate[...], b_gate[...]) + nt(gup[...], b_up[...]))
    for col in range(0, width, 256):
        cols = slice(col, col + 256)
        value = (
            nt(ggate[...], w_gu[cols, :wide]) + nt(gup[...], w_gu[cols, wide:]) + nn(gz_gu, a_gu[:, cols])
        )
        block_out(micro == 0, gnear, gsingle, gpair, col, value)
    flow.give(3, 4, 5)
    z_down = low(nt(act[...], a_down))
    for col in range(0, width, 256):
        cols = slice(col, col + 256)
        value = nn(act[...], w_down[:, cols]) + nn(z_down, b_down[:, cols])
        block_out(micro == 0, near, single, pair, col, value)
    ga_gu[...] = low(tn(gz_gu, hs[...]))
    gb_down[...] = low(tn(z_down, gs[...]))
    g_own[:RANK, :] = low(tn(gz_down, act[...]))
    g_own[RANK : 2 * RANK, :] = low(tn(z_gu, ggate[...])[:RANK])
    g_own[2 * RANK :, :] = low(tn(z_gu, gup[...])[RANK:])


def adapter_rows(lay, micro_count, windows, flow, me, c0, c1, c2, c3, *refs):
    here = me[0]
    outs, used, flat = refs[:-2], refs[-2], refs[-1]
    width, own, hidden = lay.width, lay.own, lay.hidden
    flat[...] = jnp.zeros_like(flat)
    flow.need(4)
    quarter = c0.shape[2]
    for k, piece in enumerate((c0, c1, c2, c3)):
        for f, window in enumerate(windows):
            cols = pl.ds(pl.multiple_of(window + (here ^ k) * quarter, 128), quarter)
            flat[:, cols] = flat[:, cols] + piece[f]

    def own_columns(rows, at):
        return flat[rows, pl.ds(pl.multiple_of(at + here * own, 128), own)]

    for m in range(micro_count):
        rows = slice(m * RANK, (m + 1) * RANK)
        a_in, b_in, a_gu, a_out, b_out, b_down = outs[6 * m : 6 * (m + 1)]
        b_in[...] = jnp.zeros_like(b_in)
        for p in range(4):
            part = slice(p * RANK, (p + 1) * RANK)
            a_in[part, :] = flat[rows, lay.a_in + p * width : lay.a_in + (p + 1) * width]
            b_in[part, p * own : (p + 1) * own] = own_columns(rows, lay.b_in + p * lay.value_width)
        for i in range(2):
            a_gu[i * RANK : (i + 1) * RANK, :] = flat[rows, lay.a_gu + i * width : lay.a_gu + (i + 1) * width]
        a_out[...] = own_columns(rows, lay.a_out)
        b_out[...] = flat[rows, lay.b_out : lay.b_out + width]
        b_down[...] = flat[rows, lay.b_down : lay.b_down + width]
        for i, at in enumerate((lay.a_down, lay.b_gu, lay.b_gu + hidden)):
            used[(3 * m + i) * RANK : (3 * m + i + 1) * RANK, :] = flat[rows, at : at + hidden]


SMEM = pl.BlockSpec(memory_space=pltpu.SMEM)
VMEM = pl.BlockSpec(memory_space=pltpu.VMEM)


class Flow:
    def __init__(self, stages, far_in, near_in, far_out, near_out, sems):
        self.coming = [
            pltpu.make_async_copy(far, near, sems.at[i]) for i, (far, near) in enumerate(zip(far_in, near_in))
        ]
        at = len(self.coming)
        self.going = [
            pltpu.make_async_copy(near, far, sems.at[at + i]) for i, (far, near) in enumerate(zip(far_out, near_out))
        ]
        self.sent, self.stages = set(), list(stages) + [len(self.coming)]
        self.started = self.ready = 0
        self.start()

    def start(self):
        if self.stages:
            upto = self.stages.pop(0)
            for copy in self.coming[self.started : upto]:
                copy.start()
            self.started = upto

    def need(self, upto):
        while self.ready < upto:
            if self.ready == self.started:
                self.start()
            self.coming[self.ready].wait()
            self.ready += 1
            if self.ready == self.started:
                self.start()

    def give(self, *which):
        for i in which:
            if i not in self.sent:
                self.sent.add(i)
                self.going[i].start()

    def close(self):
        self.need(len(self.coming))
        self.give(*range(len(self.going)))
        for copy in self.going:
            copy.wait()


def flowing(body, stages, scalars, arrays, results, *refs):
    smem, refs = refs[:scalars], refs[scalars:]
    far_in, refs = refs[:arrays], refs[arrays:]
    far_out, refs = refs[:results], refs[results:]
    near_in, refs = refs[:arrays], refs[arrays:]
    near_out, refs = refs[:results], refs[results:]
    sems, scratch = refs[0], refs[1:]
    flow = Flow(stages, far_in, near_in, far_out, near_out, sems)
    body(flow, *smem, *near_in, *near_out, *scratch)
    flow.close()


def kernel_call(body, name, out_shape, scratch, args, scalars=1, flops=0, stages=()):
    size = sum(a.size * a.dtype.itemsize for a in args) + sum(o.size * o.dtype.itemsize for o in out_shape)
    arrays = args[scalars:]
    far = pl.BlockSpec(memory_space=pl.ANY)
    buffers = [pltpu.VMEM(a.shape, a.dtype) for a in (*arrays, *out_shape)]
    return pl.pallas_call(
        partial(flowing, body, stages, scalars, len(arrays), len(out_shape)),
        out_shape=tuple(out_shape),
        in_specs=[SMEM] * scalars + [far] * len(arrays),
        out_specs=tuple([far] * len(out_shape)),
        scratch_shapes=[*buffers, pltpu.SemaphoreType.DMA((len(buffers),)), *scratch],
        compiler_params=pltpu.CompilerParams(vmem_limit_bytes=VMEM_LIMIT),
        cost_estimate=pl.CostEstimate(flops=flops, bytes_accessed=int(size), transcendentals=0),
        name=name,
    )(*args)


class Kernels:
    def __init__(self, lay, heads, head, span, blocks, width, own, wide, windows, quarter, flat, ranks, step):
        shape = jax.ShapeDtypeStruct
        rows = blocks * span
        self.lay, self.sizes = lay, (heads, span, blocks)
        self.windows, self.step = windows, step
        self.blocks = [shape((span, width), f32), shape((span, width), bf16), shape((2, span, width), bf16)]
        send = (ranks, RANK, quarter)
        self.sends = [shape(send, bf16), shape(send, bf16), shape((2, *send), bf16)]
        self.z_out = shape((rows, RANK), bf16)
        self.saved = [
            shape((rows, width), bf16),
            shape((rows, 4 * RANK), bf16),
            shape((rows, 3 * own), bf16),
            shape((rows, own), bf16),
            shape((rows, 128), f32),
            shape((rows, own), bf16),
            shape((2, rows, own), bf16),
            shape((heads, blocks, head, head), bf16),
            shape((3, heads, blocks, span, span), bf16),
        ]
        self.small = [shape((2 * RANK, width), bf16), shape((3 * RANK, wide), bf16), shape((RANK, width), bf16)]
        self.w_gu, self.w_down = shape((width, 2 * wide), bf16), shape((wide, width), bf16)
        self.w_in, self.w_out = shape((width, 4 * own + 128), bf16), shape((own, width), bf16)
        ext = pltpu.VMEM((rows + 8, 3 * own), f32)
        state = pltpu.VMEM((heads, head, head), f32)
        self.kq = shape((heads, blocks, 2 * span, head), bf16)
        self.v = shape((heads, blocks, span, head), bf16)
        keep = pltpu.VMEM((3, heads * blocks, span, span), f32)
        self.state = state
        self.first_scratch = [pltpu.VMEM((8, 128), f32), ext, keep]
        self.forward_scratch = [
            pltpu.VMEM((8, 128), f32),
            ext,
            state,
            pltpu.VMEM(self.kq.shape, bf16),
            pltpu.VMEM(self.v.shape, f32),
            keep,
        ]
        self.feed_scratch = (
            [pltpu.VMEM((rows, width), bf16)] * 2
            + [pltpu.VMEM((2 * RANK, wide), bf16)] * 2
            + [pltpu.VMEM((rows, wide), bf16)] * 3
            + [pltpu.VMEM((rows, wide), f32)] * 2
        )
        self.backward_scratch = [
            ext,
            pltpu.VMEM((8, 3 * own), f32),
            state,
            pltpu.VMEM((rows, width), bf16),
            pltpu.VMEM((rows, own), bf16),
            pltpu.VMEM((rows, 4 * own), bf16),
            pltpu.VMEM((rows, 128), bf16),
            pltpu.VMEM((RANK, flat), bf16),
        ]

    def forward(self, m, me, table, w_in, x, gain, adapters, cw, rb, hg):
        outs = kernel_call(
            partial(mixer_forward, self.lay, *self.sizes, len(w_in)),
            "mixer_forward",
            self.saved + [self.w_in],
            self.forward_scratch,
            (me, table, *x, gain, *adapters, cw, rb, hg, *w_in),
            scalars=2,
            stages=(),
            flops=6_000_000_000,
        )
        return outs[:-1], outs[-1]

    def first(self, m, me, w_in, x, gain, adapters, cw, rb):
        return kernel_call(
            partial(mixer_first, self.lay, *self.sizes),
            "mixer_first",
            self.saved[:5] + [self.kq, self.v, self.saved[8]],
            self.first_scratch,
            (me, *x, gain, *adapters, cw, rb, w_in),
            stages=(),
            flops=5_000_000_000,
        )

    def second(self, m, me, w_out, done, adapters, rb, hg):
        h1, z_in, pre, gate, small, kq, v, tri = done
        outs = kernel_call(
            partial(mixer_second, self.lay, m, *self.sizes),
            "mixer_second",
            self.blocks + [self.z_out] + self.saved[5:8],
            [self.state],
            (me, kq, v, tri, gate, small, rb, hg, *adapters, w_out),
            flops=3_000_000_000,
        )
        return outs[:3], outs[3], (h1, z_in, pre, gate, small, *outs[4:], tri)

    def output(self, m, me, w_out, gated, adapters):
        outs = kernel_call(
            partial(mixer_output, self.lay, m, self.step),
            "mixer_output",
            self.blocks + [self.z_out, self.w_out],
            [],
            (me, gated, *adapters, *w_out),
            flops=1_000_000_000,
        )
        return outs[:3], outs[3], outs[4]

    def feed(self, m, table, h2, cot, w_gu, w_down, a_gu, b_down, hidden):
        whole, packed = len(w_gu) == 1, w_down is None
        if whole:
            body = partial(feed_forward_whole, self.lay, m)
        else:
            body = partial(feed_forward_blocks, self.lay, m, len(w_gu), w_gu[0].shape[0] if packed else 0)
        more = [] if whole else [self.w_gu] + ([self.w_down] if packed else [])
        outs = kernel_call(
            body,
            "feed_forward",
            self.blocks * 2 + self.small + more,
            self.feed_scratch,
            (*([] if whole else [table]), *h2, a_gu, hidden, *w_gu, *cot, b_down, *([] if packed else [w_down])),
            scalars=0 if whole else 1,
            stages=(6 + len(w_gu),),
            flops=5_000_000_000,
        )
        full = w_gu[0] if whole else outs[9]
        return outs[:3], outs[3:6], outs[6:9], full, outs[10] if packed else w_down

    def backward(self, m, me, w_in, w_out, g_branch, in_adapters, out_adapters, cw, rb, hg, z_out, saved, small):
        h1, z_in, pre, gates_in, small_in, gated, ou_in, s_in, tri_in = saved
        outs = kernel_call(
            partial(mixer_backward, self.lay, m, *self.sizes, self.windows),
            "mixer_backward",
            self.blocks + self.sends,
            self.backward_scratch,
            (
                me,
                *g_branch,
                *out_adapters,
                w_out,
                *in_adapters,
                cw,
                rb,
                hg,
                pre,
                gates_in,
                small_in,
                ou_in,
                s_in,
                tri_in,
                z_out,
                gated,
                z_in,
                w_in,
                h1,
                *small,
            ),
            stages=(18,),
            flops=9_000_000_000,
        )
        return outs[:3], outs[3:]


def rms_norm(inputs, scales):
    return inputs * lax.rsqrt(jnp.mean(inputs * inputs, -1, keepdims=True) + epsilon) * scales


def own_lanes(value, start, size):
    return lax.dynamic_slice_in_dim(value, start, size, axis=value.ndim - 1)


def shards(
    tokens,
    cotangent,
    lengths,
    adapter_index,
    step_count,
    w_in,
    w_out,
    w_gu,
    w_down,
    conv_weight,
    norm_gains,
    head_gain,
    decay_rate,
    decay_bias,
    adapters,
    first_moment,
    second_moment,
):
    micro_count, _, span, width = tokens.shape
    ranks = lax.axis_size("fsdp")
    parts = lax.axis_size("seq")
    here = lax.axis_index("seq")
    place = lax.axis_index("fsdp")
    all_heads = decay_rate.shape[0]
    heads = all_heads // parts
    value_width = conv_weight.shape[1] // 3
    own = value_width // parts
    hidden = w_gu.shape[1] // 2
    piece = w_down.shape[0] // parts
    wide = -(-hidden // parts // 256) * 256
    padded = wide // ranks
    columns = adapters.shape[1]
    shard_rows = adapters.shape[0]
    rows = parts * span
    me = here.astype(jnp.int32).reshape(1)
    lay = Layout(width, value_width, hidden, parts)
    shape = jax.ShapeDtypeStruct

    bits = [1 << i for i in range(ranks.bit_length() - 1)]
    picks = lax.dynamic_update_slice(
        jnp.zeros((ranks, 128), jnp.int32), jnp.pad(adapter_index.T, ((0, 0), (0, 128 - micro_count))), (place, 0)
    )
    picks = butterfly(picks, "fsdp", bits[:1])

    def heads_slice(part):
        return own_lanes(w_in, part * value_width + here * own, own)

    small = jnp.concatenate(
        [
            own_lanes(w_in, 4 * value_width + here * heads, heads),
            own_lanes(w_in, 4 * value_width + all_heads + here * heads, heads),
            jnp.zeros((w_in.shape[0], 128 - 2 * heads), bf16),
        ],
        1,
    )
    in_rows = w_in.shape[0]
    local_out = own_lanes(w_out, here * (width // parts), width // parts)
    local_in = jnp.concatenate(
        [local_out[:in_rows], local_out[in_rows:]] + [heads_slice(p) for p in range(4)] + [small], 1
    )
    ring = RingGather(local_in)

    window = -(-(shard_rows + 127) // (128 * parts)) * 128 * parts
    quarter = window // parts
    windows = [shard_rows * f // 128 * 128 for f in range(ranks)]
    flat_width = windows[-1] + window
    offset = (shard_rows * place) % 128
    framed = lax.dynamic_update_slice(
        jnp.zeros((window, columns), bf16), adapters.astype(bf16), (offset, 0)
    )
    framed = lax.dynamic_slice_in_dim(framed, here * quarter, quarter, 0)
    conv_own = jnp.concatenate(
        [own_lanes(conv_weight, p * value_width + here * own, own) for p in range(3)], 1
    )
    rate_bias = jnp.zeros((8, 128), f32)
    rate_bias = rate_bias.at[0, :heads].set(lax.dynamic_slice(decay_rate, (here * heads,), (heads,)))
    rate_bias = rate_bias.at[1, :heads].set(lax.dynamic_slice(decay_bias, (here * heads,), (heads,)))
    gain_row = head_gain.reshape(1, -1)

    far_tokens = [gather_far(tokens[m, 0]) for m in range(micro_count)]
    positions = here * span + jnp.arange(span)
    cots = [
        cotangent[m, 0].astype(f32) * (positions < lengths[m, 0]).astype(f32)[:, None]
        for m in range(micro_count)
    ]
    picks = butterfly(picks, "fsdp", bits[1:])
    wanted = (picks[:, :micro_count, None] * RANK + jnp.arange(RANK)[None, None, :]).reshape(-1)
    select = (wanted[:, None] == jnp.arange(columns)[None, :]).astype(bf16)
    chosen = nt(select, framed).astype(bf16).reshape(ranks, micro_count * RANK, quarter)
    conv_own, rate_bias, table = ring.advance(conv_own, rate_bias, ring.table)
    chosen = lax.all_to_all(chosen, "fsdp", 0, 0)

    unit = after(jnp.arange(wide), ring.right)
    unit_of = (unit // padded) * w_down.shape[0] + here * piece + unit % padded
    unit_of = jnp.where(unit % padded < piece, unit_of, -1)
    spread = (jnp.arange(hidden)[:, None] == unit_of[None, :]).astype(bf16)
    local_gu = jnp.concatenate(
        [nn(w_gu[:, i * hidden : (i + 1) * hidden], spread).astype(bf16) for i in range(2)], 1
    )
    local_down = jnp.pad(
        lax.dynamic_slice_in_dim(w_down, here * piece, piece, 0), ((0, padded - piece), (0, 0))
    )
    if in_rows % 128 == 0 and 4 * padded == 3 * in_rows:
        split, step = width // 4 * 3, in_rows // 4
        thirds = [local_down[i * step : (i + 1) * step, split:] for i in range(3)]
        packed = jnp.concatenate([local_down[:, :split], jnp.concatenate(thirds, 1)], 0)
        local_gu = jnp.concatenate([local_gu, packed], 1)
    pieces = [gather_near(*far) for far in far_tokens]
    far_cots = [gather_far(low(cot)) for cot in cots]
    (far_tokens,) = ring.advance(far_tokens)

    chosen, local_gu, pieces, far_cots = ring.advance(chosen, local_gu, pieces, far_cots)
    cot_pieces = [gather_near(*far) for far in far_cots]
    chosen, beyond = ring.advance(*gather_far(chosen))
    chosen = gather_near(chosen, beyond)
    while not ring.done():
        ring.advance()
    quarter_width = 2 * (width // parts)
    out_sorted = pl.pallas_call(
        partial(split_out, min(block.shape[0] for block in ring.blocks)),
        grid=(1,),
        out_shape=[shape((width // parts, quarter_width), bf16)] * parts,
        in_specs=[SMEM, SMEM]
        + [pl.BlockSpec((block.shape[0], quarter_width), lambda i: (0, 0)) for block in ring.blocks],
        out_specs=[pl.BlockSpec((width // parts, quarter_width), lambda i: (0, 0))] * parts,
        name="split_out",
    )(me, table, *ring.blocks)
    out_quarters = [swapped(out_sorted[k], k) if k else out_sorted[k] for k in range(parts)]
    per_micro = [
        shape((4 * RANK, width), bf16),
        shape((4 * RANK, 4 * own), bf16),
        shape((2 * RANK, width), bf16),
        shape((RANK, own), bf16),
        shape((RANK, width), bf16),
        shape((RANK, width), bf16),
    ]
    *adapted, used = kernel_call(
        partial(adapter_rows, lay, micro_count, windows),
        "adapter_rows",
        per_micro * micro_count + [shape((3 * micro_count * RANK, hidden), bf16)],
        [pltpu.VMEM((micro_count * RANK, flat_width), bf16)],
        (me, *chosen),
    )
    adapted = [adapted[6 * m : 6 * (m + 1)] for m in range(micro_count)]
    hidden_own = nn(used, spread).astype(bf16)
    second_ring = RingGather(after(local_gu, ring.right))
    if in_rows % 128 == 0 and 4 * padded == 3 * in_rows:
        full_down = None
    else:
        full_down = lax.all_gather(after(local_down, ring.right), "fsdp", axis=0, tiled=True)

    first_gain = norm_gains[0].reshape(1, -1)
    micros = range(micro_count)
    inputs = [tokens[m, 0].astype(f32) for m in micros]
    kernels = Kernels(
        lay, heads, head_gain.shape[0], span, parts, width, own, wide, windows, quarter, flat_width, ranks, in_rows
    )

    def feed(m, h2, cot, w_gu, w_down):
        return kernels.feed(m, table, h2, cot, w_gu, w_down, adapted[m][2], adapted[m][5], hidden_own)

    def backward(m, g_branch, z_out, saved, small_grads):
        return kernels.backward(
            m,
            me,
            full_in,
            full_out,
            g_branch,
            adapted[m][:2],
            adapted[m][3:5],
            conv_own,
            rate_bias,
            gain_row,
            z_out,
            saved,
            small_grads,
        )

    def second_norm(middle):
        h2, pull = jax.vjp(partial(rms_norm, scales=norm_gains[1]), middle)
        return low(h2), pull

    def input_gradient(m, g_middle, g_h1):
        pull = jax.vjp(partial(rms_norm, scales=norm_gains[0]), inputs[m])[1]
        return low(g_middle + pull(low(g_h1).astype(f32))[0])

    saved0, full_in = kernels.forward(
        0, me, table, ring.blocks, pieces[0], first_gain, adapted[0][:2], conv_own, rate_bias, gain_row
    )
    (saved0,) = second_ring.advance(saved0)
    out0, z_out0, full_out = kernels.output(0, me, out_quarters, saved0[5], adapted[0][3:5])
    got0 = scatter_far(out0[2])
    begun1 = kernels.first(1, me, full_in, pieces[1], first_gain, adapted[1][:2], conv_own, rate_bias)
    got0, begun1 = second_ring.advance(got0, begun1)
    middle0 = inputs[0] + scatter_near(out0[0], out0[1], got0)
    h20, pull0 = second_norm(middle0)
    far0 = gather_far(h20)
    begun1 = held(begun1, h20)
    out1, z_out1, saved1 = kernels.second(1, me, full_out, begun1, adapted[1][3:5], rate_bias, gain_row)
    far0, out1 = second_ring.advance(far0, out1)
    h20, hidden_own = second_ring.advance(gather_near(*far0), hidden_own)
    while not second_ring.done():
        second_ring.advance()
    got1 = scatter_far(out1[2])
    last0, g_out0, grads0, full_gu, full_down = feed(0, h20, cot_pieces[0], second_ring.blocks, full_down)
    got1, last0, g_out0, grads0 = held((got1, last0, g_out0, grads0))
    middle1 = inputs[1] + scatter_near(out1[0], out1[1], got1)
    h21, pull1 = second_norm(middle1)
    h21 = gather_seq(h21)
    g_out0, h21 = held((g_out0, h21))
    g_got0 = scatter_far(g_out0[2])
    last1, g_out1, grads1, full_gu, full_down = feed(1, h21, cot_pieces[1], [full_gu], full_down)
    g_got0, last1, g_out1, grads1 = held((g_got0, last1, g_out1, grads1))
    g_h20 = scatter_near(g_out0[0], g_out0[1], g_got0)
    g_middle0 = cots[0] + pull0(low(g_h20).astype(f32))[0]
    branch0 = gather_far(low(g_middle0))
    hidden0, hidden1 = [nt(g[1], spread).astype(bf16) for g in (grads0, grads1)]
    branch0, hidden0, hidden1 = held((branch0, hidden0, hidden1))
    branch0 = gather_near(*branch0)
    g_h21 = after(scatter_seq(*g_out1), branch0[2])
    g_middle1 = cots[1] + pull1(low(g_h21).astype(f32))[0]
    branch0, g_middle1, last0 = held((branch0, g_middle1, last0))
    far1 = gather_far(low(g_middle1))
    last_got0 = scatter_far(last0[2])
    g_in0, sums0 = backward(0, branch0, z_out0, saved0, (grads0[0], hidden0, grads0[2]))
    far1, last_got0, last1, g_in0, sums0 = held((far1, last_got0, last1, g_in0, sums0))
    branch1 = gather_near(*far1)
    mixed0 = low(middle0 + scatter_near(last0[0], last0[1], last_got0))
    sums_got0 = scatter_far(sums0[2])
    g_in_got0 = scatter_far(g_in0[2])
    g_in1, sums1 = backward(1, branch1, z_out1, saved1, (grads1[0], hidden1, grads1[2]))
    sums_got0, g_in_got0, g_in1, sums1 = held((sums_got0, g_in_got0, g_in1, sums1))
    total1 = low(scatter_seq(sums1[0].astype(f32), *sums1[1:]))
    total0 = low(scatter_near(sums0[0].astype(f32), sums0[1], sums_got0))
    total = jnp.concatenate([total0, total1], 1)
    total, g_in1, last1 = held((total, g_in1, last1))
    arrived = lax.all_to_all(total, "fsdp", 0, 0)
    arrived, g_in_got0 = held((arrived, g_in_got0))
    mixed1 = low(middle1 + scatter_seq(*last1))
    grad_tokens0 = input_gradient(0, g_middle0, scatter_near(g_in0[0], g_in0[1], g_in_got0))
    grad_tokens1 = input_gradient(1, g_middle1, scatter_seq(*g_in1))
    mine = tn(arrived.reshape(-1, quarter), select)
    at = here * quarter + jnp.arange(quarter)
    mine = jnp.where(((at >= offset) & (at < offset + shard_rows))[:, None], mine, 0.0)
    squares = jnp.full((8, 128), jnp.sum(mine * mine))
    shard_grad = jnp.concatenate(in_seq_order(gather_seq(low(mine))), 0)
    shard_grad = lax.optimization_barrier(shard_grad)
    squares = total_over(total_over(squares, "seq"), "fsdp")[0, 0]
    shard_grad = lax.dynamic_slice_in_dim(shard_grad, offset, shard_rows, 0).astype(f32)
    norm_value = jnp.sqrt(squares)
    clipped = shard_grad * (CLIP_LIMIT / jnp.maximum(norm_value, CLIP_LIMIT))
    new_first = FIRST_DECAY * first_moment + (1.0 - FIRST_DECAY) * clipped
    new_second = SECOND_DECAY * second_moment + (1.0 - SECOND_DECAY) * clipped * clipped
    counter = step_count[0].astype(f32)
    corrected_first = new_first / (1.0 - jnp.power(FIRST_DECAY, counter))
    corrected_second = new_second / (1.0 - jnp.power(SECOND_DECAY, counter))
    update = -LEARN_RATE * (
        corrected_first / (jnp.sqrt(corrected_second) + ADAM_EPSILON) + WEIGHT_DECAY * adapters
    )
    return (
        jnp.stack([mixed0, mixed1], 0)[:, None],
        jnp.stack([grad_tokens0, grad_tokens1], 0)[:, None],
        update,
        new_first,
        new_second,
        norm_value.reshape(1),
    )


def solution(mesh):
    in_specs = (
        P(None, "fsdp", "seq", None),
        P(None, "fsdp", "seq", None),
        P(None, "fsdp"),
        P(None, "fsdp"),
        P(),
        P("fsdp", None),
        P("fsdp", None),
        P("fsdp", None),
        P("fsdp", None),
        P(),
        P(),
        P(),
        P(),
        P(),
        P("fsdp", None),
        P("fsdp", None),
        P("fsdp", None),
    )
    out_specs = (
        P(None, "fsdp", "seq", None),
        P(None, "fsdp", "seq", None),
        P("fsdp", None),
        P("fsdp", None),
        P("fsdp", None),
        P(),
    )
    return jax.shard_map(shards, mesh=mesh, in_specs=in_specs, out_specs=out_specs, check_vma=False)
```
